512 devices in a mesh: ens: 16 (over x, y_lo), lat: 32 (over y_hi, z, core).
Axes of the slice: x: 4, y: 8 (y_hi: 2, y_lo: 4; y = y_hi * 4 + y_lo), z: 8, core: 2. Of those that a mesh axis runs over, the one named last changes fastest.
Arguments:
- features: bfloat16 [128, 128, 128], P('lat'), may hold values from -6 to 6
- random_perturbation: bfloat16 [16, 128, 128, 128], P('ens', 'lat'), may hold values from -6 to 6
- observed_truth: float32 [69, 128, 128], P(None, 'lat'), may hold values from -6 to 6
- stencil_taps: float32 [49, 128], replicated, may hold values from -0.875 to 0.875
- affine_factor: float32 [128], replicated, may hold values from 0.5 to 1.5
- widen_matrix: bfloat16 [512, 128], P('lat'), may hold values from -0.5 to 0.5
- shrink_matrix: bfloat16 [512, 128], P('lat'), may hold values from -0.25 to 0.25
- readout_matrix: bfloat16 [69, 128], replicated, may hold values from -0.5 to 0.5
Outputs:
- crps_score: float32 [], replicated
- stencil_taps_sensitivity: float32 [49, 128], replicated
- affine_factor_sensitivity: float32 [128], replicated
- widen_matrix_sensitivity: float32 [512, 128], P('lat')
- shrink_matrix_sensitivity: float32 [512, 128], P('lat')
- readout_matrix_sensitivity: float32 [69, 128], replicated
- sample_outlook: bfloat16 [16, 69, 128, 128], P('ens', None, 'lat')
- sample_average_spread: float32 [16, 69, 128, 128], P('ens', None, 'lat')
The draws below stay inside these ranges and needn't reach their ends.
All inputs are finite; a program needn't handle non-finite values.
Results may differ from the reference program's by a relative error of at most 0.0024.
The reference program's roundings to bfloat16 on the way count: a program that leaves them out, or rounds other values in their place, can miss the bound.
Values may be sent and summed in bfloat16 or wider, within the bound.
No kernel may reach another device: no remote copies, remote signals or barrier semaphores. Data moves between devices by JAX's collectives and lax.ppermute only.
A program may use at most 64 MiB of HBM per device.

```python
import math
import jax
import jax.numpy as jnp
from jax import lax

CHANNEL_COUNT = 128
EXPANSION_WIDTH = 512
OUTPUT_QUANTITY = 69
STENCIL_SIDE = 7
ZONAL_SPAN = 128
MEMBERS = 16
MERIDIAN_SPAN = 128


def block_scale(rng, dims, split, least, high):
    def one(dim, shards_of):
        draws = jax.random.uniform(jax.random.fold_in(jax.random.fold_in(rng, 6), dim), (shards_of,), jnp.float32, least / len(split), high / len(split))
        return jnp.repeat(jnp.exp(draws), dims[dim] // shards_of).reshape((-1,) + (1,) * (len(dims) - dim - 1))

    gain = one(*split[0])
    for cut in split[1:]:
        gain = gain * one(*cut)
    return gain


def gaussian(own_key, extent, scale, reach, split=(), dtype=jnp.bfloat16):
    values = scale * jax.random.normal(own_key, extent, jnp.float32)
    if split:
        values = values * block_scale(own_key, extent, split, -0.22, 0.18)
    return jnp.clip(values, -reach, reach).astype(dtype)


def setup_inputs(seed: int = 0) -> dict:
    arg_keys = jax.random.split(jax.random.key(seed), 9)
    return {
        "features": gaussian(arg_keys[0], (MERIDIAN_SPAN, ZONAL_SPAN, CHANNEL_COUNT), 1.0, 6.0, ((0, 32),)),
        "random_perturbation": gaussian(arg_keys[1], (MEMBERS, MERIDIAN_SPAN, ZONAL_SPAN, CHANNEL_COUNT), 1.0, 6.0, ((0, 16), (1, 32))),
        "observed_truth": gaussian(arg_keys[2], (OUTPUT_QUANTITY, MERIDIAN_SPAN, ZONAL_SPAN), 1.0, 6.0, ((1, 32),), jnp.float32),
        "stencil_taps": gaussian(arg_keys[3], (STENCIL_SIDE * STENCIL_SIDE, CHANNEL_COUNT), (STENCIL_SIDE * STENCIL_SIDE) ** -0.5, 0.875, (), jnp.float32),
        "affine_factor": jnp.clip(1.0 + 0.1 * jax.random.normal(arg_keys[4], (CHANNEL_COUNT,), jnp.float32), 0.5, 1.5),
        "widen_matrix": gaussian(arg_keys[5], (EXPANSION_WIDTH, CHANNEL_COUNT), CHANNEL_COUNT ** -0.5, 0.5, ((0, 32),)),
        "shrink_matrix": gaussian(arg_keys[6], (EXPANSION_WIDTH, CHANNEL_COUNT), EXPANSION_WIDTH ** -0.5, 0.25, ((0, 32),)),
        "readout_matrix": gaussian(arg_keys[7], (OUTPUT_QUANTITY, CHANNEL_COUNT), CHANNEL_COUNT ** -0.5, 0.5),
    }


SQRT_TWO_PI = 0.7978845608028654
CUBIC = 0.044715
EPSILON = 1e-06
SMOOTHING = 0.01

def smooth_magnitude(value):
    return jnp.sqrt(value * value + SMOOTHING)

def smooth_slope(value):
    return value * lax.rsqrt(value * value + SMOOTHING)

def gelu_tanh(northern_margin):
    return 0.5 * northern_margin * (1.0 + jnp.tanh(SQRT_TWO_PI * (northern_margin + CUBIC * northern_margin * northern_margin * northern_margin)))

def gelu_slope(northern_margin):
    inner = jnp.tanh(SQRT_TWO_PI * (northern_margin + CUBIC * northern_margin * northern_margin * northern_margin))
    return 0.5 * (1.0 + inner) + 0.5 * northern_margin * (1.0 - inner * inner) * SQRT_TWO_PI * (1.0 + 3.0 * CUBIC * northern_margin * northern_margin)

def depthwise(margin_extended, stencil_taps, meridian_slab):
    half = STENCIL_SIDE // 2
    wide = margin_extended.astype(jnp.float32)
    axis_rows = wide.ndim - 3
    result = jnp.zeros(wide.shape[:axis_rows] + (meridian_slab,) + wide.shape[axis_rows + 1:], jnp.float32)
    for offset_row in range(STENCIL_SIDE):
        band = lax.slice_in_dim(wide, offset_row, offset_row + meridian_slab, axis=axis_rows)
        for offset_col in range(STENCIL_SIDE):
            result = result + stencil_taps[offset_row * STENCIL_SIDE + offset_col] * jnp.roll(band, half - offset_col, axis=-2)
    return result

def kernel_grad(margin_extended, upstream, meridian_slab):
    half = STENCIL_SIDE // 2
    wide = margin_extended.astype(jnp.float32)
    axis_rows = wide.ndim - 3
    channels = upstream.shape[-1]
    taps = []
    for offset_row in range(STENCIL_SIDE):
        band = lax.slice_in_dim(wide, offset_row, offset_row + meridian_slab, axis=axis_rows)
        for offset_col in range(STENCIL_SIDE):
            shifted = jnp.roll(band, half - offset_col, axis=-2)
            taps.append(lax.optimization_barrier(jnp.sum((upstream * shifted).reshape(-1, channels), axis=0)))
    return jnp.stack(taps)

def normalize(depth_out):
    centre = lax.optimization_barrier(jnp.mean(depth_out, axis=-1, keepdims=True))
    centred = depth_out - centre
    variance = lax.optimization_barrier(jnp.mean(centred * centred, axis=-1, keepdims=True))
    reciprocal_spread = lax.rsqrt(variance + EPSILON)
    return (centred * reciprocal_spread, reciprocal_spread)

def sample_evaluation(planar_map, margin_extended, stencil_taps, affine_factor, widen_matrix, shrink_matrix, readout_matrix):
    meridian_slab, zonal_points, channels = planar_map.shape
    depth_out = depthwise(margin_extended, stencil_taps, meridian_slab)
    factor_multiplied, reciprocal_spread = normalize(depth_out)
    standardized_activation = (affine_factor * factor_multiplied).astype(jnp.bfloat16).reshape(meridian_slab * zonal_points, channels)
    northern_margin = lax.dot_general(standardized_activation, widen_matrix, (((1,), (1,)), ((), ())), preferred_element_type=jnp.float32)
    nonlinear_response = gelu_tanh(northern_margin).astype(jnp.bfloat16)
    mixed = jnp.dot(nonlinear_response, shrink_matrix, preferred_element_type=jnp.float32)
    skip_activation = (planar_map.reshape(meridian_slab * zonal_points, channels).astype(jnp.float32) + mixed).astype(jnp.bfloat16)
    sample_outlook = lax.dot_general(readout_matrix, skip_activation, (((1,), (1,)), ((), ())), preferred_element_type=jnp.float32).astype(jnp.bfloat16)
    return (sample_outlook, (factor_multiplied, reciprocal_spread, standardized_activation, northern_margin, nonlinear_response, skip_activation))

def reverse_sample_sweep(margin_extended, carried_signal, stored_intermediates, affine_factor, widen_matrix, shrink_matrix, readout_matrix):
    factor_multiplied, reciprocal_spread, standardized_activation, northern_margin, nonlinear_response, skip_activation = stored_intermediates
    meridian_slab, zonal_points, channels = factor_multiplied.shape
    readout_matrix_sensitivity = jnp.dot(carried_signal, skip_activation, preferred_element_type=jnp.float32)
    back_residual = lax.dot_general(carried_signal, readout_matrix, (((0,), (0,)), ((), ())), preferred_element_type=jnp.float32).astype(jnp.bfloat16)
    shrink_matrix_sensitivity = lax.dot_general(nonlinear_response, back_residual, (((0,), (0,)), ((), ())), preferred_element_type=jnp.float32)
    back_gate = lax.dot_general(back_residual, shrink_matrix, (((1,), (1,)), ((), ())), preferred_element_type=jnp.float32)
    back_upper = (back_gate * gelu_slope(northern_margin)).astype(jnp.bfloat16)
    widen_matrix_sensitivity = lax.dot_general(back_upper, standardized_activation, (((0,), (0,)), ((), ())), preferred_element_type=jnp.float32)
    back_norm = jnp.dot(back_upper, widen_matrix, preferred_element_type=jnp.float32).reshape(meridian_slab, zonal_points, channels)
    affine_factor_sensitivity = lax.optimization_barrier(jnp.sum((back_norm * factor_multiplied).reshape(-1, channels), axis=0))
    back_scaled = back_norm * affine_factor
    back_depth = reciprocal_spread * (back_scaled - lax.optimization_barrier(jnp.mean(back_scaled, axis=-1, keepdims=True)) - factor_multiplied * lax.optimization_barrier(jnp.mean(back_scaled * factor_multiplied, axis=-1, keepdims=True)))
    stencil_taps_sensitivity = kernel_grad(margin_extended, back_depth, meridian_slab)
    return (stencil_taps_sensitivity, affine_factor_sensitivity, widen_matrix_sensitivity, shrink_matrix_sensitivity, readout_matrix_sensitivity)

def reference(features, random_perturbation, observed_truth, stencil_taps, affine_factor, widen_matrix, shrink_matrix, readout_matrix):
    half = STENCIL_SIDE // 2
    row_index = jnp.arange(MERIDIAN_SPAN).astype(jnp.float32)
    area = jnp.cos(math.pi * ((row_index + 0.5) / MERIDIAN_SPAN - 0.5)).astype(jnp.float32)
    weight = (area * (1.0 / (MERIDIAN_SPAN * ZONAL_SPAN)))[None, None, :, None]

    def member_field(member_noise):
        planar_map = (features.astype(jnp.float32) + member_noise.astype(jnp.float32)).astype(jnp.bfloat16)
        margin_extended = jnp.pad(planar_map, ((half, half), (0, 0), (0, 0)))
        return (planar_map, margin_extended)

    def estimated_outputs(member_noise):
        planar_map, margin_extended = member_field(member_noise)
        sample_outlook, ignored_entry = sample_evaluation(planar_map, margin_extended, stencil_taps, affine_factor, widen_matrix, shrink_matrix, readout_matrix)
        return sample_outlook.reshape(OUTPUT_QUANTITY, MERIDIAN_SPAN, ZONAL_SPAN)
    sample_outlooks = lax.map(estimated_outputs, random_perturbation)
    numeric_tensor = sample_outlooks.astype(jnp.float32)

    def pair_step(carry, other):
        gap = numeric_tensor - other[None]
        return ((carry[0] + smooth_magnitude(gap), carry[1] + smooth_slope(gap)), None)
    nil_filled = jnp.zeros_like(numeric_tensor)
    (spread, ranks), ignored_entry = lax.scan(pair_step, (nil_filled, nil_filled), numeric_tensor)
    miss = numeric_tensor - observed_truth[None]
    pair_norm = 1.0 / (MEMBERS * (MEMBERS - 1))
    crps_score = jnp.sum(weight * (smooth_magnitude(miss) / MEMBERS - 0.5 * pair_norm * spread))
    flows = (weight * (smooth_slope(miss) / MEMBERS - pair_norm * ranks)).astype(jnp.bfloat16)

    def accumulate(carry, inputs):
        member_noise, sample_signal = inputs
        planar_map, margin_extended = member_field(member_noise)
        ignored_entry, stored_intermediates = sample_evaluation(planar_map, margin_extended, stencil_taps, affine_factor, widen_matrix, shrink_matrix, readout_matrix)
        sensitivities = reverse_sample_sweep(margin_extended, sample_signal.reshape(OUTPUT_QUANTITY, MERIDIAN_SPAN * ZONAL_SPAN), stored_intermediates, affine_factor, widen_matrix, shrink_matrix, readout_matrix)
        return (jax.tree.map(jnp.add, carry, sensitivities), None)
    begin_offset = (jnp.zeros((STENCIL_SIDE * STENCIL_SIDE, CHANNEL_COUNT), jnp.float32), jnp.zeros((CHANNEL_COUNT,), jnp.float32), jnp.zeros((EXPANSION_WIDTH, CHANNEL_COUNT), jnp.float32), jnp.zeros((EXPANSION_WIDTH, CHANNEL_COUNT), jnp.float32), jnp.zeros((OUTPUT_QUANTITY, CHANNEL_COUNT), jnp.float32))
    (stencil_taps_sensitivity, affine_factor_sensitivity, widen_matrix_sensitivity, shrink_matrix_sensitivity, readout_matrix_sensitivity), ignored_entry = lax.scan(accumulate, begin_offset, (random_perturbation, flows))
    sample_average_spread = spread / (MEMBERS - 1)
    return (crps_score, stencil_taps_sensitivity, affine_factor_sensitivity, widen_matrix_sensitivity, shrink_matrix_sensitivity, readout_matrix_sensitivity, sample_outlooks, sample_average_spread)
```

```python
import math

import jax
import jax.numpy as jnp
from jax import lax
from jax.sharding import PartitionSpec as P

STENCIL_SIDE = 7
SQRT_TWO_PI = 0.7978845608028654
CUBIC = 0.044715
EPSILON = 1e-06
SMOOTHING = 0.01
PER_CHUNK = 5
CHUNK_ROWS = 8


def core_swap(value):
    count = lax.axis_size("lat")
    return lax.ppermute(value, "lat", [(i, i ^ 1) for i in range(count)])


def odd_swap(value):
    count = lax.axis_size("lat")
    pairs = [(i, i + 1) for i in range(1, count - 1, 2)]
    return lax.ppermute(value, "lat", pairs + [(b, a) for a, b in pairs])


def halo_rows(field, half):
    even = lax.rem(lax.axis_index("lat"), 2) == 0
    head, tail = field[:half], field[field.shape[0] - half :]
    partner = core_swap(jnp.where(even, tail, head))
    other = odd_swap(jnp.where(even, head, tail))
    above = jnp.where(even, other, partner)
    below = jnp.where(even, partner, other)
    return above, below


def exchange(value, axis, groups=None):
    return lax.all_to_all(value, axis, 0, 0, tiled=True, axis_index_groups=groups)


def gelu_parts(u):
    inner = jnp.tanh(SQRT_TWO_PI * (u + CUBIC * u * u * u))
    value = 0.5 * u * (1.0 + inner)
    slope = 0.5 * (1.0 + inner) + 0.5 * u * (1.0 - inner * inner) * SQRT_TWO_PI * (
        1.0 + 3.0 * CUBIC * u * u
    )
    return value, slope


def depthwise(extended, taps, rows):
    half = STENCIL_SIDE // 2
    wide = extended.astype(jnp.float32)
    result = jnp.zeros((rows,) + wide.shape[1:], jnp.float32)
    for a in range(STENCIL_SIDE):
        band = wide[a : a + rows]
        for b in range(STENCIL_SIDE):
            result = result + taps[a * STENCIL_SIDE + b] * jnp.roll(band, half - b, axis=1)
    return result


def kernel_grad(extended, upstream):
    half = STENCIL_SIDE // 2
    wide = extended.astype(jnp.float32)
    rows, _, channels = upstream.shape
    taps = []
    for a in range(STENCIL_SIDE):
        band = wide[a : a + rows]
        for b in range(STENCIL_SIDE):
            shifted = jnp.roll(band, half - b, axis=1)
            taps.append(jnp.sum((upstream * shifted).reshape(-1, channels), axis=0))
    return jnp.stack(taps)


def spread_rows(table, members):
    width = table.shape[1]
    table = jnp.pad(table, ((0, members * PER_CHUNK - table.shape[0]), (0, 0)))
    table = table.reshape(members, PER_CHUNK, width)
    table = jnp.pad(table, ((0, 0), (0, CHUNK_ROWS - PER_CHUNK), (0, 0)))
    return table.reshape(members * CHUNK_ROWS, width)


def gather_rows(table, members, variables):
    width = table.shape[1]
    table = table.reshape(members, CHUNK_ROWS, width)[:, :PER_CHUNK]
    return table.reshape(members * PER_CHUNK, width)[:variables]


def on_device(
    features,
    random_perturbation,
    observed_truth,
    stencil_taps,
    affine_factor,
    widen_matrix,
    shrink_matrix,
    readout_matrix,
):
    f32, bf16 = jnp.float32, jnp.bfloat16
    rows, zonal, channels = features.shape
    variables = readout_matrix.shape[0]
    half = STENCIL_SIDE // 2
    bands, members = lax.axis_size("lat"), lax.axis_size("ens")
    band, member = lax.axis_index("lat"), lax.axis_index("ens")
    core = lax.rem(band, 2)
    points = rows * zonal
    latitudes = rows * bands
    owned = widen_matrix.shape[0]
    hidden = owned * bands

    field = (features.astype(f32) + random_perturbation[0].astype(f32)).astype(bf16)
    pair = jnp.concatenate([widen_matrix, shrink_matrix], axis=0)
    both = exchange(jnp.broadcast_to(pair[None], (bands,) + pair.shape), "lat")
    above, below = halo_rows(field, half)
    extended = jnp.concatenate([above, field, below], axis=0)
    widen = both[:, :owned].reshape(hidden, channels)
    shrink = both[:, owned:].reshape(hidden, channels)

    depth = depthwise(extended, stencil_taps, rows)
    centred = depth - jnp.mean(depth, axis=-1, keepdims=True)
    inverse = lax.rsqrt(jnp.mean(centred * centred, axis=-1, keepdims=True) + EPSILON)
    scaled = centred * inverse
    normed = (affine_factor * scaled).astype(bf16).reshape(points, channels)
    upper = lax.dot_general(normed, widen, (((1,), (1,)), ((), ())), preferred_element_type=f32)
    value, slope = gelu_parts(upper)
    gated = value.astype(bf16)
    mixed = jnp.dot(gated, shrink, preferred_element_type=f32)
    residual = (field.reshape(points, channels).astype(f32) + mixed).astype(bf16)
    readout_spread = spread_rows(readout_matrix, members)
    outlook_spread = lax.dot_general(
        readout_spread, residual, (((1,), (1,)), ((), ())), preferred_element_type=f32
    ).astype(bf16)
    sample_outlook = gather_rows(outlook_spread, members, variables).reshape(
        1, variables, rows, zonal
    )

    everyone = exchange(outlook_spread.reshape(members, CHUNK_ROWS, points), "ens").astype(f32)
    truth = lax.dynamic_index_in_dim(
        spread_rows(observed_truth.reshape(variables, points), members).reshape(
            members, CHUNK_ROWS, points
        ),
        member,
        0,
        keepdims=False,
    )
    latitude = (band * rows + jnp.arange(points, dtype=jnp.int32) // zonal).astype(f32)
    area = jnp.cos(math.pi * ((latitude + 0.5) / latitudes - 0.5))
    weight = (area * (1.0 / (latitudes * zonal)))[None, None, :]
    real = (
        lax.broadcasted_iota(jnp.int32, (1, CHUNK_ROWS, 1), 1)
        < jnp.minimum(PER_CHUNK, variables - member * PER_CHUNK)
    )
    pair_norm = 1.0 / (members * (members - 1))
    gap = everyone[:, None] - everyone[None]
    square = gap * gap + SMOOTHING
    root = lax.rsqrt(square)
    spread = jnp.sum(square * root, axis=1)
    ranks = jnp.sum(gap * root, axis=1)
    miss = everyone - truth[None]
    square = miss * miss + SMOOTHING
    root = lax.rsqrt(square)
    loss = jnp.sum(
        jnp.where(real, weight * (square * root / members - 0.5 * pair_norm * spread), 0.0)
    )
    flow = (weight * (miss * root / members - pair_norm * ranks)).astype(bf16)
    average = (spread / (members - 1)).astype(bf16)
    back = exchange(jnp.concatenate([flow, average], axis=1), "ens")
    flow = back[:, :CHUNK_ROWS].reshape(members * CHUNK_ROWS, points)
    sample_average_spread = (
        gather_rows(back[:, CHUNK_ROWS:].reshape(members * CHUNK_ROWS, points), members, variables)
        .astype(f32)
        .reshape(1, variables, rows, zonal)
    )

    readout_grad = gather_rows(
        jnp.dot(flow, residual, preferred_element_type=f32), members, variables
    )
    back_residual = lax.dot_general(
        flow, readout_spread, (((0,), (0,)), ((), ())), preferred_element_type=f32
    ).astype(bf16)
    shrink_grad = lax.dot_general(
        gated, back_residual, (((0,), (0,)), ((), ())), preferred_element_type=f32
    )
    back_gate = lax.dot_general(
        back_residual, shrink, (((1,), (1,)), ((), ())), preferred_element_type=f32
    )
    back_upper = (back_gate * slope).astype(bf16)
    widen_grad = lax.dot_general(
        back_upper, normed, (((0,), (0,)), ((), ())), preferred_element_type=f32
    )
    back_norm = jnp.dot(back_upper, widen, preferred_element_type=f32).reshape(
        rows, zonal, channels
    )
    gain_grad = jnp.sum((back_norm * scaled).reshape(-1, channels), axis=0)
    g = back_norm * affine_factor
    back_depth = inverse * (
        g
        - jnp.mean(g, axis=-1, keepdims=True)
        - scaled * jnp.mean(g * scaled, axis=-1, keepdims=True)
    )
    taps_grad = kernel_grad(extended, back_depth)

    small = jnp.concatenate(
        [
            readout_grad,
            taps_grad,
            gain_grad[None],
            jnp.broadcast_to(loss, (1, channels)),
            jnp.zeros((128 - variables - 51, channels), f32),
        ],
        axis=0,
    )
    halves = bands // 2
    share = 128 // (2 * members)
    big = jnp.stack([widen_grad, shrink_grad]).reshape(2, halves, 2, members, channels)
    packed = jnp.concatenate(
        [
            big.transpose(2, 3, 0, 1, 4).reshape(2, members, 2 * halves, channels),
            small.reshape(2, members, share, channels),
        ],
        axis=2,
    )
    mine = lax.dynamic_index_in_dim(packed, core, 0, keepdims=False)
    theirs = core_swap(lax.dynamic_index_in_dim(packed, 1 - core, 0, keepdims=False))
    part = jnp.sum(exchange(mine + theirs, "ens"), axis=0)
    same_core = [list(range(c, bands, 2)) for c in range(2)]
    outgoing = jnp.concatenate(
        [
            part[: 2 * halves].reshape(2, halves, channels).transpose(1, 0, 2),
            jnp.broadcast_to(part[None, 2 * halves :], (halves, share, channels)),
        ],
        axis=1,
    )
    done = jnp.sum(exchange(outgoing, "lat", same_core), axis=0)
    final = exchange(jnp.broadcast_to(done[None], (members,) + done.shape), "ens")
    owned_up, owned_down = final[:, 0], final[:, 1]
    half_small = final[:, 2:].reshape(members * share, channels)
    other_small = core_swap(half_small)
    low = jnp.where(core == 0, half_small, other_small)
    high = jnp.where(core == 0, other_small, half_small)
    small = jnp.concatenate([low, high], axis=0)
    return (
        small[variables + 50, 0],
        small[variables : variables + 49],
        small[variables + 49],
        owned_up,
        owned_down,
        small[:variables],
        sample_outlook,
        sample_average_spread,
    )


def solution(mesh):
    in_specs = (
        P("lat", None, None),
        P("ens", "lat", None, None),
        P(None, "lat", None),
        P(),
        P(),
        P("lat", None),
        P("lat", None),
        P(),
    )
    out_specs = (
        P(),
        P(),
        P(),
        P("lat", None),
        P("lat", None),
        P(),
        P("ens", None, "lat", None),
        P("ens", None, "lat", None),
    )
    return jax.shard_map(
        on_device, mesh=mesh, in_specs=in_specs, out_specs=out_specs, check_vma=False
    )
```

```python
import math

import jax
import jax.numpy as jnp
from jax import lax
from jax.sharding import PartitionSpec as P

STENCIL_SIDE = 7
SQRT_TWO_PI = 0.7978845608028654
CUBIC = 0.044715
EPSILON = 1e-06
SMOOTHING = 0.01
PER_CHUNK = 5
CHUNK_ROWS = 8


def core_swap(value):
    count = lax.axis_size("lat")
    return lax.ppermute(value, "lat", [(i, i ^ 1) for i in range(count)])


def odd_swap(value):
    count = lax.axis_size("lat")
    pairs = [(i, i + 1) for i in range(1, count - 1, 2)]
    return lax.ppermute(value, "lat", pairs + [(b, a) for a, b in pairs])


def halo_rows(field, half):
    even = lax.rem(lax.axis_index("lat"), 2) == 0
    head, tail = field[:half], field[field.shape[0] - half :]
    partner = core_swap(jnp.where(even, tail, head))
    other = odd_swap(jnp.where(even, head, tail))
    above = jnp.where(even, other, partner)
    below = jnp.where(even, partner, other)
    return above, below


def exchange(value, axis, groups=None):
    return lax.all_to_all(value, axis, 0, 0, tiled=True, axis_index_groups=groups)


AXES = ("ens", "lat")


def weight_groups(members, bands):
    def at(e, band):
        e = e if band < bands // 2 else e // 4 * 4 + (e + 2) % 4
        return e * bands + band

    return [[at(e, band) for band in range(bands)] for e in range(members)]


def plane_groups(members, bands):
    half = bands // 2
    return [
        [e * bands + h * half + rest for e in range(members) for h in range(2)]
        for rest in range(half)
    ]


def gelu_parts(u):
    inner = jnp.tanh(SQRT_TWO_PI * (u + CUBIC * u * u * u))
    value = 0.5 * u * (1.0 + inner)
    slope = 0.5 * (1.0 + inner) + 0.5 * u * (1.0 - inner * inner) * SQRT_TWO_PI * (
        1.0 + 3.0 * CUBIC * u * u
    )
    return value, slope


def depthwise(extended, taps, rows):
    half = STENCIL_SIDE // 2
    wide = extended.astype(jnp.float32)
    result = jnp.zeros((rows,) + wide.shape[1:], jnp.float32)
    for a in range(STENCIL_SIDE):
        band = wide[a : a + rows]
        for b in range(STENCIL_SIDE):
            result = result + taps[a * STENCIL_SIDE + b] * jnp.roll(band, half - b, axis=1)
    return result


def kernel_grad(extended, upstream):
    half = STENCIL_SIDE // 2
    wide = extended.astype(jnp.float32)
    rows, _, channels = upstream.shape
    taps = []
    for a in range(STENCIL_SIDE):
        band = wide[a : a + rows]
        for b in range(STENCIL_SIDE):
            shifted = jnp.roll(band, half - b, axis=1)
            taps.append(jnp.sum((upstream * shifted).reshape(-1, channels), axis=0))
    return jnp.stack(taps)


def spread_rows(table, members):
    width = table.shape[1]
    table = jnp.pad(table, ((0, members * PER_CHUNK - table.shape[0]), (0, 0)))
    table = table.reshape(members, PER_CHUNK, width)
    table = jnp.pad(table, ((0, 0), (0, CHUNK_ROWS - PER_CHUNK), (0, 0)))
    return table.reshape(members * CHUNK_ROWS, width)


def gather_rows(table, members, variables):
    width = table.shape[1]
    table = table.reshape(members, CHUNK_ROWS, width)[:, :PER_CHUNK]
    return table.reshape(members * PER_CHUNK, width)[:variables]


def on_device(
    features,
    random_perturbation,
    observed_truth,
    stencil_taps,
    affine_factor,
    widen_matrix,
    shrink_matrix,
    readout_matrix,
):
    f32, bf16 = jnp.float32, jnp.bfloat16
    rows, zonal, channels = features.shape
    variables = readout_matrix.shape[0]
    half = STENCIL_SIDE // 2
    bands, members = lax.axis_size("lat"), lax.axis_size("ens")
    band, member = lax.axis_index("lat"), lax.axis_index("ens")
    core = lax.rem(band, 2)
    points = rows * zonal
    latitudes = rows * bands
    owned = widen_matrix.shape[0]
    hidden = owned * bands

    field = (features.astype(f32) + random_perturbation[0].astype(f32)).astype(bf16)
    pair = jnp.concatenate([widen_matrix, shrink_matrix], axis=0)
    both = exchange(
        jnp.broadcast_to(pair[None], (bands,) + pair.shape), AXES, weight_groups(members, bands)
    )
    above, below = halo_rows(field, half)
    extended = jnp.concatenate([above, field, below], axis=0)
    widen = both[:, :owned].reshape(hidden, channels)
    shrink = both[:, owned:].reshape(hidden, channels)

    depth = depthwise(extended, stencil_taps, rows)
    centred = depth - jnp.mean(depth, axis=-1, keepdims=True)
    inverse = lax.rsqrt(jnp.mean(centred * centred, axis=-1, keepdims=True) + EPSILON)
    scaled = centred * inverse
    normed = (affine_factor * scaled).astype(bf16).reshape(points, channels)
    upper = lax.dot_general(normed, widen, (((1,), (1,)), ((), ())), preferred_element_type=f32)
    value, slope = gelu_parts(upper)
    gated = value.astype(bf16)
    mixed = jnp.dot(gated, shrink, preferred_element_type=f32)
    residual = (field.reshape(points, channels).astype(f32) + mixed).astype(bf16)
    readout_spread = spread_rows(readout_matrix, members)
    outlook_spread = lax.dot_general(
        readout_spread, residual, (((1,), (1,)), ((), ())), preferred_element_type=f32
    ).astype(bf16)
    sample_outlook = gather_rows(outlook_spread, members, variables).reshape(
        1, variables, rows, zonal
    )

    everyone = exchange(outlook_spread.reshape(members, CHUNK_ROWS, points), "ens").astype(f32)
    truth = lax.dynamic_index_in_dim(
        spread_rows(observed_truth.reshape(variables, points), members).reshape(
            members, CHUNK_ROWS, points
        ),
        member,
        0,
        keepdims=False,
    )
    latitude = (band * rows + jnp.arange(points, dtype=jnp.int32) // zonal).astype(f32)
    area = jnp.cos(math.pi * ((latitude + 0.5) / latitudes - 0.5))
    weight = (area * (1.0 / (latitudes * zonal)))[None, None, :]
    real = (
        lax.broadcasted_iota(jnp.int32, (1, CHUNK_ROWS, 1), 1)
        < jnp.minimum(PER_CHUNK, variables - member * PER_CHUNK)
    )
    pair_norm = 1.0 / (members * (members - 1))
    gap = everyone[:, None] - everyone[None]
    square = gap * gap + SMOOTHING
    root = lax.rsqrt(square)
    spread = jnp.sum(square * root, axis=1)
    ranks = jnp.sum(gap * root, axis=1)
    miss = everyone - truth[None]
    square = miss * miss + SMOOTHING
    root = lax.rsqrt(square)
    loss = jnp.sum(
        jnp.where(real, weight * (square * root / members - 0.5 * pair_norm * spread), 0.0)
    )
    flow = (weight * (miss * root / members - pair_norm * ranks)).astype(bf16)
    average = (spread / (members - 1)).astype(bf16)
    back = exchange(jnp.concatenate([flow, average], axis=1), "ens")
    flow = back[:, :CHUNK_ROWS].reshape(members * CHUNK_ROWS, points)
    sample_average_spread = (
        gather_rows(back[:, CHUNK_ROWS:].reshape(members * CHUNK_ROWS, points), members, variables)
        .astype(f32)
        .reshape(1, variables, rows, zonal)
    )

    readout_grad = gather_rows(
        jnp.dot(flow, residual, preferred_element_type=f32), members, variables
    )
    back_residual = lax.dot_general(
        flow, readout_spread, (((0,), (0,)), ((), ())), preferred_element_type=f32
    ).astype(bf16)
    shrink_grad = lax.dot_general(
        gated, back_residual, (((0,), (0,)), ((), ())), preferred_element_type=f32
    )
    back_gate = lax.dot_general(
        back_residual, shrink, (((1,), (1,)), ((), ())), preferred_element_type=f32
    )
    back_upper = (back_gate * slope).astype(bf16)
    widen_grad = lax.dot_general(
        back_upper, normed, (((0,), (0,)), ((), ())), preferred_element_type=f32
    )
    back_norm = jnp.dot(back_upper, widen, preferred_element_type=f32).reshape(
        rows, zonal, channels
    )
    gain_grad = jnp.sum((back_norm * scaled).reshape(-1, channels), axis=0)
    g = back_norm * affine_factor
    back_depth = inverse * (
        g
        - jnp.mean(g, axis=-1, keepdims=True)
        - scaled * jnp.mean(g * scaled, axis=-1, keepdims=True)
    )
    taps_grad = kernel_grad(extended, back_depth)

    small = jnp.concatenate(
        [
            readout_grad,
            taps_grad,
            gain_grad[None],
            jnp.broadcast_to(loss, (1, channels)),
            jnp.zeros((128 - variables - 51, channels), f32),
        ],
        axis=0,
    )
    depth_z = bands // 4
    share = 128 // members
    big = jnp.stack([widen_grad, shrink_grad]).reshape(2, 2, depth_z, 2, members, channels)
    big = big.transpose(3, 4, 1, 0, 2, 5).reshape(2, 2 * members, 2 * depth_z, channels)
    tail = jnp.broadcast_to(
        small.reshape(members, 1, share, channels), (members, 2, share, channels)
    ).reshape(2 * members, share, channels)
    mine = lax.dynamic_index_in_dim(big, core, 0, keepdims=False)
    sent = lax.dynamic_index_in_dim(big, 1 - core, 0, keepdims=False)
    theirs = core_swap(jnp.concatenate([sent, tail], axis=1))
    both_cores = jnp.concatenate([mine, tail], axis=1) + theirs
    part = jnp.sum(exchange(both_cores, AXES, plane_groups(members, bands)), axis=0)
    columns = [
        list(range(h * bands // 2 + c, (h + 1) * bands // 2, 2)) for h in range(2) for c in range(2)
    ]
    outgoing = jnp.concatenate(
        [
            part[: 2 * depth_z].reshape(2, depth_z, channels).transpose(1, 0, 2),
            jnp.broadcast_to(part[None, 2 * depth_z :], (depth_z, share, channels)),
        ],
        axis=1,
    )
    done = jnp.sum(exchange(outgoing, "lat", columns), axis=0)
    final = exchange(jnp.broadcast_to(done[None], (members,) + done.shape), "ens")
    owned_up, owned_down = final[:, 0], final[:, 1]
    small = final[:, 2:].reshape(members * share, channels)
    return (
        small[variables + 50, 0],
        small[variables : variables + 49],
        small[variables + 49],
        owned_up,
        owned_down,
        small[:variables],
        sample_outlook,
        sample_average_spread,
    )


def solution(mesh):
    in_specs = (
        P("lat", None, None),
        P("ens", "lat", None, None),
        P(None, "lat", None),
        P(),
        P(),
        P("lat", None),
        P("lat", None),
        P(),
    )
    out_specs = (
        P(),
        P(),
        P(),
        P("lat", None),
        P("lat", None),
        P(),
        P("ens", None, "lat", None),
        P("ens", None, "lat", None),
    )
    return jax.shard_map(
        on_device, mesh=mesh, in_specs=in_specs, out_specs=out_specs, check_vma=False
    )
```

```python
import math

import jax
import jax.numpy as jnp
from jax import lax
from jax.experimental import pallas as pl
from jax.experimental.pallas import tpu as pltpu
from jax.sharding import PartitionSpec as P

STENCIL_SIDE = 7
SQRT_TWO_PI = 0.7978845608028654
CUBIC = 0.044715
EPSILON = 1e-06
SMOOTHING = 0.01
PER_CHUNK = 5
CHUNK_ROWS = 8
EDGE = 8
STRIP = 16
TAPS_AT = 69
DEPTH_Z = 8
F32, BF16 = jnp.float32, jnp.bfloat16


def core_swap(value):
    count = lax.axis_size("lat")
    return lax.ppermute(value, "lat", [(i, i ^ 1) for i in range(count)])


def odd_swap(value):
    count = lax.axis_size("lat")
    pairs = [(i, i + 1) for i in range(1, count - 1, 2)]
    return lax.ppermute(value, "lat", pairs + [(b, a) for a, b in pairs])


def halo_rows(field, half):
    even = lax.rem(lax.axis_index("lat"), 2) == 0
    head, tail = field[:half], field[field.shape[0] - half :]
    return core_swap(jnp.where(even, tail, head)), odd_swap(jnp.where(even, head, tail))


def exchange(value, axis, groups=None):
    return lax.all_to_all(value, axis, 0, 0, tiled=True, axis_index_groups=groups)


AXES = ("ens", "lat")


def weight_groups(members, bands):
    def at(e, band):
        e = e if band < bands // 2 else e // 4 * 4 + (e + 2) % 4
        return e * bands + band

    return [[at(e, band) for band in range(bands)] for e in range(members)]


def plane_groups(members, bands):
    half = bands // 2
    return [
        [e * bands + h * half + rest for e in range(members) for h in range(2)]
        for rest in range(half)
    ]


def gelu_parts(u):
    inner = jnp.tanh(SQRT_TWO_PI * (u + CUBIC * u * u * u))
    value = 0.5 * u * (1.0 + inner)
    slope = 0.5 * (1.0 + inner) + 0.5 * u * (1.0 - inner * inner) * SQRT_TWO_PI * (
        1.0 + 3.0 * CUBIC * u * u
    )
    return value, slope


def vmem_call(body, outs, scratch=(), scalars=0, vectors=0):
    vmem = pl.BlockSpec(memory_space=pltpu.VMEM)
    smem = pl.BlockSpec(memory_space=pltpu.SMEM)
    return pl.pallas_call(
        body,
        out_shape=[jax.ShapeDtypeStruct(shape, dtype) for shape, dtype in outs],
        in_specs=[smem] * scalars + [vmem] * vectors,
        out_specs=[vmem] * len(outs),
        scratch_shapes=list(scratch),
    )


def dot(a, b, contract):
    return lax.dot_general(a, b, ((contract[:1], contract[1:]), ((), ())), preferred_element_type=F32)


def stencil_body(place, field, partner, other, taps, gain, ext, scaled, inverse, normed):
    even = place[0] == 0
    rows, zonal, _ = field.shape
    half = STENCIL_SIDE // 2
    for r in range(rows + 2 * half):
        if r < half:
            row = jnp.where(even, other[r].astype(F32), partner[r].astype(F32))
        elif r < rows + half:
            row = field[r - half].astype(F32)
        else:
            k = r - rows - half
            row = jnp.where(even, partner[k].astype(F32), other[k].astype(F32))
        ext[r, EDGE : EDGE + zonal, :] = row
        ext[r, EDGE - half : EDGE, :] = row[zonal - half :]
        ext[r, EDGE + zonal : EDGE + zonal + half, :] = row[:half]
    for start in range(0, zonal, STRIP):
        total = jnp.zeros((rows, STRIP, field.shape[2]), F32)
        for b in range(STENCIL_SIDE):
            first = EDGE - half + b + start
            slab = ext[:, first : first + STRIP, :]
            for a in range(STENCIL_SIDE):
                k = a * STENCIL_SIDE + b
                total = total + taps[k : k + 1, :][None] * slab[a : a + rows]
        centred = total - jnp.mean(total, axis=-1, keepdims=True)
        recip = lax.rsqrt(jnp.mean(centred * centred, axis=-1, keepdims=True) + EPSILON)
        value = centred * recip
        rounded = (gain[...][None] * value).astype(BF16)
        wide = jnp.broadcast_to(recip, value.shape)
        for i in range(rows):
            at = pl.ds(i * zonal + start, STRIP)
            scaled[at, :] = value[i]
            inverse[at, :] = wide[i]
            normed[at, :] = rounded[i]


def selector(rows, columns, chunk_bits, offsets, turned):
    place = lax.broadcasted_iota(jnp.int32, (rows, columns), 1 if turned else 0)
    variable = lax.broadcasted_iota(jnp.int32, (rows, columns), 0 if turned else 1)
    chunk = lax.shift_right_logical(place, chunk_bits)
    inside = place & ((1 << chunk_bits) - 1)
    result = jnp.zeros((rows, columns), F32)
    for offset in offsets:
        j = inside - offset
        hit = (j >= 0) & (j < PER_CHUNK) & (chunk * PER_CHUNK + j == variable)
        result = jnp.where(hit, 1.0, result)
    return result.astype(BF16)


def mlp_body(normed, both, field, readout, gated, slope, residual, chunks, upper):
    owned = both.shape[1] // 2
    hidden, channels = both.shape[0] * owned, both.shape[2]
    points = normed.shape[0]
    widen = both[:, :owned, :].reshape(hidden, channels)
    shrink = both[:, owned:, :].reshape(hidden, channels)
    upper[...] = dot(normed[...], widen, (1, 1))

    def step(i, carry):
        at = pl.ds(pl.multiple_of(i * 16, 16), 16)
        value, tilt = gelu_parts(upper[at, :])
        gated[at, :] = value.astype(BF16)
        slope[at, :] = tilt
        return carry

    lax.fori_loop(0, points // 16, step, 0, unroll=2)
    mixed = dot(gated[...], shrink, (1, 0))
    residual[...] = (field[...].reshape(points, channels).astype(F32) + mixed).astype(BF16)
    members = chunks.shape[0]
    spread = dot(selector(members * CHUNK_ROWS, readout.shape[0], 3, (0,), False), readout[...], (1, 0))
    outlook = dot(spread.astype(BF16), residual[...], (1, 1))
    for e in range(members):
        chunks[e] = outlook[e * CHUNK_ROWS : (e + 1) * CHUNK_ROWS].astype(BF16)


def outlook_body(readout, residual, out):
    out[...] = dot(readout[...], residual[...], (1, 1)).astype(BF16)


def pair_body(place, everyone, truth, weight, payload, loss, rows, seen):
    member = place[1]
    members, _, points = everyone.shape
    variables, bands, lanes = truth.shape
    for j in range(PER_CHUNK):
        row = truth[jnp.minimum(member * PER_CHUNK + j, variables - 1)]
        for q in range(bands):
            seen[j : j + 1, q * lanes : (q + 1) * lanes] = row[q : q + 1]
    seen[PER_CHUNK:, :] = jnp.zeros((CHUNK_ROWS - PER_CHUNK, points), F32)
    limit = jnp.minimum(PER_CHUNK, variables - member * PER_CHUNK)
    real = lax.broadcasted_iota(jnp.int32, (CHUNK_ROWS, lanes), 0) < limit
    pair_norm = 1.0 / (members * (members - 1))
    lost = jnp.zeros((CHUNK_ROWS, lanes), F32)
    for q in range(points // lanes):
        at = slice(q * lanes, (q + 1) * lanes)
        y = [everyone[m, :, at].astype(F32) for m in range(members)]
        spread = [jnp.full((CHUNK_ROWS, lanes), SMOOTHING**0.5, F32) for _ in range(members)]
        ranks = [jnp.zeros((CHUNK_ROWS, lanes), F32) for _ in range(members)]
        for m in range(members):
            for k in range(m):
                gap = y[m] - y[k]
                square = gap * gap + SMOOTHING
                root = lax.rsqrt(square)
                size, tilt = square * root, gap * root
                spread[m], spread[k] = spread[m] + size, spread[k] + size
                ranks[m], ranks[k] = ranks[m] + tilt, ranks[k] - tilt
        scale = weight[0:1, at]
        for m in range(members):
            miss = y[m] - seen[:, at]
            square = miss * miss + SMOOTHING
            root = lax.rsqrt(square)
            term = scale * (square * root * (1.0 / members) - 0.5 * pair_norm * spread[m])
            lost = lost + jnp.where(real, term, 0.0)
            flow = scale * (miss * root * (1.0 / members) - pair_norm * ranks[m])
            average = spread[m] * (1.0 / (members - 1))
            high = average.astype(BF16).astype(F32)
            rows[m, 0:CHUNK_ROWS, at] = jnp.where(real, flow, 0.0)
            rows[m, PER_CHUNK : PER_CHUNK + CHUNK_ROWS, at] = high
            rows[m, 2 * PER_CHUNK : 16, at] = (average - high)[: 16 - 2 * PER_CHUNK]
    for m in range(members):
        payload[m] = rows[m].astype(BF16)
    loss[...] = jnp.sum(lost, axis=0, keepdims=True)


def average_body(back, out):
    members, height, points = back.shape
    pick = selector(out.shape[0], members * height, 4, (PER_CHUNK, 2 * PER_CHUNK), True)
    out[...] = dot(pick, back[...].reshape(members * height, points), (1, 0))


def backward_body(
    back, readout, residual, gated, slope, normed, scaled, inverse, gain, both,
    widen_grad, shrink_grad, readout_grad, gain_grad, back_depth, gate, back_upper,
):
    members, height, points = back.shape
    owned = both.shape[1] // 2
    hidden, channels = both.shape[0] * owned, both.shape[2]
    widen = both[:, :owned, :].reshape(hidden, channels)
    shrink = both[:, owned:, :].reshape(hidden, channels)
    flow = back[...].reshape(members * height, points)
    spread = dot(selector(members * height, readout.shape[0], 4, (0,), False), readout[...], (1, 0))
    back_residual = dot(flow, spread.astype(BF16), (0, 0)).astype(BF16)
    gate[...] = dot(back_residual, shrink, (1, 1))
    readout_grad[...] = dot(flow, residual[...], (1, 0))
    shrink_grad[...] = dot(gated[...], back_residual, (0, 0))

    def step(i, carry):
        at = pl.ds(pl.multiple_of(i * 16, 16), 16)
        back_upper[at, :] = (gate[at, :] * slope[at, :]).astype(BF16)
        return carry

    lax.fori_loop(0, points // 16, step, 0, unroll=2)
    back_norm = dot(back_upper[...], widen, (1, 0))
    widen_grad[...] = dot(back_upper[...], normed[...], (0, 0))
    value = scaled[...]
    product = back_norm * value
    gain_grad[...] = jnp.sum(product, axis=0, keepdims=True)
    g = back_norm * gain[...]
    p = jnp.mean(g, axis=-1, keepdims=True)
    q = jnp.mean(g * value, axis=-1, keepdims=True)
    back_depth[...] = inverse[...] * (g - p - value * q)


def pack_body(place, back_depth, ext, widen_grad, shrink_grad, readout_grad, gain_grad, loss, send, keep, small):
    first_core = place[0] == 0
    half = STENCIL_SIDE // 2
    zonal = ext.shape[1] - 2 * EDGE
    rows = back_depth.shape[0] // zonal
    channels = ext.shape[2]
    members = small.shape[0] // CHUNK_ROWS
    height = readout_grad.shape[0] // members
    small[TAPS_AT + 48 :, :] = jnp.zeros((small.shape[0] - TAPS_AT - 48, channels), F32)
    for e in range(members):
        count = min(PER_CHUNK, TAPS_AT - e * PER_CHUNK)
        if count > 0:
            small[e * PER_CHUNK : e * PER_CHUNK + count, :] = readout_grad[e * height : e * height + count, :]
    for b in range(STENCIL_SIDE):
        totals = [jnp.zeros((STRIP, channels), F32) for _ in range(STENCIL_SIDE)]
        for start in range(0, zonal, STRIP):
            first = EDGE - half + b + start
            slab = ext[:, first : first + STRIP, :]
            up = [back_depth[i * zonal + start : i * zonal + start + STRIP, :] for i in range(rows)]
            for a in range(STENCIL_SIDE):
                for i in range(rows):
                    totals[a] = totals[a] + up[i] * slab[i + a]
        for a in range(STENCIL_SIDE):
            k = TAPS_AT + a * STENCIL_SIDE + b
            small[k : k + 1, :] = jnp.sum(totals[a], axis=0, keepdims=True)
    small[TAPS_AT + 49 : TAPS_AT + 50, :] = gain_grad[...]
    small[TAPS_AT + 50 : TAPS_AT + 51, :] = loss[...]
    depth_z = DEPTH_Z
    for e in range(members):
        tail = small[e * CHUNK_ROWS : (e + 1) * CHUNK_ROWS, :]
        for h in range(2):
            d = 2 * e + h
            for mat, grad in enumerate((widen_grad, shrink_grad)):
                base = h * depth_z * 2 * members + e
                even = grad[pl.ds(base, depth_z, stride=2 * members), :]
                odd = grad[pl.ds(base + members, depth_z, stride=2 * members), :]
                keep[d, mat * depth_z : (mat + 1) * depth_z, :] = jnp.where(first_core, even, odd)
                send[d, mat * depth_z : (mat + 1) * depth_z, :] = jnp.where(first_core, odd, even)
            keep[d, 2 * depth_z :, :] = tail
            send[d, 2 * depth_z :, :] = tail


def plane_body(arrived, out):
    total = jnp.sum(arrived[...], axis=0)
    depth_z = out.shape[0]
    for z in range(depth_z):
        out[z, 0:CHUNK_ROWS, :] = total[2 * depth_z :]
        out[z, CHUNK_ROWS : CHUNK_ROWS + 1, :] = total[z : z + 1]
        out[z, CHUNK_ROWS + 1 : CHUNK_ROWS + 2, :] = total[depth_z + z : depth_z + z + 1]


def column_body(arrived, out):
    out[...] = jnp.broadcast_to(jnp.sum(arrived[...], axis=0)[None], out.shape)


def final_body(arrived, up, down, taps, gain, readout, loss, small):
    members = arrived.shape[0]
    for e in range(members):
        small[e * CHUNK_ROWS : (e + 1) * CHUNK_ROWS, :] = arrived[e, 0:CHUNK_ROWS, :]
        up[e : e + 1, :] = arrived[e, CHUNK_ROWS : CHUNK_ROWS + 1, :]
        down[e : e + 1, :] = arrived[e, CHUNK_ROWS + 1 : CHUNK_ROWS + 2, :]
    readout[...] = small[0:TAPS_AT, :]
    taps[...] = small[TAPS_AT : TAPS_AT + 49, :]
    gain[...] = small[TAPS_AT + 49 : TAPS_AT + 50, :]
    loss[...] = jnp.sum(small[TAPS_AT + 50 : TAPS_AT + 51, :], axis=1, keepdims=True)


def on_device(
    features,
    random_perturbation,
    observed_truth,
    stencil_taps,
    affine_factor,
    widen_matrix,
    shrink_matrix,
    readout_matrix,
):
    rows, zonal, channels = features.shape
    variables = readout_matrix.shape[0]
    half = STENCIL_SIDE // 2
    bands, members = lax.axis_size("lat"), lax.axis_size("ens")
    band, member = lax.axis_index("lat"), lax.axis_index("ens")
    points = rows * zonal
    latitudes = rows * bands
    hidden = widen_matrix.shape[0] * bands
    depth_z = DEPTH_Z
    share = CHUNK_ROWS
    place = jnp.stack([lax.rem(band, 2), member]).astype(jnp.int32)
    gain = affine_factor.reshape(1, channels)

    pair = jnp.concatenate([widen_matrix, shrink_matrix], axis=0)
    both = exchange(
        jnp.broadcast_to(pair[None], (bands,) + pair.shape), AXES, weight_groups(members, bands)
    )
    field = (features.astype(F32) + random_perturbation[0].astype(F32)).astype(BF16)
    partner, other = halo_rows(field, half)
    latitude = (band * rows + jnp.arange(points, dtype=jnp.int32) // zonal).astype(F32)
    area = jnp.cos(math.pi * ((latitude + 0.5) / latitudes - 0.5))
    weight = (area * (1.0 / (latitudes * zonal)))[None, :]

    wide = (rows + 2 * half, zonal + 2 * EDGE, channels)
    ext, scaled, inverse, normed = vmem_call(
        stencil_body,
        [(wide, F32), ((points, channels), F32), ((points, channels), F32), ((points, channels), BF16)],
        scalars=1,
        vectors=5,
    )(place, field, partner, other, stencil_taps, gain)
    gated, slope, residual, chunks = vmem_call(
        mlp_body,
        [
            ((points, hidden), BF16),
            ((points, hidden), F32),
            ((points, channels), BF16),
            ((members, CHUNK_ROWS, points), BF16),
        ],
        [pltpu.VMEM((points, hidden), F32)],
        vectors=4,
    )(normed, both, field, readout_matrix)
    everyone = exchange(chunks, "ens")
    (outlook,) = vmem_call(outlook_body, [((variables, points), BF16)], vectors=2)(
        readout_matrix, residual
    )
    sample_outlook = outlook.reshape(1, variables, rows, zonal)
    payload, loss = vmem_call(
        pair_body,
        [((members, 16, points), BF16), ((1, zonal), F32)],
        [pltpu.VMEM((members, 16, points), F32), pltpu.VMEM((CHUNK_ROWS, points), F32)],
        scalars=1,
        vectors=3,
    )(place, everyone, observed_truth, weight)
    back = exchange(payload, "ens")
    (average,) = vmem_call(average_body, [((variables, points), F32)], vectors=1)(back)
    sample_average_spread = average.reshape(1, variables, rows, zonal)

    widen_grad, shrink_grad, readout_grad, gain_grad, back_depth = vmem_call(
        backward_body,
        [
            ((hidden, channels), F32),
            ((hidden, channels), F32),
            ((members * 16, channels), F32),
            ((1, channels), F32),
            ((points, channels), F32),
        ],
        [pltpu.VMEM((points, hidden), F32), pltpu.VMEM((points, hidden), BF16)],
        vectors=10,
    )(back, readout_matrix, residual, gated, slope, normed, scaled, inverse, gain, both)
    packet = ((2 * members, 2 * depth_z + share, channels), F32)
    send, keep = vmem_call(
        pack_body,
        [packet, packet],
        [pltpu.VMEM((members * share, channels), F32)],
        scalars=1,
        vectors=7,
    )(place, back_depth, ext, widen_grad, shrink_grad, readout_grad, gain_grad, loss)

    arrived = exchange(keep + core_swap(send), AXES, plane_groups(members, bands))
    columns = [
        list(range(h * bands // 2 + c, (h + 1) * bands // 2, 2)) for h in range(2) for c in range(2)
    ]
    (outgoing,) = vmem_call(plane_body, [((depth_z, share + 2, channels), F32)], vectors=1)(arrived)
    arrived = exchange(outgoing, "lat", columns)
    (outgoing,) = vmem_call(column_body, [((members, share + 2, channels), F32)], vectors=1)(arrived)
    arrived = exchange(outgoing, "ens")
    up, down, taps, gain_total, readout, loss = vmem_call(
        final_body,
        [
            ((members, channels), F32),
            ((members, channels), F32),
            ((STENCIL_SIDE * STENCIL_SIDE, channels), F32),
            ((1, channels), F32),
            ((variables, channels), F32),
            ((1, 1), F32),
        ],
        [pltpu.VMEM((members * share, channels), F32)],
        vectors=1,
    )(arrived)
    return (
        loss.reshape(()),
        taps,
        gain_total.reshape(channels),
        up,
        down,
        readout,
        sample_outlook,
        sample_average_spread,
    )


def solution(mesh):
    in_specs = (
        P("lat", None, None),
        P("ens", "lat", None, None),
        P(None, "lat", None),
        P(),
        P(),
        P("lat", None),
        P("lat", None),
        P(),
    )
    out_specs = (
        P(),
        P(),
        P(),
        P("lat", None),
        P("lat", None),
        P(),
        P("ens", None, "lat", None),
        P("ens", None, "lat", None),
    )
    return jax.shard_map(
        on_device, mesh=mesh, in_specs=in_specs, out_specs=out_specs, check_vma=False
    )
```

```python
import math

import jax
import jax.numpy as jnp
from jax import lax
from jax.experimental import pallas as pl
from jax.experimental.pallas import tpu as pltpu
from jax.sharding import PartitionSpec as P

STENCIL_SIDE = 7
SQRT_TWO_PI = 0.7978845608028654
CUBIC = 0.044715
EPSILON = 1e-06
SMOOTHING = 0.01
PER_CHUNK = 5
CHUNK_ROWS = 8
EDGE = 8
STRIP = 16
TAPS_AT = 69
DEPTH_Z = 8
F32, BF16 = jnp.float32, jnp.bfloat16


def core_swap(value):
    count = lax.axis_size("lat")
    return lax.ppermute(value, "lat", [(i, i ^ 1) for i in range(count)])


def odd_swap(value):
    count = lax.axis_size("lat")
    pairs = [(i, i + 1) for i in range(1, count - 1, 2)]
    return lax.ppermute(value, "lat", pairs + [(b, a) for a, b in pairs])


def halo_rows(field, half):
    even = lax.rem(lax.axis_index("lat"), 2) == 0
    head, tail = field[:half], field[field.shape[0] - half :]
    return core_swap(jnp.where(even, tail, head)), odd_swap(jnp.where(even, head, tail))


def exchange(value, axis, groups=None):
    return lax.all_to_all(value, axis, 0, 0, tiled=True, axis_index_groups=groups)


AXES = ("ens", "lat")


def weight_groups(members, bands):
    def at(e, band):
        e = e if band < bands // 2 else e // 4 * 4 + (e + 2) % 4
        return e * bands + band

    return [[at(e, band) for band in range(bands)] for e in range(members)]


def plane_groups(members, bands):
    half = bands // 2
    return [
        [e * bands + h * half + rest for e in range(members) for h in range(2)]
        for rest in range(half)
    ]


def gelu_value(u):
    inner = jnp.tanh(SQRT_TWO_PI * (u + CUBIC * u * u * u))
    return 0.5 * u * (1.0 + inner)


def gelu_slope(u):
    inner = jnp.tanh(SQRT_TWO_PI * (u + CUBIC * u * u * u))
    return 0.5 * (1.0 + inner) + 0.5 * u * (1.0 - inner * inner) * SQRT_TWO_PI * (
        1.0 + 3.0 * CUBIC * u * u
    )


def vmem_call(body, outs, scratch=(), scalars=0, vectors=0):
    vmem = pl.BlockSpec(memory_space=pltpu.VMEM)
    smem = pl.BlockSpec(memory_space=pltpu.SMEM)
    return pl.pallas_call(
        body,
        out_shape=[jax.ShapeDtypeStruct(shape, dtype) for shape, dtype in outs],
        in_specs=[smem] * scalars + [vmem] * vectors,
        out_specs=[vmem] * len(outs),
        scratch_shapes=list(scratch),
    )


def dot(a, b, contract):
    return lax.dot_general(a, b, ((contract[:1], contract[1:]), ((), ())), preferred_element_type=F32)


def stencil_body(place, field, partner, other, taps, gain, ext, scaled, inverse, normed):
    even = place[0] == 0
    rows, zonal, _ = field.shape
    half = STENCIL_SIDE // 2
    for r in range(rows + 2 * half):
        if r < half:
            row = jnp.where(even, other[r].astype(F32), partner[r].astype(F32))
        elif r < rows + half:
            row = field[r - half].astype(F32)
        else:
            k = r - rows - half
            row = jnp.where(even, partner[k].astype(F32), other[k].astype(F32))
        ext[r, EDGE : EDGE + zonal, :] = row
        ext[r, EDGE - half : EDGE, :] = row[zonal - half :]
        ext[r, EDGE + zonal : EDGE + zonal + half, :] = row[:half]
    for start in range(0, zonal, STRIP):
        total = jnp.zeros((rows, STRIP, field.shape[2]), F32)
        for b in range(STENCIL_SIDE):
            first = EDGE - half + b + start
            slab = ext[:, first : first + STRIP, :]
            for a in range(STENCIL_SIDE):
                k = a * STENCIL_SIDE + b
                total = total + taps[k : k + 1, :][None] * slab[a : a + rows]
        centred = total - jnp.mean(total, axis=-1, keepdims=True)
        recip = lax.rsqrt(jnp.mean(centred * centred, axis=-1, keepdims=True) + EPSILON)
        value = centred * recip
        rounded = (gain[...][None] * value).astype(BF16)
        wide = jnp.broadcast_to(recip, value.shape)
        for i in range(rows):
            at = pl.ds(i * zonal + start, STRIP)
            scaled[at, :] = value[i]
            inverse[at, :] = wide[i]
            normed[at, :] = rounded[i]


def selector(rows, columns, chunk_bits, offsets, turned):
    place = lax.broadcasted_iota(jnp.int32, (rows, columns), 1 if turned else 0)
    variable = lax.broadcasted_iota(jnp.int32, (rows, columns), 0 if turned else 1)
    chunk = lax.shift_right_logical(place, chunk_bits)
    inside = place & ((1 << chunk_bits) - 1)
    result = jnp.zeros((rows, columns), F32)
    for offset in offsets:
        j = inside - offset
        hit = (j >= 0) & (j < PER_CHUNK) & (chunk * PER_CHUNK + j == variable)
        result = jnp.where(hit, 1.0, result)
    return result.astype(BF16)


def mlp_body(normed, both, field, readout, gated, upper, residual, chunks):
    owned = both.shape[1] // 2
    hidden, channels = both.shape[0] * owned, both.shape[2]
    points = normed.shape[0]
    widen = both[:, :owned, :].reshape(hidden, channels)
    shrink = both[:, owned:, :].reshape(hidden, channels)
    upper[...] = dot(normed[...], widen, (1, 1))

    def step(i, carry):
        at = pl.ds(pl.multiple_of(i * 16, 16), 16)
        gated[at, :] = gelu_value(upper[at, :]).astype(BF16)
        return carry

    lax.fori_loop(0, points // 16, step, 0, unroll=2)
    mixed = dot(gated[...], shrink, (1, 0))
    residual[...] = (field[...].reshape(points, channels).astype(F32) + mixed).astype(BF16)
    members = chunks.shape[0]
    spread = dot(selector(members * CHUNK_ROWS, readout.shape[0], 3, (0,), False), readout[...], (1, 0))
    outlook = dot(spread.astype(BF16), residual[...], (1, 1))
    for e in range(members):
        chunks[e] = outlook[e * CHUNK_ROWS : (e + 1) * CHUNK_ROWS].astype(BF16)


def slope_body(upper, slope):
    def step(i, carry):
        at = pl.ds(pl.multiple_of(i * 16, 16), 16)
        slope[at, :] = gelu_slope(upper[at, :])
        return carry

    lax.fori_loop(0, upper.shape[0] // 16, step, 0, unroll=2)


def outlook_body(readout, residual, out):
    out[...] = dot(readout[...], residual[...], (1, 1)).astype(BF16)


def pair_body(place, everyone, truth, weight, payload, loss, rows, seen):
    member = place[1]
    members, _, points = everyone.shape
    variables, bands, lanes = truth.shape
    for j in range(PER_CHUNK):
        row = truth[jnp.minimum(member * PER_CHUNK + j, variables - 1)]
        for q in range(bands):
            seen[j : j + 1, q * lanes : (q + 1) * lanes] = row[q : q + 1]
    seen[PER_CHUNK:, :] = jnp.zeros((CHUNK_ROWS - PER_CHUNK, points), F32)
    limit = jnp.minimum(PER_CHUNK, variables - member * PER_CHUNK)
    real = lax.broadcasted_iota(jnp.int32, (CHUNK_ROWS, lanes), 0) < limit
    pair_norm = 1.0 / (members * (members - 1))
    lost = jnp.zeros((CHUNK_ROWS, lanes), F32)
    for q in range(points // lanes):
        at = slice(q * lanes, (q + 1) * lanes)
        y = [everyone[m, :, at].astype(F32) for m in range(members)]
        spread = [jnp.full((CHUNK_ROWS, lanes), SMOOTHING**0.5, F32) for _ in range(members)]
        ranks = [jnp.zeros((CHUNK_ROWS, lanes), F32) for _ in range(members)]
        for m in range(members):
            for k in range(m):
                gap = y[m] - y[k]
                square = gap * gap + SMOOTHING
                root = lax.rsqrt(square)
                size, tilt = square * root, gap * root
                spread[m], spread[k] = spread[m] + size, spread[k] + size
                ranks[m], ranks[k] = ranks[m] + tilt, ranks[k] - tilt
        scale = weight[0:1, at]
        for m in range(members):
            miss = y[m] - seen[:, at]
            square = miss * miss + SMOOTHING
            root = lax.rsqrt(square)
            term = scale * (square * root * (1.0 / members) - 0.5 * pair_norm * spread[m])
            lost = lost + jnp.where(real, term, 0.0)
            flow = scale * (miss * root * (1.0 / members) - pair_norm * ranks[m])
            average = spread[m] * (1.0 / (members - 1))
            high = average.astype(BF16).astype(F32)
            rows[m, 0:CHUNK_ROWS, at] = jnp.where(real, flow, 0.0)
            rows[m, PER_CHUNK : PER_CHUNK + CHUNK_ROWS, at] = high
            rows[m, 2 * PER_CHUNK : 16, at] = (average - high)[: 16 - 2 * PER_CHUNK]
    for m in range(members):
        payload[m] = rows[m].astype(BF16)
    loss[...] = jnp.sum(lost, axis=0, keepdims=True)


def average_body(back, out):
    members, height, points = back.shape
    pick = selector(out.shape[0], members * height, 4, (PER_CHUNK, 2 * PER_CHUNK), True)
    out[...] = dot(pick, back[...].reshape(members * height, points), (1, 0))


def backward_body(
    back, readout, residual, gated, slope, normed, scaled, inverse, gain, both,
    widen_grad, shrink_grad, readout_grad, gain_grad, back_depth, gate, back_upper,
):
    members, height, points = back.shape
    owned = both.shape[1] // 2
    hidden, channels = both.shape[0] * owned, both.shape[2]
    widen = both[:, :owned, :].reshape(hidden, channels)
    shrink = both[:, owned:, :].reshape(hidden, channels)
    flow = back[...].reshape(members * height, points)
    spread = dot(selector(members * height, readout.shape[0], 4, (0,), False), readout[...], (1, 0))
    back_residual = dot(flow, spread.astype(BF16), (0, 0)).astype(BF16)
    gate[...] = dot(back_residual, shrink, (1, 1))
    readout_grad[...] = dot(flow, residual[...], (1, 0))
    shrink_grad[...] = dot(gated[...], back_residual, (0, 0))

    def step(i, carry):
        at = pl.ds(pl.multiple_of(i * 16, 16), 16)
        back_upper[at, :] = (gate[at, :] * slope[at, :]).astype(BF16)
        return carry

    lax.fori_loop(0, points // 16, step, 0, unroll=2)
    back_norm = dot(back_upper[...], widen, (1, 0))
    widen_grad[...] = dot(back_upper[...], normed[...], (0, 0))
    value = scaled[...]
    product = back_norm * value
    gain_grad[...] = jnp.sum(product, axis=0, keepdims=True)
    g = back_norm * gain[...]
    p = jnp.mean(g, axis=-1, keepdims=True)
    q = jnp.mean(g * value, axis=-1, keepdims=True)
    back_depth[...] = inverse[...] * (g - p - value * q)


def pack_body(place, back_depth, ext, widen_grad, shrink_grad, readout_grad, gain_grad, loss, send, keep, small):
    first_core = place[0] == 0
    half = STENCIL_SIDE // 2
    zonal = ext.shape[1] - 2 * EDGE
    rows = back_depth.shape[0] // zonal
    channels = ext.shape[2]
    members = small.shape[0] // CHUNK_ROWS
    height = readout_grad.shape[0] // members
    small[TAPS_AT + 48 :, :] = jnp.zeros((small.shape[0] - TAPS_AT - 48, channels), F32)
    for e in range(members):
        count = min(PER_CHUNK, TAPS_AT - e * PER_CHUNK)
        if count > 0:
            small[e * PER_CHUNK : e * PER_CHUNK + count, :] = readout_grad[e * height : e * height + count, :]
    for b in range(STENCIL_SIDE):
        totals = [jnp.zeros((STRIP, channels), F32) for _ in range(STENCIL_SIDE)]
        for start in range(0, zonal, STRIP):
            first = EDGE - half + b + start
            slab = ext[:, first : first + STRIP, :]
            up = [back_depth[i * zonal + start : i * zonal + start + STRIP, :] for i in range(rows)]
            for a in range(STENCIL_SIDE):
                for i in range(rows):
                    totals[a] = totals[a] + up[i] * slab[i + a]
        for a in range(STENCIL_SIDE):
            k = TAPS_AT + a * STENCIL_SIDE + b
            small[k : k + 1, :] = jnp.sum(totals[a], axis=0, keepdims=True)
    small[TAPS_AT + 49 : TAPS_AT + 50, :] = gain_grad[...]
    small[TAPS_AT + 50 : TAPS_AT + 51, :] = loss[...]
    depth_z = DEPTH_Z
    for e in range(members):
        tail = small[e * CHUNK_ROWS : (e + 1) * CHUNK_ROWS, :]
        for h in range(2):
            d = 2 * e + h
            for mat, grad in enumerate((widen_grad, shrink_grad)):
                base = h * depth_z * 2 * members + e
                even = grad[pl.ds(base, depth_z, stride=2 * members), :]
                odd = grad[pl.ds(base + members, depth_z, stride=2 * members), :]
                keep[d, mat * depth_z : (mat + 1) * depth_z, :] = jnp.where(first_core, even, odd)
                send[d, mat * depth_z : (mat + 1) * depth_z, :] = jnp.where(first_core, odd, even)
            keep[d, 2 * depth_z :, :] = tail
            send[d, 2 * depth_z :, :] = tail


def gradient_body(
    place, back, readout, residual, gated, slope, normed, scaled, inverse, gain, both, ext, loss,
    send, keep, gate, back_upper, widen_grad, shrink_grad, readout_grad, gain_grad, back_depth, small,
):
    backward_body(
        back, readout, residual, gated, slope, normed, scaled, inverse, gain, both,
        widen_grad, shrink_grad, readout_grad, gain_grad, back_depth, gate, back_upper,
    )
    pack_body(
        place, back_depth, ext, widen_grad, shrink_grad, readout_grad, gain_grad, loss,
        send, keep, small,
    )


def final_body(arrived, up, down, taps, gain, readout, loss, small):
    members = arrived.shape[0]
    for e in range(members):
        small[e * CHUNK_ROWS : (e + 1) * CHUNK_ROWS, :] = arrived[e, 0:CHUNK_ROWS, :]
        up[e : e + 1, :] = arrived[e, CHUNK_ROWS : CHUNK_ROWS + 1, :]
        down[e : e + 1, :] = arrived[e, CHUNK_ROWS + 1 : CHUNK_ROWS + 2, :]
    readout[...] = small[0:TAPS_AT, :]
    taps[...] = small[TAPS_AT : TAPS_AT + 49, :]
    gain[...] = small[TAPS_AT + 49 : TAPS_AT + 50, :]
    loss[...] = jnp.sum(small[TAPS_AT + 50 : TAPS_AT + 51, :], axis=1, keepdims=True)


def on_device(
    features,
    random_perturbation,
    observed_truth,
    stencil_taps,
    affine_factor,
    widen_matrix,
    shrink_matrix,
    readout_matrix,
):
    rows, zonal, channels = features.shape
    variables = readout_matrix.shape[0]
    half = STENCIL_SIDE // 2
    bands, members = lax.axis_size("lat"), lax.axis_size("ens")
    band, member = lax.axis_index("lat"), lax.axis_index("ens")
    points = rows * zonal
    latitudes = rows * bands
    hidden = widen_matrix.shape[0] * bands
    depth_z = DEPTH_Z
    share = CHUNK_ROWS
    place = jnp.stack([lax.rem(band, 2), member]).astype(jnp.int32)
    gain = affine_factor.reshape(1, channels)

    field = (features.astype(F32) + random_perturbation[0].astype(F32)).astype(BF16)
    partner, other = halo_rows(field, half)
    shape = (bands,) + widen_matrix.shape
    pair = jnp.concatenate(
        [jnp.broadcast_to(widen_matrix[None], shape), jnp.broadcast_to(shrink_matrix[None], shape)],
        axis=1,
    )
    both = exchange(pair, AXES, weight_groups(members, bands))
    latitude = (band * rows + jnp.arange(points, dtype=jnp.int32) // zonal).astype(F32)
    area = jnp.cos(math.pi * ((latitude + 0.5) / latitudes - 0.5))
    weight = (area * (1.0 / (latitudes * zonal)))[None, :]

    wide = (rows + 2 * half, zonal + 2 * EDGE, channels)
    ext, scaled, inverse, normed = vmem_call(
        stencil_body,
        [(wide, F32), ((points, channels), F32), ((points, channels), F32), ((points, channels), BF16)],
        scalars=1,
        vectors=5,
    )(place, field, partner, other, stencil_taps, gain)
    gated, upper, residual, chunks = vmem_call(
        mlp_body,
        [
            ((points, hidden), BF16),
            ((points, hidden), F32),
            ((points, channels), BF16),
            ((members, CHUNK_ROWS, points), BF16),
        ],
        vectors=4,
    )(normed, both, field, readout_matrix)
    everyone = exchange(chunks, "ens")
    (slope,) = vmem_call(slope_body, [((points, hidden), F32)], vectors=1)(upper)
    (outlook,) = vmem_call(outlook_body, [((variables, points), BF16)], vectors=2)(
        readout_matrix, residual
    )
    sample_outlook = outlook.reshape(1, variables, rows, zonal)
    payload, loss = vmem_call(
        pair_body,
        [((members, 16, points), BF16), ((1, zonal), F32)],
        [pltpu.VMEM((members, 16, points), F32), pltpu.VMEM((CHUNK_ROWS, points), F32)],
        scalars=1,
        vectors=3,
    )(place, everyone, observed_truth, weight)
    back = exchange(payload, "ens")
    (average,) = vmem_call(average_body, [((variables, points), F32)], vectors=1)(back)
    sample_average_spread = average.reshape(1, variables, rows, zonal)

    packet = ((2 * members, 2 * depth_z + share, channels), F32)
    send, keep = vmem_call(
        gradient_body,
        [packet, packet],
        [
            pltpu.VMEM((points, hidden), F32),
            pltpu.VMEM((points, hidden), BF16),
            pltpu.VMEM((hidden, channels), F32),
            pltpu.VMEM((hidden, channels), F32),
            pltpu.VMEM((members * 16, channels), F32),
            pltpu.VMEM((1, channels), F32),
            pltpu.VMEM((points, channels), F32),
            pltpu.VMEM((members * share, channels), F32),
        ],
        scalars=1,
        vectors=12,
    )(
        place, back, readout_matrix, residual, gated, slope, normed, scaled, inverse, gain, both,
        ext, loss,
    )

    arrived = exchange(keep + core_swap(send), AXES, plane_groups(members, bands))
    columns = [
        list(range(h * bands // 2 + c, (h + 1) * bands // 2, 2)) for h in range(2) for c in range(2)
    ]
    part = jnp.sum(arrived, axis=0)
    outgoing = jnp.concatenate(
        [
            jnp.broadcast_to(part[None, 2 * depth_z :], (depth_z, share, channels)),
            part[: 2 * depth_z].reshape(2, depth_z, channels).transpose(1, 0, 2),
        ],
        axis=1,
    )
    done = jnp.sum(exchange(outgoing, "lat", columns), axis=0)
    arrived = exchange(jnp.broadcast_to(done[None], (members,) + done.shape), "ens")
    up, down, taps, gain_total, readout, loss = vmem_call(
        final_body,
        [
            ((members, channels), F32),
            ((members, channels), F32),
            ((STENCIL_SIDE * STENCIL_SIDE, channels), F32),
            ((1, channels), F32),
            ((variables, channels), F32),
            ((1, 1), F32),
        ],
        [pltpu.VMEM((members * share, channels), F32)],
        vectors=1,
    )(arrived)
    return (
        loss.reshape(()),
        taps,
        gain_total.reshape(channels),
        up,
        down,
        readout,
        sample_outlook,
        sample_average_spread,
    )


def solution(mesh):
    in_specs = (
        P("lat", None, None),
        P("ens", "lat", None, None),
        P(None, "lat", None),
        P(),
        P(),
        P("lat", None),
        P("lat", None),
        P(),
    )
    out_specs = (
        P(),
        P(),
        P(),
        P("lat", None),
        P("lat", None),
        P(),
        P("ens", None, "lat", None),
        P("ens", None, "lat", None),
    )

    return jax.shard_map(
        on_device, mesh=mesh, in_specs=in_specs, out_specs=out_specs, check_vma=False
    )
```

```python
import math

import jax
import jax.numpy as jnp
from jax import lax
from jax.experimental import pallas as pl
from jax.experimental.pallas import tpu as pltpu
from jax.sharding import PartitionSpec as P

STENCIL_SIDE = 7
SQRT_TWO_PI = 0.7978845608028654
CUBIC = 0.044715
EPSILON = 1e-06
SMOOTHING = 0.01
PER_CHUNK = 5
CHUNK_ROWS = 8
EDGE = 8
STRIP = 16
TAPS_AT = 69
DEPTH_Z = 8
F32, BF16 = jnp.float32, jnp.bfloat16


def core_swap(value):
    count = lax.axis_size("lat")
    return lax.ppermute(value, "lat", [(i, i ^ 1) for i in range(count)])


def odd_swap(value):
    count = lax.axis_size("lat")
    pairs = [(i, i + 1) for i in range(1, count - 1, 2)]
    return lax.ppermute(value, "lat", pairs + [(b, a) for a, b in pairs])


def halo_rows(field, half):
    even = lax.rem(lax.axis_index("lat"), 2) == 0
    head, tail = field[:half], field[field.shape[0] - half :]
    return core_swap(jnp.where(even, tail, head)), odd_swap(jnp.where(even, head, tail))


def exchange(value, axis, groups=None):
    return lax.all_to_all(value, axis, 0, 0, tiled=True, axis_index_groups=groups)


AXES = ("ens", "lat")


def weight_groups(members, bands):
    def at(e, band):
        e = e if band < bands // 2 else e // 4 * 4 + (e + 2) % 4
        return e * bands + band

    return [[at(e, band) for band in range(bands)] for e in range(members)]


def plane_groups(members, bands):
    half = bands // 2
    return [
        [e * bands + h * half + rest for e in range(members) for h in range(2)]
        for rest in range(half)
    ]


def gelu_value(u):
    inner = jnp.tanh(SQRT_TWO_PI * (u + CUBIC * u * u * u))
    return 0.5 * u * (1.0 + inner)


def gelu_slope(u):
    inner = jnp.tanh(SQRT_TWO_PI * (u + CUBIC * u * u * u))
    return 0.5 * (1.0 + inner) + 0.5 * u * (1.0 - inner * inner) * SQRT_TWO_PI * (
        1.0 + 3.0 * CUBIC * u * u
    )


def vmem_call(body, outs, scratch=(), scalars=0, vectors=0, kept=()):
    vmem = pl.BlockSpec(memory_space=pltpu.VMEM)
    smem = pl.BlockSpec(memory_space=pltpu.SMEM)
    call = pl.pallas_call(
        body,
        out_shape=[
            jax.ShapeDtypeStruct(*out) if i in kept else pltpu.VMEM(*out)
            for i, out in enumerate(outs)
        ],
        in_specs=[smem] * scalars + [vmem] * vectors,
        out_specs=[vmem] * len(outs),
        scratch_shapes=list(scratch),
        compiler_params=pltpu.CompilerParams(vmem_limit_bytes=16 << 20),
    )

    def run(*operands):
        operands = operands[:scalars] + tuple(
            pltpu.with_memory_space_constraint(x, pltpu.VMEM) for x in operands[scalars:]
        )
        return call(*operands)

    return run


def dot(a, b, contract):
    return lax.dot_general(a, b, ((contract[:1], contract[1:]), ((), ())), preferred_element_type=F32)


def stencil_body(place, field, partner, other, taps, gain, ext, scaled, inverse, normed):
    even = place[0] == 0
    rows, zonal, _ = field.shape
    half = STENCIL_SIDE // 2
    for r in range(rows + 2 * half):
        if r < half:
            row = jnp.where(even, other[r].astype(F32), partner[r].astype(F32))
        elif r < rows + half:
            row = field[r - half].astype(F32)
        else:
            k = r - rows - half
            row = jnp.where(even, partner[k].astype(F32), other[k].astype(F32))
        ext[r, EDGE : EDGE + zonal, :] = row
        ext[r, EDGE - half : EDGE, :] = row[zonal - half :]
        ext[r, EDGE + zonal : EDGE + zonal + half, :] = row[:half]
    for start in range(0, zonal, STRIP):
        total = jnp.zeros((rows, STRIP, field.shape[2]), F32)
        for b in range(STENCIL_SIDE):
            first = EDGE - half + b + start
            slab = ext[:, first : first + STRIP, :]
            for a in range(STENCIL_SIDE):
                k = a * STENCIL_SIDE + b
                total = total + taps[k : k + 1, :][None] * slab[a : a + rows]
        centred = total - jnp.mean(total, axis=-1, keepdims=True)
        recip = lax.rsqrt(jnp.mean(centred * centred, axis=-1, keepdims=True) + EPSILON)
        value = centred * recip
        rounded = (gain[...][None] * value).astype(BF16)
        wide = jnp.broadcast_to(recip, value.shape)
        for i in range(rows):
            at = pl.ds(i * zonal + start, STRIP)
            scaled[at, :] = value[i]
            inverse[at, :] = wide[i]
            normed[at, :] = rounded[i]


def selector(rows, columns, chunk_bits, offsets, turned):
    place = lax.broadcasted_iota(jnp.int32, (rows, columns), 1 if turned else 0)
    variable = lax.broadcasted_iota(jnp.int32, (rows, columns), 0 if turned else 1)
    chunk = lax.shift_right_logical(place, chunk_bits)
    inside = place & ((1 << chunk_bits) - 1)
    result = jnp.zeros((rows, columns), F32)
    for offset in offsets:
        j = inside - offset
        hit = (j >= 0) & (j < PER_CHUNK) & (chunk * PER_CHUNK + j == variable)
        result = jnp.where(hit, 1.0, result)
    return result.astype(BF16)


def mlp_body(normed, both, field, readout, gated, upper, residual, chunks):
    owned = both.shape[1] // 2
    hidden, channels = both.shape[0] * owned, both.shape[2]
    points = normed.shape[0]
    widen = both[:, :owned, :].reshape(hidden, channels)
    shrink = both[:, owned:, :].reshape(hidden, channels)
    upper[...] = dot(normed[...], widen, (1, 1))

    def step(i, carry):
        at = pl.ds(pl.multiple_of(i * 16, 16), 16)
        gated[at, :] = gelu_value(upper[at, :]).astype(BF16)
        return carry

    lax.fori_loop(0, points // 16, step, 0, unroll=2)
    mixed = dot(gated[...], shrink, (1, 0))
    residual[...] = (field[...].reshape(points, channels).astype(F32) + mixed).astype(BF16)
    members = chunks.shape[0]
    spread = dot(selector(members * CHUNK_ROWS, readout.shape[0], 3, (0,), False), readout[...], (1, 0))
    outlook = dot(spread.astype(BF16), residual[...], (1, 1))
    for e in range(members):
        chunks[e] = outlook[e * CHUNK_ROWS : (e + 1) * CHUNK_ROWS].astype(BF16)


def slope_body(upper, slope):
    def step(i, carry):
        at = pl.ds(pl.multiple_of(i * 16, 16), 16)
        slope[at, :] = gelu_slope(upper[at, :])
        return carry

    lax.fori_loop(0, upper.shape[0] // 16, step, 0, unroll=2)


def outlook_body(readout, residual, out):
    out[...] = dot(readout[...], residual[...], (1, 1)).astype(BF16)


def pair_body(place, everyone, truth, weight, payload, loss, rows, seen):
    member = place[1]
    members, _, points = everyone.shape
    variables, bands, lanes = truth.shape
    for j in range(PER_CHUNK):
        row = truth[jnp.minimum(member * PER_CHUNK + j, variables - 1)]
        for q in range(bands):
            seen[j : j + 1, q * lanes : (q + 1) * lanes] = row[q : q + 1]
    seen[PER_CHUNK:, :] = jnp.zeros((CHUNK_ROWS - PER_CHUNK, points), F32)
    limit = jnp.minimum(PER_CHUNK, variables - member * PER_CHUNK)
    real = lax.broadcasted_iota(jnp.int32, (CHUNK_ROWS, lanes), 0) < limit
    pair_norm = 1.0 / (members * (members - 1))
    lost = jnp.zeros((CHUNK_ROWS, lanes), F32)
    for q in range(points // lanes):
        at = slice(q * lanes, (q + 1) * lanes)
        y = [everyone[m, :, at].astype(F32) for m in range(members)]
        spread = [jnp.full((CHUNK_ROWS, lanes), SMOOTHING**0.5, F32) for _ in range(members)]
        ranks = [jnp.zeros((CHUNK_ROWS, lanes), F32) for _ in range(members)]
        for m in range(members):
            for k in range(m):
                gap = y[m] - y[k]
                square = gap * gap + SMOOTHING
                root = lax.rsqrt(square)
                size, tilt = square * root, gap * root
                spread[m], spread[k] = spread[m] + size, spread[k] + size
                ranks[m], ranks[k] = ranks[m] + tilt, ranks[k] - tilt
        scale = weight[0:1, at]
        for m in range(members):
            miss = y[m] - seen[:, at]
            square = miss * miss + SMOOTHING
            root = lax.rsqrt(square)
            term = scale * (square * root * (1.0 / members) - 0.5 * pair_norm * spread[m])
            lost = lost + jnp.where(real, term, 0.0)
            flow = scale * (miss * root * (1.0 / members) - pair_norm * ranks[m])
            average = spread[m] * (1.0 / (members - 1))
            high = average.astype(BF16).astype(F32)
            rows[m, 0:CHUNK_ROWS, at] = jnp.where(real, flow, 0.0)
            rows[m, PER_CHUNK : PER_CHUNK + CHUNK_ROWS, at] = high
            rows[m, 2 * PER_CHUNK : 16, at] = (average - high)[: 16 - 2 * PER_CHUNK]
    for m in range(members):
        payload[m] = rows[m].astype(BF16)
    loss[...] = jnp.sum(lost, axis=0, keepdims=True)


def average_body(back, out):
    members, height, points = back.shape
    pick = selector(out.shape[0], members * height, 4, (PER_CHUNK, 2 * PER_CHUNK), True)
    out[...] = dot(pick, back[...].reshape(members * height, points), (1, 0))


def backward_body(
    back, readout, residual, gated, slope, normed, scaled, inverse, gain, both,
    widen_grad, shrink_grad, readout_grad, gain_grad, back_depth, gate, back_upper,
):
    members, height, points = back.shape
    owned = both.shape[1] // 2
    hidden, channels = both.shape[0] * owned, both.shape[2]
    widen = both[:, :owned, :].reshape(hidden, channels)
    shrink = both[:, owned:, :].reshape(hidden, channels)
    flow = back[...].reshape(members * height, points)
    spread = dot(selector(members * height, readout.shape[0], 4, (0,), False), readout[...], (1, 0))
    back_residual = dot(flow, spread.astype(BF16), (0, 0)).astype(BF16)
    gate[...] = dot(back_residual, shrink, (1, 1))
    readout_grad[...] = dot(flow, residual[...], (1, 0))
    shrink_grad[...] = dot(gated[...], back_residual, (0, 0))

    def step(i, carry):
        at = pl.ds(pl.multiple_of(i * 16, 16), 16)
        back_upper[at, :] = (gate[at, :] * slope[at, :]).astype(BF16)
        return carry

    lax.fori_loop(0, points // 16, step, 0, unroll=2)
    back_norm = dot(back_upper[...], widen, (1, 0))
    widen_grad[...] = dot(back_upper[...], normed[...], (0, 0))
    value = scaled[...]
    product = back_norm * value
    gain_grad[...] = jnp.sum(product, axis=0, keepdims=True)
    g = back_norm * gain[...]
    p = jnp.mean(g, axis=-1, keepdims=True)
    q = jnp.mean(g * value, axis=-1, keepdims=True)
    back_depth[...] = inverse[...] * (g - p - value * q)


def pack_body(place, back_depth, ext, widen_grad, shrink_grad, readout_grad, gain_grad, loss, send, keep, small):
    first_core = place[0] == 0
    half = STENCIL_SIDE // 2
    zonal = ext.shape[1] - 2 * EDGE
    rows = back_depth.shape[0] // zonal
    channels = ext.shape[2]
    members = small.shape[0] // CHUNK_ROWS
    height = readout_grad.shape[0] // members
    small[TAPS_AT + 48 :, :] = jnp.zeros((small.shape[0] - TAPS_AT - 48, channels), F32)
    for e in range(members):
        count = min(PER_CHUNK, TAPS_AT - e * PER_CHUNK)
        if count > 0:
            small[e * PER_CHUNK : e * PER_CHUNK + count, :] = readout_grad[e * height : e * height + count, :]
    for b in range(STENCIL_SIDE):
        totals = [jnp.zeros((STRIP, channels), F32) for _ in range(STENCIL_SIDE)]
        for start in range(0, zonal, STRIP):
            first = EDGE - half + b + start
            slab = ext[:, first : first + STRIP, :]
            up = [back_depth[i * zonal + start : i * zonal + start + STRIP, :] for i in range(rows)]
            for a in range(STENCIL_SIDE):
                for i in range(rows):
                    totals[a] = totals[a] + up[i] * slab[i + a]
        for a in range(STENCIL_SIDE):
            k = TAPS_AT + a * STENCIL_SIDE + b
            small[k : k + 1, :] = jnp.sum(totals[a], axis=0, keepdims=True)
    small[TAPS_AT + 49 : TAPS_AT + 50, :] = gain_grad[...]
    small[TAPS_AT + 50 : TAPS_AT + 51, :] = loss[...]
    depth_z = DEPTH_Z
    for e in range(members):
        tail = small[e * CHUNK_ROWS : (e + 1) * CHUNK_ROWS, :]
        for h in range(2):
            d = 2 * e + h
            for mat, grad in enumerate((widen_grad, shrink_grad)):
                base = h * depth_z * 2 * members + e
                even = grad[pl.ds(base, depth_z, stride=2 * members), :]
                odd = grad[pl.ds(base + members, depth_z, stride=2 * members), :]
                keep[d, mat * depth_z : (mat + 1) * depth_z, :] = jnp.where(first_core, even, odd)
                send[d, mat * depth_z : (mat + 1) * depth_z, :] = jnp.where(first_core, odd, even)
            keep[d, 2 * depth_z :, :] = tail
            send[d, 2 * depth_z :, :] = tail


def gradient_body(
    place, back, readout, residual, gated, slope, normed, scaled, inverse, gain, both, ext, loss,
    send, keep, gate, back_upper, widen_grad, shrink_grad, readout_grad, gain_grad, back_depth, small,
):
    backward_body(
        back, readout, residual, gated, slope, normed, scaled, inverse, gain, both,
        widen_grad, shrink_grad, readout_grad, gain_grad, back_depth, gate, back_upper,
    )
    pack_body(
        place, back_depth, ext, widen_grad, shrink_grad, readout_grad, gain_grad, loss,
        send, keep, small,
    )


def final_body(arrived, up, down, taps, gain, readout, loss, small):
    members = arrived.shape[0]
    for e in range(members):
        small[e * CHUNK_ROWS : (e + 1) * CHUNK_ROWS, :] = arrived[e, 0:CHUNK_ROWS, :]
        up[e : e + 1, :] = arrived[e, CHUNK_ROWS : CHUNK_ROWS + 1, :]
        down[e : e + 1, :] = arrived[e, CHUNK_ROWS + 1 : CHUNK_ROWS + 2, :]
    readout[...] = small[0:TAPS_AT, :]
    taps[...] = small[TAPS_AT : TAPS_AT + 49, :]
    gain[...] = small[TAPS_AT + 49 : TAPS_AT + 50, :]
    loss[...] = jnp.sum(small[TAPS_AT + 50 : TAPS_AT + 51, :], axis=1, keepdims=True)


def on_device(
    features,
    random_perturbation,
    observed_truth,
    stencil_taps,
    affine_factor,
    widen_matrix,
    shrink_matrix,
    readout_matrix,
):
    rows, zonal, channels = features.shape
    variables = readout_matrix.shape[0]
    half = STENCIL_SIDE // 2
    bands, members = lax.axis_size("lat"), lax.axis_size("ens")
    band, member = lax.axis_index("lat"), lax.axis_index("ens")
    points = rows * zonal
    latitudes = rows * bands
    hidden = widen_matrix.shape[0] * bands
    depth_z = DEPTH_Z
    share = CHUNK_ROWS
    place = jnp.stack([lax.rem(band, 2), member]).astype(jnp.int32)
    gain = affine_factor.reshape(1, channels)

    field = (features.astype(F32) + random_perturbation[0].astype(F32)).astype(BF16)
    partner, other = halo_rows(field, half)
    shape = (bands,) + widen_matrix.shape
    pair = jnp.concatenate(
        [jnp.broadcast_to(widen_matrix[None], shape), jnp.broadcast_to(shrink_matrix[None], shape)],
        axis=1,
    )
    both = exchange(pair, AXES, weight_groups(members, bands))
    latitude = (band * rows + jnp.arange(points, dtype=jnp.int32) // zonal).astype(F32)
    area = jnp.cos(math.pi * ((latitude + 0.5) / latitudes - 0.5))
    weight = (area * (1.0 / (latitudes * zonal)))[None, :]

    wide = (rows + 2 * half, zonal + 2 * EDGE, channels)
    ext, scaled, inverse, normed = vmem_call(
        stencil_body,
        [(wide, F32), ((points, channels), F32), ((points, channels), F32), ((points, channels), BF16)],
        scalars=1,
        vectors=5,
    )(place, field, partner, other, stencil_taps, gain)
    gated, upper, residual, chunks = vmem_call(
        mlp_body,
        [
            ((points, hidden), BF16),
            ((points, hidden), F32),
            ((points, channels), BF16),
            ((members, CHUNK_ROWS, points), BF16),
        ],
        vectors=4,
    )(normed, both, field, readout_matrix)
    everyone = exchange(chunks, "ens")
    (slope,) = vmem_call(slope_body, [((points, hidden), F32)], vectors=1)(upper)
    (outlook,) = vmem_call(outlook_body, [((variables, points), BF16)], vectors=2)(
        readout_matrix, residual
    )
    sample_outlook = outlook.reshape(1, variables, rows, zonal)
    payload, loss = vmem_call(
        pair_body,
        [((members, 16, points), BF16), ((1, zonal), F32)],
        [pltpu.VMEM((members, 16, points), F32), pltpu.VMEM((CHUNK_ROWS, points), F32)],
        scalars=1,
        vectors=3,
    )(place, everyone, observed_truth, weight)
    back = exchange(payload, "ens")
    (average,) = vmem_call(average_body, [((variables, points), F32)], vectors=1)(back)
    sample_average_spread = average.reshape(1, variables, rows, zonal)

    packet = ((2 * members, 2 * depth_z + share, channels), F32)
    send, keep = vmem_call(
        gradient_body,
        [packet, packet],
        [
            pltpu.VMEM((points, hidden), F32),
            pltpu.VMEM((points, hidden), BF16),
            pltpu.VMEM((hidden, channels), F32),
            pltpu.VMEM((hidden, channels), F32),
            pltpu.VMEM((members * 16, channels), F32),
            pltpu.VMEM((1, channels), F32),
            pltpu.VMEM((points, channels), F32),
            pltpu.VMEM((members * share, channels), F32),
        ],
        scalars=1,
        vectors=12,
    )(
        place, back, readout_matrix, residual, gated, slope, normed, scaled, inverse, gain, both,
        ext, loss,
    )

    arrived = exchange(keep + core_swap(send), AXES, plane_groups(members, bands))
    columns = [
        list(range(h * bands // 2 + c, (h + 1) * bands // 2, 2)) for h in range(2) for c in range(2)
    ]
    part = jnp.sum(arrived, axis=0)
    outgoing = jnp.concatenate(
        [
            jnp.broadcast_to(part[None, 2 * depth_z :], (depth_z, share, channels)),
            part[: 2 * depth_z].reshape(2, depth_z, channels).transpose(1, 0, 2),
        ],
        axis=1,
    )
    done = jnp.sum(exchange(outgoing, "lat", columns), axis=0)
    arrived = exchange(jnp.broadcast_to(done[None], (members,) + done.shape), "ens")
    up, down, taps, gain_total, readout, loss = vmem_call(
        final_body,
        [
            ((members, channels), F32),
            ((members, channels), F32),
            ((STENCIL_SIDE * STENCIL_SIDE, channels), F32),
            ((1, channels), F32),
            ((variables, channels), F32),
            ((1, 1), F32),
        ],
        [pltpu.VMEM((members * share, channels), F32)],
        vectors=1,
    )(arrived)
    return (
        loss.reshape(()),
        taps,
        gain_total.reshape(channels),
        up,
        down,
        readout,
        sample_outlook,
        sample_average_spread,
    )


def solution(mesh):
    in_specs = (
        P("lat", None, None),
        P("ens", "lat", None, None),
        P(None, "lat", None),
        P(),
        P(),
        P("lat", None),
        P("lat", None),
        P(),
    )
    out_specs = (
        P(),
        P(),
        P(),
        P("lat", None),
        P("lat", None),
        P(),
        P("ens", None, "lat", None),
        P("ens", None, "lat", None),
    )

    return jax.shard_map(
        on_device, mesh=mesh, in_specs=in_specs, out_specs=out_specs, check_vma=False
    )
```

```python
import math

import jax
import jax.numpy as jnp
from jax import lax
from jax.experimental import pallas as pl
from jax.experimental.pallas import tpu as pltpu
from jax.sharding import PartitionSpec as P

STENCIL_SIDE = 7
SQRT_TWO_PI = 0.7978845608028654
CUBIC = 0.044715
EPSILON = 1e-06
SMOOTHING = 0.01
PER_CHUNK = 5
CHUNK_ROWS = 8
EDGE = 8
STRIP = 16
TAPS_AT = 69
DEPTH_Z = 8
F32, BF16 = jnp.float32, jnp.bfloat16


def core_swap(value):
    count = lax.axis_size("lat")
    return lax.ppermute(value, "lat", [(i, i ^ 1) for i in range(count)])


def odd_swap(value):
    count = lax.axis_size("lat")
    pairs = [(i, i + 1) for i in range(1, count - 1, 2)]
    return lax.ppermute(value, "lat", pairs + [(b, a) for a, b in pairs])


def halo_rows(field, half):
    even = lax.rem(lax.axis_index("lat"), 2) == 0
    head, tail = field[:half], field[field.shape[0] - half :]
    return core_swap(jnp.where(even, tail, head)), odd_swap(jnp.where(even, head, tail))


def exchange(value, axis, groups=None):
    return lax.all_to_all(value, axis, 0, 0, tiled=True, axis_index_groups=groups)


AXES = ("ens", "lat")


def weight_groups(members, bands):
    half = bands // 2
    groups = []
    for e in range(members):
        far = e // 4 * 4 + (e + 2) % 4
        for c in range(2):
            groups.append(
                [e * bands + b for b in range(c, half, 2)]
                + [far * bands + b for b in range(half + c, bands, 2)]
            )
    return groups


def plane_groups(members, bands):
    half = bands // 2
    return [
        [e * bands + h * half + rest for e in range(members) for h in range(2)]
        for rest in range(half)
    ]


def gelu_value(u):
    inner = jnp.tanh(SQRT_TWO_PI * (u + CUBIC * u * u * u))
    return 0.5 * u * (1.0 + inner)


def gelu_slope(u):
    inner = jnp.tanh(SQRT_TWO_PI * (u + CUBIC * u * u * u))
    return 0.5 * (1.0 + inner) + 0.5 * u * (1.0 - inner * inner) * SQRT_TWO_PI * (
        1.0 + 3.0 * CUBIC * u * u
    )


def vmem_call(body, outs, scratch=(), scalars=0, vectors=0, kept=(), aliases=None):
    vmem = pl.BlockSpec(memory_space=pltpu.VMEM)
    smem = pl.BlockSpec(memory_space=pltpu.SMEM)
    call = pl.pallas_call(
        body,
        out_shape=[
            jax.ShapeDtypeStruct(*out) if i in kept else pltpu.VMEM(*out)
            for i, out in enumerate(outs)
        ],
        in_specs=[smem] * scalars + [vmem] * vectors,
        out_specs=[vmem] * len(outs),
        scratch_shapes=list(scratch),
        input_output_aliases=aliases or {},
        compiler_params=pltpu.CompilerParams(vmem_limit_bytes=16 << 20),
    )

    def run(*operands):
        operands = operands[:scalars] + tuple(
            pltpu.with_memory_space_constraint(x, pltpu.VMEM) for x in operands[scalars:]
        )
        return call(*operands)

    return run


def dot(a, b, contract):
    return lax.dot_general(a, b, ((contract[:1], contract[1:]), ((), ())), preferred_element_type=F32)


def stencil_body(place, field, partner, other, taps, gain, ext, scaled, inverse, normed):
    even = place[0] == 0
    rows, zonal, _ = field.shape
    half = STENCIL_SIDE // 2
    for r in range(rows + 2 * half):
        if r < half:
            row = jnp.where(even, other[r].astype(F32), partner[r].astype(F32))
        elif r < rows + half:
            row = field[r - half].astype(F32)
        else:
            k = r - rows - half
            row = jnp.where(even, partner[k].astype(F32), other[k].astype(F32))
        ext[r, EDGE : EDGE + zonal, :] = row
        ext[r, EDGE - half : EDGE, :] = row[zonal - half :]
        ext[r, EDGE + zonal : EDGE + zonal + half, :] = row[:half]
    for start in range(0, zonal, STRIP):
        total = jnp.zeros((rows, STRIP, field.shape[2]), F32)
        for b in range(STENCIL_SIDE):
            first = EDGE - half + b + start
            slab = ext[:, first : first + STRIP, :]
            for a in range(STENCIL_SIDE):
                k = a * STENCIL_SIDE + b
                total = total + taps[k : k + 1, :][None] * slab[a : a + rows]
        centred = total - jnp.mean(total, axis=-1, keepdims=True)
        recip = lax.rsqrt(jnp.mean(centred * centred, axis=-1, keepdims=True) + EPSILON)
        value = centred * recip
        rounded = (gain[...][None] * value).astype(BF16)
        wide = jnp.broadcast_to(recip, value.shape)
        for i in range(rows):
            at = pl.ds(i * zonal + start, STRIP)
            scaled[at, :] = value[i]
            inverse[at, :] = wide[i]
            normed[at, :] = rounded[i]


def selector(rows, columns, chunk_bits, offsets, turned):
    place = lax.broadcasted_iota(jnp.int32, (rows, columns), 1 if turned else 0)
    variable = lax.broadcasted_iota(jnp.int32, (rows, columns), 0 if turned else 1)
    chunk = lax.shift_right_logical(place, chunk_bits)
    inside = place & ((1 << chunk_bits) - 1)
    result = jnp.zeros((rows, columns), F32)
    for offset in offsets:
        j = inside - offset
        hit = (j >= 0) & (j < PER_CHUNK) & (chunk * PER_CHUNK + j == variable)
        result = jnp.where(hit, 1.0, result)
    return result.astype(BF16)


def matrices(shards):
    count, owned, channels = shards.shape[0], shards.shape[1] // 2, shards.shape[2]
    return (
        shards[:, :owned, :].reshape(count * owned, channels),
        shards[:, owned:, :].reshape(count * owned, channels),
    )


def mlp_body(normed, mine, theirs, field, readout, gated, upper, residual, chunks):
    points, channels = normed.shape
    halves = [matrices(mine), matrices(theirs)]
    wide = upper.shape[1] // 2
    for k, (widen, _) in enumerate(halves):
        upper[:, k * wide : (k + 1) * wide] = dot(normed[...], widen, (1, 1))

    def step(i, carry):
        at = pl.ds(pl.multiple_of(i * 16, 16), 16)
        gated[at, :] = gelu_value(upper[at, :]).astype(BF16)
        return carry

    lax.fori_loop(0, points // 16, step, 0, unroll=2)
    mixed = sum(
        dot(gated[:, k * wide : (k + 1) * wide], shrink, (1, 0))
        for k, (_, shrink) in enumerate(halves)
    )
    residual[...] = (field[...].reshape(points, channels).astype(F32) + mixed).astype(BF16)
    members = chunks.shape[0]
    spread = dot(selector(members * CHUNK_ROWS, readout.shape[0], 3, (0,), False), readout[...], (1, 0))
    outlook = dot(spread.astype(BF16), residual[...], (1, 1))
    for e in range(members):
        chunks[e] = outlook[e * CHUNK_ROWS : (e + 1) * CHUNK_ROWS].astype(BF16)


def slope_body(upper, slope):
    def step(i, carry):
        at = pl.ds(pl.multiple_of(i * 16, 16), 16)
        slope[at, :] = gelu_slope(upper[at, :])
        return carry

    lax.fori_loop(0, upper.shape[0] // 16, step, 0, unroll=2)


def outlook_body(readout, residual, out):
    out[...] = dot(readout[...], residual[...], (1, 1)).astype(BF16)


def pair_body(place, everyone, truth, weight, payload, loss, rows, seen):
    member = place[1]
    members, _, points = everyone.shape
    variables, bands, lanes = truth.shape
    for j in range(PER_CHUNK):
        row = truth[jnp.minimum(member * PER_CHUNK + j, variables - 1)]
        for q in range(bands):
            seen[j : j + 1, q * lanes : (q + 1) * lanes] = row[q : q + 1]
    seen[PER_CHUNK:, :] = jnp.zeros((CHUNK_ROWS - PER_CHUNK, points), F32)
    limit = jnp.minimum(PER_CHUNK, variables - member * PER_CHUNK)
    real = lax.broadcasted_iota(jnp.int32, (CHUNK_ROWS, lanes), 0) < limit
    pair_norm = 1.0 / (members * (members - 1))
    lost = jnp.zeros((CHUNK_ROWS, lanes), F32)
    for q in range(points // lanes):
        at = slice(q * lanes, (q + 1) * lanes)
        y = [everyone[m, :, at].astype(F32) for m in range(members)]
        spread = [jnp.full((CHUNK_ROWS, lanes), SMOOTHING**0.5, F32) for _ in range(members)]
        ranks = [jnp.zeros((CHUNK_ROWS, lanes), F32) for _ in range(members)]
        for m in range(members):
            for k in range(m):
                gap = y[m] - y[k]
                square = gap * gap + SMOOTHING
                root = lax.rsqrt(square)
                size, tilt = square * root, gap * root
                spread[m], spread[k] = spread[m] + size, spread[k] + size
                ranks[m], ranks[k] = ranks[m] + tilt, ranks[k] - tilt
        scale = weight[0:1, at]
        for m in range(members):
            miss = y[m] - seen[:, at]
            square = miss * miss + SMOOTHING
            root = lax.rsqrt(square)
            term = scale * (square * root * (1.0 / members) - 0.5 * pair_norm * spread[m])
            lost = lost + jnp.where(real, term, 0.0)
            flow = scale * (miss * root * (1.0 / members) - pair_norm * ranks[m])
            average = spread[m] * (1.0 / (members - 1))
            high = average.astype(BF16).astype(F32)
            rows[m, 0:CHUNK_ROWS, at] = jnp.where(real, flow, 0.0)
            rows[m, PER_CHUNK : PER_CHUNK + CHUNK_ROWS, at] = high
            rows[m, 2 * PER_CHUNK : 16, at] = (average - high)[: 16 - 2 * PER_CHUNK]
    for m in range(members):
        payload[m] = rows[m].astype(BF16)
    loss[...] = jnp.sum(lost, axis=0, keepdims=True)


def average_body(back, out):
    members, height, points = back.shape
    pick = selector(out.shape[0], members * height, 4, (PER_CHUNK, 2 * PER_CHUNK), True)
    out[...] = dot(pick, back[...].reshape(members * height, points), (1, 0))


def backward_body(
    back, readout, residual, gated, slope, normed, scaled, inverse, gain, mine, theirs,
    widen_grad, shrink_grad, readout_grad, gain_grad, back_depth, gate, back_upper,
):
    members, height, points = back.shape
    halves = [matrices(mine), matrices(theirs)]
    wide = slope.shape[1] // 2
    flow = back[...].reshape(members * height, points)
    spread = dot(selector(members * height, readout.shape[0], 4, (0,), False), readout[...], (1, 0))
    back_residual = dot(flow, spread.astype(BF16), (0, 0)).astype(BF16)
    for k, (_, shrink) in enumerate(halves):
        gate[:, k * wide : (k + 1) * wide] = dot(back_residual, shrink, (1, 1))
    readout_grad[...] = dot(flow, residual[...], (1, 0))
    shrink_grad[...] = dot(gated[...], back_residual, (0, 0))

    def step(i, carry):
        at = pl.ds(pl.multiple_of(i * 16, 16), 16)
        back_upper[at, :] = (gate[at, :] * slope[at, :]).astype(BF16)
        return carry

    lax.fori_loop(0, points // 16, step, 0, unroll=2)
    back_norm = sum(
        dot(back_upper[:, k * wide : (k + 1) * wide], widen, (1, 0))
        for k, (widen, _) in enumerate(halves)
    )
    widen_grad[...] = dot(back_upper[...], normed[...], (0, 0))
    value = scaled[...]
    product = back_norm * value
    gain_grad[...] = jnp.sum(product, axis=0, keepdims=True)
    g = back_norm * gain[...]
    p = jnp.mean(g, axis=-1, keepdims=True)
    q = jnp.mean(g * value, axis=-1, keepdims=True)
    back_depth[...] = inverse[...] * (g - p - value * q)


def pack_body(back_depth, ext, widen_grad, shrink_grad, readout_grad, gain_grad, loss, send, keep, small):
    half = STENCIL_SIDE // 2
    zonal = ext.shape[1] - 2 * EDGE
    rows = back_depth.shape[0] // zonal
    channels = ext.shape[2]
    members = small.shape[0] // CHUNK_ROWS
    height = readout_grad.shape[0] // members
    small[TAPS_AT + 48 :, :] = jnp.zeros((small.shape[0] - TAPS_AT - 48, channels), F32)
    for e in range(members):
        count = min(PER_CHUNK, TAPS_AT - e * PER_CHUNK)
        if count > 0:
            small[e * PER_CHUNK : e * PER_CHUNK + count, :] = readout_grad[e * height : e * height + count, :]
    for b in range(STENCIL_SIDE):
        totals = [jnp.zeros((STRIP, channels), F32) for _ in range(STENCIL_SIDE)]
        for start in range(0, zonal, STRIP):
            first = EDGE - half + b + start
            slab = ext[:, first : first + STRIP, :]
            up = [back_depth[i * zonal + start : i * zonal + start + STRIP, :] for i in range(rows)]
            for a in range(STENCIL_SIDE):
                for i in range(rows):
                    totals[a] = totals[a] + up[i] * slab[i + a]
        for a in range(STENCIL_SIDE):
            k = TAPS_AT + a * STENCIL_SIDE + b
            small[k : k + 1, :] = jnp.sum(totals[a], axis=0, keepdims=True)
    small[TAPS_AT + 49 : TAPS_AT + 50, :] = gain_grad[...]
    small[TAPS_AT + 50 : TAPS_AT + 51, :] = loss[...]
    depth_z = DEPTH_Z
    for e in range(members):
        tail = small[e * CHUNK_ROWS : (e + 1) * CHUNK_ROWS, :]
        for h in range(2):
            d = 2 * e + h
            for mat, grad in enumerate((widen_grad, shrink_grad)):
                at = slice(mat * depth_z, (mat + 1) * depth_z)
                base = h * depth_z * members + e
                keep[d, at, :] = grad[pl.ds(base, depth_z, stride=members), :]
                base = base + 2 * depth_z * members
                send[d, at, :] = grad[pl.ds(base, depth_z, stride=members), :]
            keep[d, 2 * depth_z :, :] = tail
            send[d, 2 * depth_z :, :] = tail


def gradient_body(
    back, readout, residual, gated, slope, normed, scaled, inverse, gain, mine, theirs, ext, loss,
    send, keep, gate, back_upper, widen_grad, shrink_grad, readout_grad, gain_grad, back_depth, small,
):
    backward_body(
        back, readout, residual, gated, slope, normed, scaled, inverse, gain, mine, theirs,
        widen_grad, shrink_grad, readout_grad, gain_grad, back_depth, gate, back_upper,
    )
    pack_body(
        back_depth, ext, widen_grad, shrink_grad, readout_grad, gain_grad, loss,
        send, keep, small,
    )


def final_body(arrived, up, down, taps, gain, readout, loss, small):
    members = arrived.shape[0]
    for e in range(members):
        small[e * CHUNK_ROWS : (e + 1) * CHUNK_ROWS, :] = arrived[e, 0:CHUNK_ROWS, :]
        up[e : e + 1, :] = arrived[e, CHUNK_ROWS : CHUNK_ROWS + 1, :]
        down[e : e + 1, :] = arrived[e, CHUNK_ROWS + 1 : CHUNK_ROWS + 2, :]
    readout[...] = small[0:TAPS_AT, :]
    taps[...] = small[TAPS_AT : TAPS_AT + 49, :]
    gain[...] = small[TAPS_AT + 49 : TAPS_AT + 50, :]
    loss[...] = jnp.sum(small[TAPS_AT + 50 : TAPS_AT + 51, :], axis=1, keepdims=True)


def on_device(
    features,
    random_perturbation,
    observed_truth,
    stencil_taps,
    affine_factor,
    widen_matrix,
    shrink_matrix,
    readout_matrix,
):
    rows, zonal, channels = features.shape
    variables = readout_matrix.shape[0]
    half = STENCIL_SIDE // 2
    bands, members = lax.axis_size("lat"), lax.axis_size("ens")
    band, member = lax.axis_index("lat"), lax.axis_index("ens")
    points = rows * zonal
    latitudes = rows * bands
    hidden = widen_matrix.shape[0] * bands
    depth_z = DEPTH_Z
    share = CHUNK_ROWS
    place = jnp.stack([lax.rem(band, 2), member]).astype(jnp.int32)
    gain = affine_factor.reshape(1, channels)

    field = (features.astype(F32) + random_perturbation[0].astype(F32)).astype(BF16)
    partner, other = halo_rows(field, half)
    shape = (bands // 2,) + widen_matrix.shape
    pair = jnp.concatenate(
        [jnp.broadcast_to(widen_matrix[None], shape), jnp.broadcast_to(shrink_matrix[None], shape)],
        axis=1,
    )
    mine = exchange(pair, AXES, weight_groups(members, bands))
    mine, partner, other = lax.optimization_barrier((mine, partner, other))
    theirs = core_swap(mine)
    latitude = (band * rows + jnp.arange(points, dtype=jnp.int32) // zonal).astype(F32)
    area = jnp.cos(math.pi * ((latitude + 0.5) / latitudes - 0.5))
    weight = (area * (1.0 / (latitudes * zonal)))[None, :]

    wide = (rows + 2 * half, zonal + 2 * EDGE, channels)
    ext, scaled, inverse, normed = vmem_call(
        stencil_body,
        [
            (wide, F32),
            ((points, channels), F32),
            ((points, channels), F32),
            ((points, channels), BF16),
        ],
        scalars=1,
        vectors=5,
    )(place, field, partner, other, stencil_taps, gain)
    gated, upper, residual, chunks = vmem_call(
        mlp_body,
        [
            ((points, hidden), BF16),
            ((points, hidden), F32),
            ((points, channels), BF16),
            ((members, CHUNK_ROWS, points), BF16),
        ],
        vectors=5,
    )(normed, mine, theirs, field, readout_matrix)
    everyone = exchange(chunks, "ens")
    (slope,) = vmem_call(slope_body, [((points, hidden), F32)], vectors=1, aliases={0: 0})(upper)
    (outlook,) = vmem_call(outlook_body, [((variables, points), BF16)], vectors=2)(
        readout_matrix, residual
    )
    sample_outlook = outlook.reshape(1, variables, rows, zonal)
    payload, loss = vmem_call(
        pair_body,
        [((members, 16, points), BF16), ((1, zonal), F32)],
        [pltpu.VMEM((members, 16, points), F32), pltpu.VMEM((CHUNK_ROWS, points), F32)],
        scalars=1,
        vectors=3,
    )(place, everyone, observed_truth, weight)
    back = exchange(payload, "ens")
    (average,) = vmem_call(average_body, [((variables, points), F32)], vectors=1)(back)
    sample_average_spread = average.reshape(1, variables, rows, zonal)

    packet = ((2 * members, 2 * depth_z + share, channels), F32)
    send, keep = vmem_call(
        gradient_body,
        [packet, packet],
        [
            pltpu.VMEM((points, hidden), F32),
            pltpu.VMEM((points, hidden), BF16),
            pltpu.VMEM((hidden, channels), F32),
            pltpu.VMEM((hidden, channels), F32),
            pltpu.VMEM((members * 16, channels), F32),
            pltpu.VMEM((1, channels), F32),
            pltpu.VMEM((points, channels), F32),
            pltpu.VMEM((members * share, channels), F32),
        ],
        vectors=13,
    )(
        back, readout_matrix, residual, gated, slope, normed, scaled, inverse, gain, mine, theirs,
        ext, loss,
    )

    total = (keep + core_swap(send)).astype(BF16)
    arrived = exchange(total, AXES, plane_groups(members, bands)).astype(F32)
    columns = [
        list(range(h * bands // 2 + c, (h + 1) * bands // 2, 2)) for h in range(2) for c in range(2)
    ]
    part = jnp.sum(arrived, axis=0)
    outgoing = jnp.concatenate(
        [
            jnp.broadcast_to(part[None, 2 * depth_z :], (depth_z, share, channels)),
            part[: 2 * depth_z].reshape(2, depth_z, channels).transpose(1, 0, 2),
        ],
        axis=1,
    )
    done = jnp.sum(exchange(outgoing, "lat", columns), axis=0)
    arrived = exchange(jnp.broadcast_to(done[None], (members,) + done.shape), "ens")
    up, down, taps, gain_total, readout, loss = vmem_call(
        final_body,
        [
            ((members, channels), F32),
            ((members, channels), F32),
            ((STENCIL_SIDE * STENCIL_SIDE, channels), F32),
            ((1, channels), F32),
            ((variables, channels), F32),
            ((1, 1), F32),
        ],
        [pltpu.VMEM((members * share, channels), F32)],
        vectors=1,
        kept=range(6),
    )(arrived)
    return (
        loss.reshape(()),
        taps,
        gain_total.reshape(channels),
        up,
        down,
        readout,
        sample_outlook,
        sample_average_spread,
    )


def solution(mesh):
    in_specs = (
        P("lat", None, None),
        P("ens", "lat", None, None),
        P(None, "lat", None),
        P(),
        P(),
        P("lat", None),
        P("lat", None),
        P(),
    )
    out_specs = (
        P(),
        P(),
        P(),
        P("lat", None),
        P("lat", None),
        P(),
        P("ens", None, "lat", None),
        P("ens", None, "lat", None),
    )

    return jax.shard_map(
        on_device, mesh=mesh, in_specs=in_specs, out_specs=out_specs, check_vma=False
    )
```

```python
import math

import jax
import jax.numpy as jnp
from jax import lax
from jax.experimental import pallas as pl
from jax.experimental.pallas import tpu as pltpu
from jax.sharding import PartitionSpec as P

STENCIL_SIDE = 7
SQRT_TWO_PI = 0.7978845608028654
CUBIC = 0.044715
EPSILON = 1e-06
SMOOTHING = 0.01
PER_CHUNK = 5
CHUNK_ROWS = 8
EDGE = 8
STRIP = 16
TAPS_AT = 69
DEPTH_Z = 8
F32, BF16 = jnp.float32, jnp.bfloat16


def core_swap(value):
    count = lax.axis_size("lat")
    return lax.ppermute(value, "lat", [(i, i ^ 1) for i in range(count)])


def odd_swap(value):
    count = lax.axis_size("lat")
    pairs = [(i, i + 1) for i in range(1, count - 1, 2)]
    return lax.ppermute(value, "lat", pairs + [(b, a) for a, b in pairs])


def halo_rows(field, half):
    even = lax.rem(lax.axis_index("lat"), 2) == 0
    head, tail = field[:half], field[field.shape[0] - half :]
    return core_swap(jnp.where(even, tail, head)), odd_swap(jnp.where(even, head, tail))


def exchange(value, axis, groups=None):
    return lax.all_to_all(value, axis, 0, 0, tiled=True, axis_index_groups=groups)


AXES = ("ens", "lat")


def weight_groups(members, bands):
    half = bands // 2
    groups = []
    for e in range(members):
        far = e // 4 * 4 + (e + 2) % 4
        for c in range(2):
            groups.append(
                [e * bands + b for b in range(c, half, 2)]
                + [far * bands + b for b in range(half + c, bands, 2)]
            )
    return groups


def plane_groups(members, bands):
    half = bands // 2
    return [
        [e * bands + h * half + rest for e in range(members) for h in range(2)]
        for rest in range(half)
    ]


def gelu_value(u):
    inner = jnp.tanh(SQRT_TWO_PI * (u + CUBIC * u * u * u))
    return 0.5 * u * (1.0 + inner)


def gelu_slope(u):
    inner = jnp.tanh(SQRT_TWO_PI * (u + CUBIC * u * u * u))
    return 0.5 * (1.0 + inner) + 0.5 * u * (1.0 - inner * inner) * SQRT_TWO_PI * (
        1.0 + 3.0 * CUBIC * u * u
    )


def vmem_call(body, outs, scratch=(), scalars=0, vectors=0, kept=(), aliases=None):
    vmem = pl.BlockSpec(memory_space=pltpu.VMEM)
    smem = pl.BlockSpec(memory_space=pltpu.SMEM)
    call = pl.pallas_call(
        body,
        out_shape=[
            jax.ShapeDtypeStruct(*out) if i in kept else pltpu.VMEM(*out)
            for i, out in enumerate(outs)
        ],
        in_specs=[smem] * scalars + [vmem] * vectors,
        out_specs=[vmem] * len(outs),
        scratch_shapes=list(scratch),
        input_output_aliases=aliases or {},
        compiler_params=pltpu.CompilerParams(vmem_limit_bytes=16 << 20),
    )

    def run(*operands):
        operands = operands[:scalars] + tuple(
            pltpu.with_memory_space_constraint(x, pltpu.VMEM) for x in operands[scalars:]
        )
        return call(*operands)

    return run


def dot(a, b, contract):
    return lax.dot_general(a, b, ((contract[:1], contract[1:]), ((), ())), preferred_element_type=F32)


def fill_rows(place, field, partner, other, ext):
    even = place[0] == 0
    rows, zonal, _ = field.shape
    half = STENCIL_SIDE // 2
    for r in range(rows + 2 * half):
        if r < half:
            row = jnp.where(even, other[r].astype(F32), partner[r].astype(F32))
        elif r < rows + half:
            row = field[r - half].astype(F32)
        else:
            k = r - rows - half
            row = jnp.where(even, partner[k].astype(F32), other[k].astype(F32))
        ext[r, EDGE : EDGE + zonal, :] = row
        ext[r, EDGE - half : EDGE, :] = row[zonal - half :]
        ext[r, EDGE + zonal : EDGE + zonal + half, :] = row[:half]


def stencil_body(place, field, partner, other, taps, gain, scaled, inverse, normed, ext):
    rows, zonal, _ = field.shape
    half = STENCIL_SIDE // 2
    fill_rows(place, field, partner, other, ext)
    for start in range(0, zonal, STRIP):
        total = jnp.zeros((rows, STRIP, field.shape[2]), F32)
        for b in range(STENCIL_SIDE):
            first = EDGE - half + b + start
            slab = ext[:, first : first + STRIP, :]
            for a in range(STENCIL_SIDE):
                k = a * STENCIL_SIDE + b
                total = total + taps[k : k + 1, :][None] * slab[a : a + rows]
        centred = total - jnp.mean(total, axis=-1, keepdims=True)
        recip = lax.rsqrt(jnp.mean(centred * centred, axis=-1, keepdims=True) + EPSILON)
        value = centred * recip
        rounded = (gain[...][None] * value).astype(BF16)
        wide = jnp.broadcast_to(recip, value.shape)
        for i in range(rows):
            at = pl.ds(i * zonal + start, STRIP)
            scaled[at, :] = value[i]
            inverse[at, :] = wide[i]
            normed[at, :] = rounded[i]


def selector(rows, columns, chunk_bits, offsets, turned):
    place = lax.broadcasted_iota(jnp.int32, (rows, columns), 1 if turned else 0)
    variable = lax.broadcasted_iota(jnp.int32, (rows, columns), 0 if turned else 1)
    chunk = lax.shift_right_logical(place, chunk_bits)
    inside = place & ((1 << chunk_bits) - 1)
    result = jnp.zeros((rows, columns), F32)
    for offset in offsets:
        j = inside - offset
        hit = (j >= 0) & (j < PER_CHUNK) & (chunk * PER_CHUNK + j == variable)
        result = jnp.where(hit, 1.0, result)
    return result.astype(BF16)


def matrices(shards):
    count, owned, channels = shards.shape[0], shards.shape[1] // 2, shards.shape[2]
    return (
        shards[:, :owned, :].reshape(count * owned, channels),
        shards[:, owned:, :].reshape(count * owned, channels),
    )


def mlp_body(normed, mine, theirs, field, readout, gated, upper, residual, chunks):
    points, channels = normed.shape
    halves = [matrices(mine), matrices(theirs)]
    wide = upper.shape[1] // 2
    for k, (widen, _) in enumerate(halves):
        upper[:, k * wide : (k + 1) * wide] = dot(normed[...], widen, (1, 1))

    def step(i, carry):
        at = pl.ds(pl.multiple_of(i * 16, 16), 16)
        gated[at, :] = gelu_value(upper[at, :]).astype(BF16)
        return carry

    lax.fori_loop(0, points // 16, step, 0, unroll=2)
    mixed = sum(
        dot(gated[:, k * wide : (k + 1) * wide], shrink, (1, 0))
        for k, (_, shrink) in enumerate(halves)
    )
    residual[...] = (field[...].reshape(points, channels).astype(F32) + mixed).astype(BF16)
    members = chunks.shape[0]
    spread = dot(selector(members * CHUNK_ROWS, readout.shape[0], 3, (0,), False), readout[...], (1, 0))
    outlook = dot(spread.astype(BF16), residual[...], (1, 1))
    for e in range(members):
        chunks[e] = outlook[e * CHUNK_ROWS : (e + 1) * CHUNK_ROWS].astype(BF16)


def slope_body(upper, slope):
    def step(i, carry):
        at = pl.ds(pl.multiple_of(i * 16, 16), 16)
        slope[at, :] = gelu_slope(upper[at, :])
        return carry

    lax.fori_loop(0, upper.shape[0] // 16, step, 0, unroll=2)


def outlook_body(readout, residual, out):
    out[...] = dot(readout[...], residual[...], (1, 1)).astype(BF16)


def pair_body(place, everyone, truth, weight, payload, loss, rows, seen):
    member = place[1]
    members, _, points = everyone.shape
    _, bands, lanes = truth.shape
    variables = TAPS_AT
    first = jnp.minimum(member * PER_CHUNK, variables - PER_CHUNK)
    for j in range(PER_CHUNK):
        row = truth[jnp.minimum(member * PER_CHUNK + j, variables - 1) - first]
        for q in range(bands):
            seen[j : j + 1, q * lanes : (q + 1) * lanes] = row[q : q + 1]
    seen[PER_CHUNK:, :] = jnp.zeros((CHUNK_ROWS - PER_CHUNK, points), F32)
    limit = jnp.minimum(PER_CHUNK, variables - member * PER_CHUNK)
    real = lax.broadcasted_iota(jnp.int32, (CHUNK_ROWS, lanes), 0) < limit
    pair_norm = 1.0 / (members * (members - 1))
    lost = jnp.zeros((CHUNK_ROWS, lanes), F32)
    for q in range(points // lanes):
        at = slice(q * lanes, (q + 1) * lanes)
        y = [everyone[m, :, at].astype(F32) for m in range(members)]
        spread = [jnp.full((CHUNK_ROWS, lanes), SMOOTHING**0.5, F32) for _ in range(members)]
        ranks = [jnp.zeros((CHUNK_ROWS, lanes), F32) for _ in range(members)]
        for m in range(members):
            for k in range(m):
                gap = y[m] - y[k]
                square = gap * gap + SMOOTHING
                root = lax.rsqrt(square)
                size, tilt = square * root, gap * root
                spread[m], spread[k] = spread[m] + size, spread[k] + size
                ranks[m], ranks[k] = ranks[m] + tilt, ranks[k] - tilt
        scale = weight[0:1, at]
        for m in range(members):
            miss = y[m] - seen[:, at]
            square = miss * miss + SMOOTHING
            root = lax.rsqrt(square)
            term = scale * (square * root * (1.0 / members) - 0.5 * pair_norm * spread[m])
            lost = lost + jnp.where(real, term, 0.0)
            flow = scale * (miss * root * (1.0 / members) - pair_norm * ranks[m])
            average = spread[m] * (1.0 / (members - 1))
            high = average.astype(BF16).astype(F32)
            rows[m, 0:CHUNK_ROWS, at] = jnp.where(real, flow, 0.0)
            rows[m, PER_CHUNK : PER_CHUNK + CHUNK_ROWS, at] = high
            rows[m, 2 * PER_CHUNK : 16, at] = (average - high)[: 16 - 2 * PER_CHUNK]
    for m in range(members):
        payload[m] = rows[m].astype(BF16)
    loss[...] = jnp.sum(lost, axis=0, keepdims=True)


def average_body(back, out):
    members, height, points = back.shape
    pick = selector(out.shape[0], members * height, 4, (PER_CHUNK, 2 * PER_CHUNK), True)
    out[...] = dot(pick, back[...].reshape(members * height, points), (1, 0))


def backward_body(
    back, readout, residual, gated, slope, normed, scaled, inverse, gain, mine, theirs,
    widen_grad, shrink_grad, readout_grad, gain_grad, back_depth, gate, back_upper,
):
    members, height, points = back.shape
    halves = [matrices(mine), matrices(theirs)]
    wide = slope.shape[1] // 2
    flow = back[...].reshape(members * height, points)
    spread = dot(selector(members * height, readout.shape[0], 4, (0,), False), readout[...], (1, 0))
    back_residual = dot(flow, spread.astype(BF16), (0, 0)).astype(BF16)
    for k, (_, shrink) in enumerate(halves):
        gate[:, k * wide : (k + 1) * wide] = dot(back_residual, shrink, (1, 1))
    readout_grad[...] = dot(flow, residual[...], (1, 0))
    shrink_grad[...] = dot(gated[...], back_residual, (0, 0))

    def step(i, carry):
        at = pl.ds(pl.multiple_of(i * 16, 16), 16)
        back_upper[at, :] = (gate[at, :] * slope[at, :]).astype(BF16)
        return carry

    lax.fori_loop(0, points // 16, step, 0, unroll=2)
    back_norm = sum(
        dot(back_upper[:, k * wide : (k + 1) * wide], widen, (1, 0))
        for k, (widen, _) in enumerate(halves)
    )
    widen_grad[...] = dot(back_upper[...], normed[...], (0, 0))
    value = scaled[...]
    product = back_norm * value
    gain_grad[...] = jnp.sum(product, axis=0, keepdims=True)
    g = back_norm * gain[...]
    p = jnp.mean(g, axis=-1, keepdims=True)
    q = jnp.mean(g * value, axis=-1, keepdims=True)
    back_depth[...] = inverse[...] * (g - p - value * q)


def pack_body(back_depth, ext, widen_grad, shrink_grad, readout_grad, gain_grad, loss, send, keep, small):
    half = STENCIL_SIDE // 2
    zonal = ext.shape[1] - 2 * EDGE
    rows = back_depth.shape[0] // zonal
    channels = ext.shape[2]
    members = small.shape[0] // CHUNK_ROWS
    height = readout_grad.shape[0] // members
    small[TAPS_AT + 48 :, :] = jnp.zeros((small.shape[0] - TAPS_AT - 48, channels), F32)
    for e in range(members):
        count = min(PER_CHUNK, TAPS_AT - e * PER_CHUNK)
        if count > 0:
            small[e * PER_CHUNK : e * PER_CHUNK + count, :] = readout_grad[e * height : e * height + count, :]
    for b in range(STENCIL_SIDE):
        totals = [jnp.zeros((STRIP, channels), F32) for _ in range(STENCIL_SIDE)]
        for start in range(0, zonal, STRIP):
            first = EDGE - half + b + start
            slab = ext[:, first : first + STRIP, :]
            up = [back_depth[i * zonal + start : i * zonal + start + STRIP, :] for i in range(rows)]
            for a in range(STENCIL_SIDE):
                for i in range(rows):
                    totals[a] = totals[a] + up[i] * slab[i + a]
        for a in range(STENCIL_SIDE):
            k = TAPS_AT + a * STENCIL_SIDE + b
            small[k : k + 1, :] = jnp.sum(totals[a], axis=0, keepdims=True)
    small[TAPS_AT + 49 : TAPS_AT + 50, :] = gain_grad[...]
    small[TAPS_AT + 50 : TAPS_AT + 51, :] = loss[...]
    depth_z = DEPTH_Z
    for e in range(members):
        tail = small[e * CHUNK_ROWS : (e + 1) * CHUNK_ROWS, :]
        for h in range(2):
            d = 2 * e + h
            for mat, grad in enumerate((widen_grad, shrink_grad)):
                at = slice(mat * depth_z, (mat + 1) * depth_z)
                base = h * depth_z * members + e
                keep[d, at, :] = grad[pl.ds(base, depth_z, stride=members), :]
                base = base + 2 * depth_z * members
                send[d, at, :] = grad[pl.ds(base, depth_z, stride=members), :]
            keep[d, 2 * depth_z :, :] = tail
            send[d, 2 * depth_z :, :] = tail


def gradient_body(
    place, back, readout, residual, gated, slope, normed, scaled, inverse, gain, mine, theirs, loss,
    field, partner, other, send, keep, ext, gate, back_upper, widen_grad, shrink_grad, readout_grad, gain_grad, back_depth, small,
):
    fill_rows(place, field, partner, other, ext)
    backward_body(
        back, readout, residual, gated, slope, normed, scaled, inverse, gain, mine, theirs,
        widen_grad, shrink_grad, readout_grad, gain_grad, back_depth, gate, back_upper,
    )
    pack_body(
        back_depth, ext, widen_grad, shrink_grad, readout_grad, gain_grad, loss,
        send, keep, small,
    )


def final_body(arrived, up, down, taps, gain, readout, loss, small):
    members = arrived.shape[0]
    for e in range(members):
        small[e * CHUNK_ROWS : (e + 1) * CHUNK_ROWS, :] = arrived[e, 0:CHUNK_ROWS, :]
        up[e : e + 1, :] = arrived[e, CHUNK_ROWS : CHUNK_ROWS + 1, :]
        down[e : e + 1, :] = arrived[e, CHUNK_ROWS + 1 : CHUNK_ROWS + 2, :]
    readout[...] = small[0:TAPS_AT, :]
    taps[...] = small[TAPS_AT : TAPS_AT + 49, :]
    gain[...] = small[TAPS_AT + 49 : TAPS_AT + 50, :]
    loss[...] = jnp.sum(small[TAPS_AT + 50 : TAPS_AT + 51, :], axis=1, keepdims=True)


def on_device(
    features,
    random_perturbation,
    observed_truth,
    stencil_taps,
    affine_factor,
    widen_matrix,
    shrink_matrix,
    readout_matrix,
):
    rows, zonal, channels = features.shape
    variables = readout_matrix.shape[0]
    half = STENCIL_SIDE // 2
    bands, members = lax.axis_size("lat"), lax.axis_size("ens")
    band, member = lax.axis_index("lat"), lax.axis_index("ens")
    points = rows * zonal
    latitudes = rows * bands
    hidden = widen_matrix.shape[0] * bands
    depth_z = DEPTH_Z
    share = CHUNK_ROWS
    place = jnp.stack([lax.rem(band, 2), member]).astype(jnp.int32)
    gain = affine_factor.reshape(1, channels)

    field = (features.astype(F32) + random_perturbation[0].astype(F32)).astype(BF16)
    partner, other = halo_rows(field, half)
    shape = (bands // 2,) + widen_matrix.shape
    pair = jnp.concatenate(
        [jnp.broadcast_to(widen_matrix[None], shape), jnp.broadcast_to(shrink_matrix[None], shape)],
        axis=1,
    )
    mine = exchange(pair, AXES, weight_groups(members, bands))
    mine, partner, other = lax.optimization_barrier((mine, partner, other))
    theirs = core_swap(mine)
    latitude = (band * rows + jnp.arange(points, dtype=jnp.int32) // zonal).astype(F32)
    area = jnp.cos(math.pi * ((latitude + 0.5) / latitudes - 0.5))
    weight = (area * (1.0 / (latitudes * zonal)))[None, :]

    wide = (rows + 2 * half, zonal + 2 * EDGE, channels)
    scaled, inverse, normed = vmem_call(
        stencil_body,
        [
            ((points, channels), F32),
            ((points, channels), F32),
            ((points, channels), BF16),
        ],
        [pltpu.VMEM(wide, F32)],
        scalars=1,
        vectors=5,
    )(place, field, partner, other, stencil_taps, gain)
    gated, upper, residual, chunks = vmem_call(
        mlp_body,
        [
            ((points, hidden), BF16),
            ((points, hidden), F32),
            ((points, channels), BF16),
            ((members, CHUNK_ROWS, points), BF16),
        ],
        vectors=5,
    )(normed, mine, theirs, field, readout_matrix)
    everyone = exchange(chunks, "ens")
    (slope,) = vmem_call(slope_body, [((points, hidden), F32)], vectors=1, aliases={0: 0})(upper)
    first = jnp.minimum(member * PER_CHUNK, variables - PER_CHUNK)
    truth = lax.dynamic_slice_in_dim(observed_truth, first, PER_CHUNK, axis=0)
    (outlook,) = vmem_call(outlook_body, [((variables, points), BF16)], vectors=2)(
        readout_matrix, residual
    )
    sample_outlook = outlook.reshape(1, variables, rows, zonal)
    payload, loss = vmem_call(
        pair_body,
        [((members, 16, points), BF16), ((1, zonal), F32)],
        [pltpu.VMEM((members, 16, points), F32), pltpu.VMEM((CHUNK_ROWS, points), F32)],
        scalars=1,
        vectors=3,
    )(place, everyone, truth, weight)
    back = exchange(payload, "ens")
    (average,) = vmem_call(average_body, [((variables, points), F32)], vectors=1)(back)
    sample_average_spread = average.reshape(1, variables, rows, zonal)

    packet = ((2 * members, 2 * depth_z + share, channels), F32)
    send, keep = vmem_call(
        gradient_body,
        [packet, packet],
        [
            pltpu.VMEM(wide, F32),
            pltpu.VMEM((points, hidden), F32),
            pltpu.VMEM((points, hidden), BF16),
            pltpu.VMEM((hidden, channels), F32),
            pltpu.VMEM((hidden, channels), F32),
            pltpu.VMEM((members * 16, channels), F32),
            pltpu.VMEM((1, channels), F32),
            pltpu.VMEM((points, channels), F32),
            pltpu.VMEM((members * share, channels), F32),
        ],
        scalars=1,
        vectors=15,
    )(
        place, back, readout_matrix, residual, gated, slope, normed, scaled, inverse, gain, mine,
        theirs, loss, field, partner, other,
    )

    total = (keep + core_swap(send)).astype(BF16)
    arrived = exchange(total, AXES, plane_groups(members, bands)).astype(F32)
    columns = [
        list(range(h * bands // 2 + c, (h + 1) * bands // 2, 2)) for h in range(2) for c in range(2)
    ]
    part = jnp.sum(arrived, axis=0)
    outgoing = jnp.concatenate(
        [
            jnp.broadcast_to(part[None, 2 * depth_z :], (depth_z, share, channels)),
            part[: 2 * depth_z].reshape(2, depth_z, channels).transpose(1, 0, 2),
        ],
        axis=1,
    )
    done = jnp.sum(exchange(outgoing, "lat", columns), axis=0)
    arrived = exchange(jnp.broadcast_to(done[None], (members,) + done.shape), "ens")
    up, down, taps, gain_total, readout, loss = vmem_call(
        final_body,
        [
            ((members, channels), F32),
            ((members, channels), F32),
            ((STENCIL_SIDE * STENCIL_SIDE, channels), F32),
            ((1, channels), F32),
            ((variables, channels), F32),
            ((1, 1), F32),
        ],
        [pltpu.VMEM((members * share, channels), F32)],
        vectors=1,
        kept=range(6),
    )(arrived)
    return (
        loss.reshape(()),
        taps,
        gain_total.reshape(channels),
        up,
        down,
        readout,
        sample_outlook,
        sample_average_spread,
    )


def solution(mesh):
    in_specs = (
        P("lat", None, None),
        P("ens", "lat", None, None),
        P(None, "lat", None),
        P(),
        P(),
        P("lat", None),
        P("lat", None),
        P(),
    )
    out_specs = (
        P(),
        P(),
        P(),
        P("lat", None),
        P("lat", None),
        P(),
        P("ens", None, "lat", None),
        P("ens", None, "lat", None),
    )

    return jax.shard_map(
        on_device, mesh=mesh, in_specs=in_specs, out_specs=out_specs, check_vma=False
    )
```

```python
import math

import jax
import jax.numpy as jnp
from jax import lax
from jax.experimental import pallas as pl
from jax.experimental.pallas import tpu as pltpu
from jax.sharding import PartitionSpec as P

STENCIL_SIDE = 7
SQRT_TWO_PI = 0.7978845608028654
CUBIC = 0.044715
EPSILON = 1e-06
SMOOTHING = 0.01
PER_CHUNK = 5
CHUNK_ROWS = 8
EDGE = 8
STRIP = 16
TAPS_AT = 69
DEPTH_Z = 8
F32, BF16 = jnp.float32, jnp.bfloat16


def core_swap(value):
    count = lax.axis_size("lat")
    return lax.ppermute(value, "lat", [(i, i ^ 1) for i in range(count)])


def odd_swap(value):
    count = lax.axis_size("lat")
    pairs = [(i, i + 1) for i in range(1, count - 1, 2)]
    return lax.ppermute(value, "lat", pairs + [(b, a) for a, b in pairs])


def halo_rows(field, half):
    even = lax.rem(lax.axis_index("lat"), 2) == 0
    head, tail = field[:half], field[field.shape[0] - half :]
    return core_swap(jnp.where(even, tail, head)), odd_swap(jnp.where(even, head, tail))


def exchange(value, axis, groups=None):
    return lax.all_to_all(value, axis, 0, 0, tiled=True, axis_index_groups=groups)


AXES = ("ens", "lat")


def weight_groups(members, bands):
    half = bands // 2
    groups = []
    for e in range(members):
        far = e // 4 * 4 + (e + 2) % 4
        for c in range(2):
            groups.append(
                [e * bands + b for b in range(c, half, 2)]
                + [far * bands + b for b in range(half + c, bands, 2)]
            )
    return groups


def plane_groups(members, bands):
    half = bands // 2
    return [
        [e * bands + h * half + rest for e in range(members) for h in range(2)]
        for rest in range(half)
    ]


def gelu_value(u):
    inner = jnp.tanh(SQRT_TWO_PI * (u + CUBIC * u * u * u))
    return 0.5 * u * (1.0 + inner)


def gelu_slope(u):
    inner = jnp.tanh(SQRT_TWO_PI * (u + CUBIC * u * u * u))
    return 0.5 * (1.0 + inner) + 0.5 * u * (1.0 - inner * inner) * SQRT_TWO_PI * (
        1.0 + 3.0 * CUBIC * u * u
    )


def vmem_call(body, outs, scratch=(), scalars=0, vectors=0, kept=(), aliases=None):
    vmem = pl.BlockSpec(memory_space=pltpu.VMEM)
    smem = pl.BlockSpec(memory_space=pltpu.SMEM)
    call = pl.pallas_call(
        body,
        out_shape=[
            jax.ShapeDtypeStruct(*out) if i in kept else pltpu.VMEM(*out)
            for i, out in enumerate(outs)
        ],
        in_specs=[smem] * scalars + [vmem] * vectors,
        out_specs=[vmem] * len(outs),
        scratch_shapes=list(scratch),
        input_output_aliases=aliases or {},
        compiler_params=pltpu.CompilerParams(vmem_limit_bytes=16 << 20),
    )

    def run(*operands):
        operands = operands[:scalars] + tuple(
            pltpu.with_memory_space_constraint(x, pltpu.VMEM) for x in operands[scalars:]
        )
        return call(*operands)

    return run


def dot(a, b, contract):
    return lax.dot_general(a, b, ((contract[:1], contract[1:]), ((), ())), preferred_element_type=F32)


def fill_rows(place, field, partner, other, ext):
    even = place[0] == 0
    rows, zonal, _ = field.shape
    half = STENCIL_SIDE // 2
    for r in range(rows + 2 * half):
        if r < half:
            row = jnp.where(even, other[r].astype(F32), partner[r].astype(F32))
        elif r < rows + half:
            row = field[r - half].astype(F32)
        else:
            k = r - rows - half
            row = jnp.where(even, partner[k].astype(F32), other[k].astype(F32))
        ext[r, EDGE : EDGE + zonal, :] = row
        ext[r, EDGE - half : EDGE, :] = row[zonal - half :]
        ext[r, EDGE + zonal : EDGE + zonal + half, :] = row[:half]


def stencil_body(place, field, partner, other, taps, gain, scaled, inverse, normed, ext):
    rows, zonal, _ = field.shape
    half = STENCIL_SIDE // 2
    fill_rows(place, field, partner, other, ext)
    for start in range(0, zonal, STRIP):
        total = jnp.zeros((rows, STRIP, field.shape[2]), F32)
        for b in range(STENCIL_SIDE):
            first = EDGE - half + b + start
            slab = ext[:, first : first + STRIP, :]
            for a in range(STENCIL_SIDE):
                k = a * STENCIL_SIDE + b
                total = total + taps[k : k + 1, :][None] * slab[a : a + rows]
        centred = total - jnp.mean(total, axis=-1, keepdims=True)
        recip = lax.rsqrt(jnp.mean(centred * centred, axis=-1, keepdims=True) + EPSILON)
        value = centred * recip
        rounded = (gain[...][None] * value).astype(BF16)
        wide = jnp.broadcast_to(recip, value.shape)
        for i in range(rows):
            at = pl.ds(i * zonal + start, STRIP)
            scaled[at, :] = value[i]
            inverse[at, :] = wide[i]
            normed[at, :] = rounded[i]


def selector(rows, columns, chunk_bits, offsets, turned):
    place = lax.broadcasted_iota(jnp.int32, (rows, columns), 1 if turned else 0)
    variable = lax.broadcasted_iota(jnp.int32, (rows, columns), 0 if turned else 1)
    chunk = lax.shift_right_logical(place, chunk_bits)
    inside = place & ((1 << chunk_bits) - 1)
    result = jnp.zeros((rows, columns), F32)
    for offset in offsets:
        j = inside - offset
        hit = (j >= 0) & (j < PER_CHUNK) & (chunk * PER_CHUNK + j == variable)
        result = jnp.where(hit, 1.0, result)
    return result.astype(BF16)


def matrices(shards):
    count, owned, channels = shards.shape[0], shards.shape[1] // 2, shards.shape[2]
    return (
        shards[:, :owned, :].reshape(count * owned, channels),
        shards[:, owned:, :].reshape(count * owned, channels),
    )


def mlp_body(normed, mine, theirs, field, readout, gated, upper, residual, chunks):
    points, channels = normed.shape
    halves = [matrices(mine), matrices(theirs)]
    wide = upper.shape[1] // 2
    for k, (widen, _) in enumerate(halves):
        upper[:, k * wide : (k + 1) * wide] = dot(normed[...], widen, (1, 1))

    def step(i, carry):
        at = pl.ds(pl.multiple_of(i * 16, 16), 16)
        gated[at, :] = gelu_value(upper[at, :]).astype(BF16)
        return carry

    lax.fori_loop(0, points // 16, step, 0, unroll=2)
    mixed = sum(
        dot(gated[:, k * wide : (k + 1) * wide], shrink, (1, 0))
        for k, (_, shrink) in enumerate(halves)
    )
    residual[...] = (field[...].reshape(points, channels).astype(F32) + mixed).astype(BF16)
    members = chunks.shape[0]
    spread = dot(selector(members * CHUNK_ROWS, readout.shape[0], 3, (0,), False), readout[...], (1, 0))
    outlook = dot(spread.astype(BF16), residual[...], (1, 1))
    for e in range(members):
        chunks[e] = outlook[e * CHUNK_ROWS : (e + 1) * CHUNK_ROWS].astype(BF16)


def slope_body(upper, slope):
    def step(i, carry):
        at = pl.ds(pl.multiple_of(i * 16, 16), 16)
        slope[at, :] = gelu_slope(upper[at, :])
        return carry

    lax.fori_loop(0, upper.shape[0] // 16, step, 0, unroll=2)


def outlook_body(readout, residual, out):
    out[...] = dot(readout[...], residual[...], (1, 1)).astype(BF16)


def pair_body(place, everyone, truth, weight, payload, loss, rows, seen):
    member = place[1]
    members, _, points = everyone.shape
    _, bands, lanes = truth.shape
    variables = TAPS_AT
    first = jnp.minimum(member * PER_CHUNK, variables - PER_CHUNK)
    for j in range(PER_CHUNK):
        row = truth[jnp.minimum(member * PER_CHUNK + j, variables - 1) - first]
        for q in range(bands):
            seen[j : j + 1, q * lanes : (q + 1) * lanes] = row[q : q + 1]
    seen[PER_CHUNK:, :] = jnp.zeros((CHUNK_ROWS - PER_CHUNK, points), F32)
    limit = jnp.minimum(PER_CHUNK, variables - member * PER_CHUNK)
    real = lax.broadcasted_iota(jnp.int32, (CHUNK_ROWS, lanes), 0) < limit
    pair_norm = 1.0 / (members * (members - 1))
    lost = jnp.zeros((CHUNK_ROWS, lanes), F32)
    for q in range(points // lanes):
        at = slice(q * lanes, (q + 1) * lanes)
        y = [everyone[m, :, at].astype(F32) for m in range(members)]
        spread = [jnp.full((CHUNK_ROWS, lanes), SMOOTHING**0.5, F32) for _ in range(members)]
        ranks = [jnp.zeros((CHUNK_ROWS, lanes), F32) for _ in range(members)]
        for m in range(members):
            for k in range(m):
                gap = y[m] - y[k]
                square = gap * gap + SMOOTHING
                root = lax.rsqrt(square)
                size, tilt = square * root, gap * root
                spread[m], spread[k] = spread[m] + size, spread[k] + size
                ranks[m], ranks[k] = ranks[m] + tilt, ranks[k] - tilt
        scale = weight[0:1, at]
        for m in range(members):
            miss = y[m] - seen[:, at]
            square = miss * miss + SMOOTHING
            root = lax.rsqrt(square)
            term = scale * (square * root * (1.0 / members) - 0.5 * pair_norm * spread[m])
            lost = lost + jnp.where(real, term, 0.0)
            flow = scale * (miss * root * (1.0 / members) - pair_norm * ranks[m])
            average = spread[m] * (1.0 / (members - 1))
            high = average.astype(BF16).astype(F32)
            rows[m, 0:CHUNK_ROWS, at] = jnp.where(real, flow, 0.0)
            rows[m, PER_CHUNK : PER_CHUNK + CHUNK_ROWS, at] = high
            rows[m, 2 * PER_CHUNK : 16, at] = (average - high)[: 16 - 2 * PER_CHUNK]
    for m in range(members):
        payload[m] = rows[m].astype(BF16)
    loss[...] = jnp.sum(lost, axis=0, keepdims=True)


def average_body(back, out):
    members, height, points = back.shape
    pick = selector(out.shape[0], members * height, 4, (PER_CHUNK, 2 * PER_CHUNK), True)
    out[...] = dot(pick, back[...].reshape(members * height, points), (1, 0))


def backward_body(
    back, readout, residual, gated, slope, normed, scaled, inverse, gain, mine, theirs,
    widen_grad, shrink_grad, readout_grad, gain_grad, back_depth, gate, back_upper,
):
    members, height, points = back.shape
    halves = [matrices(mine), matrices(theirs)]
    wide = slope.shape[1] // 2
    flow = back[...].reshape(members * height, points)
    spread = dot(selector(members * height, readout.shape[0], 4, (0,), False), readout[...], (1, 0))
    back_residual = dot(flow, spread.astype(BF16), (0, 0)).astype(BF16)
    for k, (_, shrink) in enumerate(halves):
        gate[:, k * wide : (k + 1) * wide] = dot(back_residual, shrink, (1, 1))
    readout_grad[...] = dot(flow, residual[...], (1, 0))
    shrink_grad[...] = dot(gated[...], back_residual, (0, 0))

    def step(i, carry):
        at = pl.ds(pl.multiple_of(i * 16, 16), 16)
        back_upper[at, :] = (gate[at, :] * slope[at, :]).astype(BF16)
        return carry

    lax.fori_loop(0, points // 16, step, 0, unroll=2)
    back_norm = sum(
        dot(back_upper[:, k * wide : (k + 1) * wide], widen, (1, 0))
        for k, (widen, _) in enumerate(halves)
    )
    widen_grad[...] = dot(back_upper[...], normed[...], (0, 0))
    value = scaled[...]
    product = back_norm * value
    gain_grad[...] = jnp.sum(product, axis=0, keepdims=True)
    g = back_norm * gain[...]
    p = jnp.mean(g, axis=-1, keepdims=True)
    q = jnp.mean(g * value, axis=-1, keepdims=True)
    back_depth[...] = inverse[...] * (g - p - value * q)


def pack_body(back_depth, ext, widen_grad, shrink_grad, readout_grad, gain_grad, loss, packet, small, core):
    half = STENCIL_SIDE // 2
    zonal = ext.shape[1] - 2 * EDGE
    rows = back_depth.shape[0] // zonal
    channels = ext.shape[2]
    members = small.shape[0] // CHUNK_ROWS
    height = readout_grad.shape[0] // members
    small[TAPS_AT + 48 :, :] = jnp.zeros((small.shape[0] - TAPS_AT - 48, channels), F32)
    for e in range(members):
        count = min(PER_CHUNK, TAPS_AT - e * PER_CHUNK)
        if count > 0:
            small[e * PER_CHUNK : e * PER_CHUNK + count, :] = readout_grad[e * height : e * height + count, :]
    for b in range(STENCIL_SIDE):
        totals = [jnp.zeros((STRIP, channels), F32) for _ in range(STENCIL_SIDE)]
        for start in range(0, zonal, STRIP):
            first = EDGE - half + b + start
            slab = ext[:, first : first + STRIP, :]
            up = [back_depth[i * zonal + start : i * zonal + start + STRIP, :] for i in range(rows)]
            for a in range(STENCIL_SIDE):
                for i in range(rows):
                    totals[a] = totals[a] + up[i] * slab[i + a]
        for a in range(STENCIL_SIDE):
            k = TAPS_AT + a * STENCIL_SIDE + b
            small[k : k + 1, :] = jnp.sum(totals[a], axis=0, keepdims=True)
    small[TAPS_AT + 49 : TAPS_AT + 50, :] = gain_grad[...]
    small[TAPS_AT + 50 : TAPS_AT + 51, :] = loss[...]
    depth_z = DEPTH_Z
    for e in range(members):
        tail = small[e * CHUNK_ROWS : (e + 1) * CHUNK_ROWS, :]
        for h in range(2):
            d = 2 * e + h
            for mat, grad in enumerate((widen_grad, shrink_grad)):
                base = h * depth_z * members + e
                ours = grad[pl.ds(base, depth_z, stride=members), :]
                base = base + 2 * depth_z * members
                others = grad[pl.ds(base, depth_z, stride=members), :]
                first = jnp.where(core == 0, ours, others)
                second = jnp.where(core == 0, others, ours)
                at = slice(2 * mat * depth_z, 2 * (mat + 1) * depth_z)
                packet[d, at, :] = jnp.concatenate([first, second], axis=0).astype(BF16)
            packet[d, 4 * depth_z :, :] = tail.astype(BF16)


def gradient_body(
    place, back, readout, residual, gated, slope, normed, scaled, inverse, gain, mine, theirs, loss,
    field, partner, other, packet, ext, gate, back_upper, widen_grad, shrink_grad, readout_grad, gain_grad, back_depth, small,
):
    fill_rows(place, field, partner, other, ext)
    backward_body(
        back, readout, residual, gated, slope, normed, scaled, inverse, gain, mine, theirs,
        widen_grad, shrink_grad, readout_grad, gain_grad, back_depth, gate, back_upper,
    )
    pack_body(
        back_depth, ext, widen_grad, shrink_grad, readout_grad, gain_grad, loss,
        packet, small, place[0],
    )


def final_body(arrived, up, down, taps, gain, readout, loss, small):
    members = arrived.shape[0]
    for e in range(members):
        small[e * CHUNK_ROWS : (e + 1) * CHUNK_ROWS, :] = arrived[e, 0:CHUNK_ROWS, :]
        up[e : e + 1, :] = arrived[e, CHUNK_ROWS : CHUNK_ROWS + 1, :]
        down[e : e + 1, :] = arrived[e, CHUNK_ROWS + 1 : CHUNK_ROWS + 2, :]
    readout[...] = small[0:TAPS_AT, :]
    taps[...] = small[TAPS_AT : TAPS_AT + 49, :]
    gain[...] = small[TAPS_AT + 49 : TAPS_AT + 50, :]
    loss[...] = jnp.sum(small[TAPS_AT + 50 : TAPS_AT + 51, :], axis=1, keepdims=True)


def on_device(
    features,
    random_perturbation,
    observed_truth,
    stencil_taps,
    affine_factor,
    widen_matrix,
    shrink_matrix,
    readout_matrix,
):
    rows, zonal, channels = features.shape
    variables = readout_matrix.shape[0]
    half = STENCIL_SIDE // 2
    bands, members = lax.axis_size("lat"), lax.axis_size("ens")
    band, member = lax.axis_index("lat"), lax.axis_index("ens")
    points = rows * zonal
    latitudes = rows * bands
    hidden = widen_matrix.shape[0] * bands
    depth_z = DEPTH_Z
    share = CHUNK_ROWS
    place = jnp.stack([lax.rem(band, 2), member]).astype(jnp.int32)
    gain = affine_factor.reshape(1, channels)

    field = (features.astype(F32) + random_perturbation[0].astype(F32)).astype(BF16)
    partner, other = halo_rows(field, half)
    shape = (bands // 2,) + widen_matrix.shape
    pair = jnp.concatenate(
        [jnp.broadcast_to(widen_matrix[None], shape), jnp.broadcast_to(shrink_matrix[None], shape)],
        axis=1,
    )
    mine = exchange(pair, AXES, weight_groups(members, bands))
    mine, partner, other = lax.optimization_barrier((mine, partner, other))
    theirs = core_swap(mine)
    latitude = (band * rows + jnp.arange(points, dtype=jnp.int32) // zonal).astype(F32)
    area = jnp.cos(math.pi * ((latitude + 0.5) / latitudes - 0.5))
    weight = (area * (1.0 / (latitudes * zonal)))[None, :]

    wide = (rows + 2 * half, zonal + 2 * EDGE, channels)
    scaled, inverse, normed = vmem_call(
        stencil_body,
        [
            ((points, channels), F32),
            ((points, channels), F32),
            ((points, channels), BF16),
        ],
        [pltpu.VMEM(wide, F32)],
        scalars=1,
        vectors=5,
    )(place, field, partner, other, stencil_taps, gain)
    gated, upper, residual, chunks = vmem_call(
        mlp_body,
        [
            ((points, hidden), BF16),
            ((points, hidden), F32),
            ((points, channels), BF16),
            ((members, CHUNK_ROWS, points), BF16),
        ],
        vectors=5,
    )(normed, mine, theirs, field, readout_matrix)
    everyone = exchange(chunks, "ens")
    (slope,) = vmem_call(slope_body, [((points, hidden), F32)], vectors=1, aliases={0: 0})(upper)
    first = jnp.minimum(member * PER_CHUNK, variables - PER_CHUNK)
    truth = lax.dynamic_slice_in_dim(observed_truth, first, PER_CHUNK, axis=0)
    (outlook,) = vmem_call(outlook_body, [((variables, points), BF16)], vectors=2)(
        readout_matrix, residual
    )
    sample_outlook = outlook.reshape(1, variables, rows, zonal)
    payload, loss = vmem_call(
        pair_body,
        [((members, 16, points), BF16), ((1, zonal), F32)],
        [pltpu.VMEM((members, 16, points), F32), pltpu.VMEM((CHUNK_ROWS, points), F32)],
        scalars=1,
        vectors=3,
    )(place, everyone, truth, weight)
    back = exchange(payload, "ens")
    (average,) = vmem_call(average_body, [((variables, points), F32)], vectors=1)(back)
    sample_average_spread = average.reshape(1, variables, rows, zonal)

    (packet,) = vmem_call(
        gradient_body,
        [((2 * members, 4 * depth_z + share, channels), BF16)],
        [
            pltpu.VMEM(wide, F32),
            pltpu.VMEM((points, hidden), F32),
            pltpu.VMEM((points, hidden), BF16),
            pltpu.VMEM((hidden, channels), F32),
            pltpu.VMEM((hidden, channels), F32),
            pltpu.VMEM((members * 16, channels), F32),
            pltpu.VMEM((1, channels), F32),
            pltpu.VMEM((points, channels), F32),
            pltpu.VMEM((members * share, channels), F32),
        ],
        scalars=1,
        vectors=15,
    )(
        place, back, readout_matrix, residual, gated, slope, normed, scaled, inverse, gain, mine,
        theirs, loss, field, partner, other,
    )

    arrived = exchange(packet, AXES, plane_groups(members, bands)).astype(F32)
    part = jnp.sum(arrived, axis=0)
    outgoing = jnp.concatenate(
        [
            jnp.broadcast_to(part[None, 4 * depth_z :], (2 * depth_z, share, channels)),
            part[: 4 * depth_z].reshape(2, 2, depth_z, channels).transpose(2, 1, 0, 3).reshape(
                2 * depth_z, 2, channels
            ),
        ],
        axis=1,
    )
    columns = [list(range(h * bands // 2, (h + 1) * bands // 2)) for h in range(2)]
    done = jnp.sum(exchange(outgoing, "lat", columns), axis=0)
    arrived = exchange(jnp.broadcast_to(done[None], (members,) + done.shape), "ens")
    up, down, taps, gain_total, readout, loss = vmem_call(
        final_body,
        [
            ((members, channels), F32),
            ((members, channels), F32),
            ((STENCIL_SIDE * STENCIL_SIDE, channels), F32),
            ((1, channels), F32),
            ((variables, channels), F32),
            ((1, 1), F32),
        ],
        [pltpu.VMEM((members * share, channels), F32)],
        vectors=1,
        kept=range(6),
    )(arrived)
    return (
        loss.reshape(()),
        taps,
        gain_total.reshape(channels),
        up,
        down,
        readout,
        sample_outlook,
        sample_average_spread,
    )


def solution(mesh):
    in_specs = (
        P("lat", None, None),
        P("ens", "lat", None, None),
        P(None, "lat", None),
        P(),
        P(),
        P("lat", None),
        P("lat", None),
        P(),
    )
    out_specs = (
        P(),
        P(),
        P(),
        P("lat", None),
        P("lat", None),
        P(),
        P("ens", None, "lat", None),
        P("ens", None, "lat", None),
    )

    return jax.shard_map(
        on_device, mesh=mesh, in_specs=in_specs, out_specs=out_specs, check_vma=False
    )
```

```python
import math

import jax
import jax.numpy as jnp
from jax import lax
from jax.experimental import pallas as pl
from jax.experimental.pallas import tpu as pltpu
from jax.sharding import PartitionSpec as P

STENCIL_SIDE = 7
SQRT_TWO_PI = 0.7978845608028654
CUBIC = 0.044715
EPSILON = 1e-06
SMOOTHING = 0.01
PER_CHUNK = 5
CHUNK_ROWS = 8
EDGE = 8
STRIP = 16
TAPS_AT = 69
DEPTH_Z = 8
F32, BF16 = jnp.float32, jnp.bfloat16


def core_swap(value):
    count = lax.axis_size("lat")
    return lax.ppermute(value, "lat", [(i, i ^ 1) for i in range(count)])


def odd_swap(value):
    count = lax.axis_size("lat")
    pairs = [(i, i + 1) for i in range(1, count - 1, 2)]
    return lax.ppermute(value, "lat", pairs + [(b, a) for a, b in pairs])


def halo_rows(field, half):
    even = lax.rem(lax.axis_index("lat"), 2) == 0
    head, tail = field[:half], field[field.shape[0] - half :]
    return core_swap(jnp.where(even, tail, head)), odd_swap(jnp.where(even, head, tail))


def exchange(value, axis, groups=None):
    return lax.all_to_all(value, axis, 0, 0, tiled=True, axis_index_groups=groups)


AXES = ("ens", "lat")


def weight_groups(members, bands):
    half = bands // 2
    groups = []
    for e in range(members):
        far = e // 4 * 4 + (e + 2) % 4
        for c in range(2):
            groups.append(
                [e * bands + b for b in range(c, half, 2)]
                + [far * bands + b for b in range(half + c, bands, 2)]
            )
    return groups


def plane_groups(members, bands):
    half = bands // 2
    return [
        [e * bands + h * half + rest for e in range(members) for h in range(2)]
        for rest in range(half)
    ]


def gelu_value(u):
    inner = jnp.tanh(SQRT_TWO_PI * (u + CUBIC * u * u * u))
    return 0.5 * u * (1.0 + inner)


def gelu_slope(u):
    inner = jnp.tanh(SQRT_TWO_PI * (u + CUBIC * u * u * u))
    return 0.5 * (1.0 + inner) + 0.5 * u * (1.0 - inner * inner) * SQRT_TWO_PI * (
        1.0 + 3.0 * CUBIC * u * u
    )


def vmem_call(body, outs, scratch=(), scalars=0, vectors=0, kept=(), aliases=None):
    vmem = pl.BlockSpec(memory_space=pltpu.VMEM)
    smem = pl.BlockSpec(memory_space=pltpu.SMEM)
    call = pl.pallas_call(
        body,
        out_shape=[
            jax.ShapeDtypeStruct(*out) if i in kept else pltpu.VMEM(*out)
            for i, out in enumerate(outs)
        ],
        in_specs=[smem] * scalars + [vmem] * vectors,
        out_specs=[vmem] * len(outs),
        scratch_shapes=list(scratch),
        input_output_aliases=aliases or {},
        compiler_params=pltpu.CompilerParams(vmem_limit_bytes=16 << 20),
    )

    def run(*operands):
        operands = operands[:scalars] + tuple(
            pltpu.with_memory_space_constraint(x, pltpu.VMEM) for x in operands[scalars:]
        )
        return call(*operands)

    return run


def dot(a, b, contract):
    return lax.dot_general(a, b, ((contract[:1], contract[1:]), ((), ())), preferred_element_type=F32)


def fill_rows(place, field, partner, other, ext):
    even = place[0] == 0
    rows, zonal, _ = field.shape
    half = STENCIL_SIDE // 2
    for r in range(rows + 2 * half):
        if r < half:
            row = jnp.where(even, other[r].astype(F32), partner[r].astype(F32))
        elif r < rows + half:
            row = field[r - half].astype(F32)
        else:
            k = r - rows - half
            row = jnp.where(even, partner[k].astype(F32), other[k].astype(F32))
        ext[r, EDGE : EDGE + zonal, :] = row
        ext[r, EDGE - half : EDGE, :] = row[zonal - half :]
        ext[r, EDGE + zonal : EDGE + zonal + half, :] = row[:half]


def stencil_body(place, field, partner, other, taps, gain, scaled, inverse, normed, ext):
    rows, zonal, _ = field.shape
    half = STENCIL_SIDE // 2
    fill_rows(place, field, partner, other, ext)
    for start in range(0, zonal, STRIP):
        total = jnp.zeros((rows, STRIP, field.shape[2]), F32)
        for b in range(STENCIL_SIDE):
            first = EDGE - half + b + start
            slab = ext[:, first : first + STRIP, :]
            for a in range(STENCIL_SIDE):
                k = a * STENCIL_SIDE + b
                total = total + taps[k : k + 1, :][None] * slab[a : a + rows]
        centred = total - jnp.mean(total, axis=-1, keepdims=True)
        recip = lax.rsqrt(jnp.mean(centred * centred, axis=-1, keepdims=True) + EPSILON)
        value = centred * recip
        rounded = (gain[0:1, :][None] * value).astype(BF16)
        wide = jnp.broadcast_to(recip, value.shape)
        for i in range(rows):
            at = pl.ds(i * zonal + start, STRIP)
            scaled[at, :] = value[i]
            inverse[at, :] = wide[i]
            normed[at, :] = rounded[i]


def selector(rows, columns, chunk_bits, offsets, turned):
    place = lax.broadcasted_iota(jnp.int32, (rows, columns), 1 if turned else 0)
    variable = lax.broadcasted_iota(jnp.int32, (rows, columns), 0 if turned else 1)
    chunk = lax.shift_right_logical(place, chunk_bits)
    inside = place & ((1 << chunk_bits) - 1)
    result = jnp.zeros((rows, columns), F32)
    for offset in offsets:
        j = inside - offset
        hit = (j >= 0) & (j < PER_CHUNK) & (chunk * PER_CHUNK + j == variable)
        result = jnp.where(hit, 1.0, result)
    return result.astype(BF16)


def matrices(shards):
    count, owned, channels = shards.shape[0], shards.shape[1] // 2, shards.shape[2]
    return (
        shards[:, :owned, :].reshape(count * owned, channels),
        shards[:, owned:, :].reshape(count * owned, channels),
    )


def mlp_body(normed, mine, theirs, field, readout, gated, upper, residual, chunks):
    points, channels = normed.shape
    halves = [matrices(mine), matrices(theirs)]
    wide = upper.shape[1] // 2
    for k, (widen, _) in enumerate(halves):
        upper[:, k * wide : (k + 1) * wide] = dot(normed[...], widen, (1, 1))

    def step(i, carry):
        at = pl.ds(pl.multiple_of(i * 16, 16), 16)
        gated[at, :] = gelu_value(upper[at, :]).astype(BF16)
        return carry

    lax.fori_loop(0, points // 16, step, 0, unroll=2)
    mixed = sum(
        dot(gated[:, k * wide : (k + 1) * wide], shrink, (1, 0))
        for k, (_, shrink) in enumerate(halves)
    )
    residual[...] = (field[...].reshape(points, channels).astype(F32) + mixed).astype(BF16)
    members = chunks.shape[0]
    spread = dot(selector(members * CHUNK_ROWS, readout.shape[0], 3, (0,), False), readout[...], (1, 0))
    outlook = dot(spread.astype(BF16), residual[...], (1, 1))
    for e in range(members):
        chunks[e] = outlook[e * CHUNK_ROWS : (e + 1) * CHUNK_ROWS].astype(BF16)


def slope_body(upper, slope):
    def step(i, carry):
        at = pl.ds(pl.multiple_of(i * 16, 16), 16)
        slope[at, :] = gelu_slope(upper[at, :])
        return carry

    lax.fori_loop(0, upper.shape[0] // 16, step, 0, unroll=2)


def outlook_body(readout, residual, out):
    out[...] = dot(readout[...], residual[...], (1, 1)).astype(BF16)


def pair_body(place, everyone, truth, weight, payload, loss, rows, seen):
    member = place[1]
    members, _, points = everyone.shape
    _, bands, lanes = truth.shape
    variables = TAPS_AT
    first = jnp.minimum(member * PER_CHUNK, variables - PER_CHUNK)
    for j in range(PER_CHUNK):
        row = truth[jnp.minimum(member * PER_CHUNK + j, variables - 1) - first]
        for q in range(bands):
            seen[j : j + 1, q * lanes : (q + 1) * lanes] = row[q : q + 1]
    seen[PER_CHUNK:, :] = jnp.zeros((CHUNK_ROWS - PER_CHUNK, points), F32)
    limit = jnp.minimum(PER_CHUNK, variables - member * PER_CHUNK)
    real = lax.broadcasted_iota(jnp.int32, (CHUNK_ROWS, lanes), 0) < limit
    pair_norm = 1.0 / (members * (members - 1))
    lost = jnp.zeros((CHUNK_ROWS, lanes), F32)
    for q in range(points // lanes):
        at = slice(q * lanes, (q + 1) * lanes)
        y = [everyone[m, :, at].astype(F32) for m in range(members)]
        spread = [jnp.full((CHUNK_ROWS, lanes), SMOOTHING**0.5, F32) for _ in range(members)]
        ranks = [jnp.zeros((CHUNK_ROWS, lanes), F32) for _ in range(members)]
        for m in range(members):
            for k in range(m):
                gap = y[m] - y[k]
                square = gap * gap + SMOOTHING
                root = lax.rsqrt(square)
                size, tilt = square * root, gap * root
                spread[m], spread[k] = spread[m] + size, spread[k] + size
                ranks[m], ranks[k] = ranks[m] + tilt, ranks[k] - tilt
        scale = weight[0:1, at]
        for m in range(members):
            miss = y[m] - seen[:, at]
            square = miss * miss + SMOOTHING
            root = lax.rsqrt(square)
            term = scale * (square * root * (1.0 / members) - 0.5 * pair_norm * spread[m])
            lost = lost + jnp.where(real, term, 0.0)
            flow = scale * (miss * root * (1.0 / members) - pair_norm * ranks[m])
            average = spread[m] * (1.0 / (members - 1))
            high = average.astype(BF16).astype(F32)
            rows[m, 0:CHUNK_ROWS, at] = jnp.where(real, flow, 0.0)
            rows[m, PER_CHUNK : PER_CHUNK + CHUNK_ROWS, at] = high
            rows[m, 2 * PER_CHUNK : 16, at] = (average - high)[: 16 - 2 * PER_CHUNK]
    for m in range(members):
        payload[m] = rows[m].astype(BF16)
    loss[...] = jnp.sum(lost, axis=0, keepdims=True)


def average_body(back, out):
    members, height, points = back.shape
    pick = selector(out.shape[0], members * height, 4, (PER_CHUNK, 2 * PER_CHUNK), True)
    out[...] = dot(pick, back[...].reshape(members * height, points), (1, 0))


def backward_body(
    back, readout, residual, gated, slope, normed, scaled, inverse, gain, mine, theirs,
    widen_grad, shrink_grad, readout_grad, gain_grad, back_depth, gate, back_upper,
):
    members, height, points = back.shape
    halves = [matrices(mine), matrices(theirs)]
    wide = slope.shape[1] // 2
    flow = back[...].reshape(members * height, points)
    spread = dot(selector(members * height, readout.shape[0], 4, (0,), False), readout[...], (1, 0))
    back_residual = dot(flow, spread.astype(BF16), (0, 0)).astype(BF16)
    for k, (_, shrink) in enumerate(halves):
        gate[:, k * wide : (k + 1) * wide] = dot(back_residual, shrink, (1, 1))
    readout_grad[...] = dot(flow, residual[...], (1, 0))
    shrink_grad[...] = dot(gated[...], back_residual, (0, 0))

    def step(i, carry):
        at = pl.ds(pl.multiple_of(i * 16, 16), 16)
        back_upper[at, :] = (gate[at, :] * slope[at, :]).astype(BF16)
        return carry

    lax.fori_loop(0, points // 16, step, 0, unroll=2)
    back_norm = sum(
        dot(back_upper[:, k * wide : (k + 1) * wide], widen, (1, 0))
        for k, (widen, _) in enumerate(halves)
    )
    widen_grad[...] = dot(back_upper[...], normed[...], (0, 0))
    value = scaled[...]
    product = back_norm * value
    gain_grad[...] = jnp.sum(product, axis=0, keepdims=True)
    g = back_norm * gain[0:1, :]
    p = jnp.mean(g, axis=-1, keepdims=True)
    q = jnp.mean(g * value, axis=-1, keepdims=True)
    back_depth[...] = inverse[...] * (g - p - value * q)


def pack_body(back_depth, ext, widen_grad, shrink_grad, readout_grad, gain_grad, loss, send, keep, small):
    half = STENCIL_SIDE // 2
    zonal = ext.shape[1] - 2 * EDGE
    rows = back_depth.shape[0] // zonal
    channels = ext.shape[2]
    members = small.shape[0] // CHUNK_ROWS
    height = readout_grad.shape[0] // members
    small[TAPS_AT + 48 :, :] = jnp.zeros((small.shape[0] - TAPS_AT - 48, channels), F32)
    for e in range(members):
        count = min(PER_CHUNK, TAPS_AT - e * PER_CHUNK)
        if count > 0:
            small[e * PER_CHUNK : e * PER_CHUNK + count, :] = readout_grad[e * height : e * height + count, :]
    for b in range(STENCIL_SIDE):
        totals = [jnp.zeros((STRIP, channels), F32) for _ in range(STENCIL_SIDE)]
        for start in range(0, zonal, STRIP):
            first = EDGE - half + b + start
            slab = ext[:, first : first + STRIP, :]
            up = [back_depth[i * zonal + start : i * zonal + start + STRIP, :] for i in range(rows)]
            for a in range(STENCIL_SIDE):
                for i in range(rows):
                    totals[a] = totals[a] + up[i] * slab[i + a]
        for a in range(STENCIL_SIDE):
            k = TAPS_AT + a * STENCIL_SIDE + b
            small[k : k + 1, :] = jnp.sum(totals[a], axis=0, keepdims=True)
    small[TAPS_AT + 49 : TAPS_AT + 50, :] = gain_grad[...]
    small[TAPS_AT + 50 : TAPS_AT + 51, :] = loss[...]
    depth_z = DEPTH_Z
    for e in range(members):
        tail = small[e * CHUNK_ROWS : (e + 1) * CHUNK_ROWS, :]
        for h in range(2):
            d = 2 * e + h
            for mat, grad in enumerate((widen_grad, shrink_grad)):
                at = slice(mat * depth_z, (mat + 1) * depth_z)
                base = h * depth_z * members + e
                keep[d, at, :] = grad[pl.ds(base, depth_z, stride=members), :]
                base = base + 2 * depth_z * members
                send[d, at, :] = grad[pl.ds(base, depth_z, stride=members), :]
            keep[d, 2 * depth_z :, :] = tail
            send[d, 2 * depth_z :, :] = tail


def gradient_body(
    place, back, readout, residual, gated, slope, normed, scaled, inverse, gain, mine, theirs, loss,
    field, partner, other, send, keep, ext, gate, back_upper, widen_grad, shrink_grad, readout_grad, gain_grad, back_depth, small,
):
    fill_rows(place, field, partner, other, ext)
    backward_body(
        back, readout, residual, gated, slope, normed, scaled, inverse, gain, mine, theirs,
        widen_grad, shrink_grad, readout_grad, gain_grad, back_depth, gate, back_upper,
    )
    pack_body(
        back_depth, ext, widen_grad, shrink_grad, readout_grad, gain_grad, loss,
        send, keep, small,
    )


def final_body(arrived, up, down, taps, gain, readout, loss, small):
    members = arrived.shape[0]
    for e in range(members):
        small[e * CHUNK_ROWS : (e + 1) * CHUNK_ROWS, :] = arrived[e, 0:CHUNK_ROWS, :]
        up[e : e + 1, :] = arrived[e, CHUNK_ROWS : CHUNK_ROWS + 1, :]
        down[e : e + 1, :] = arrived[e, CHUNK_ROWS + 1 : CHUNK_ROWS + 2, :]
    readout[...] = small[0:TAPS_AT, :]
    taps[...] = small[TAPS_AT : TAPS_AT + 49, :]
    gain[...] = small[TAPS_AT + 49 : TAPS_AT + 50, :]
    loss[...] = jnp.sum(small[TAPS_AT + 50 : TAPS_AT + 51, :], axis=1, keepdims=True)


def on_device(
    features,
    random_perturbation,
    observed_truth,
    stencil_taps,
    affine_factor,
    widen_matrix,
    shrink_matrix,
    readout_matrix,
):
    rows, zonal, channels = features.shape
    variables = readout_matrix.shape[0]
    half = STENCIL_SIDE // 2
    bands, members = lax.axis_size("lat"), lax.axis_size("ens")
    band, member = lax.axis_index("lat"), lax.axis_index("ens")
    points = rows * zonal
    latitudes = rows * bands
    hidden = widen_matrix.shape[0] * bands
    depth_z = DEPTH_Z
    share = CHUNK_ROWS
    place = jnp.stack([lax.rem(band, 2), member]).astype(jnp.int32)
    gain = lax.optimization_barrier(jnp.broadcast_to(affine_factor[None], (8, channels)))

    field = (features.astype(F32) + random_perturbation[0].astype(F32)).astype(BF16)
    partner, other = halo_rows(field, half)
    shape = (bands // 2,) + widen_matrix.shape
    pair = jnp.concatenate(
        [jnp.broadcast_to(widen_matrix[None], shape), jnp.broadcast_to(shrink_matrix[None], shape)],
        axis=1,
    )
    mine = exchange(pair, AXES, weight_groups(members, bands))
    mine, partner, other = lax.optimization_barrier((mine, partner, other))
    theirs = core_swap(mine)
    latitude = (band * rows + jnp.arange(points, dtype=jnp.int32) // zonal).astype(F32)
    area = jnp.cos(math.pi * ((latitude + 0.5) / latitudes - 0.5))
    weight = (area * (1.0 / (latitudes * zonal)))[None, :]

    wide = (rows + 2 * half, zonal + 2 * EDGE, channels)
    scaled, inverse, normed = vmem_call(
        stencil_body,
        [
            ((points, channels), F32),
            ((points, channels), F32),
            ((points, channels), BF16),
        ],
        [pltpu.VMEM(wide, F32)],
        scalars=1,
        vectors=5,
    )(place, field, partner, other, stencil_taps, gain)
    gated, upper, residual, chunks = vmem_call(
        mlp_body,
        [
            ((points, hidden), BF16),
            ((points, hidden), F32),
            ((points, channels), BF16),
            ((members, CHUNK_ROWS, points), BF16),
        ],
        vectors=5,
    )(normed, mine, theirs, field, readout_matrix)
    everyone = exchange(chunks, "ens")
    (slope,) = vmem_call(slope_body, [((points, hidden), F32)], vectors=1, aliases={0: 0})(upper)
    first = jnp.minimum(member * PER_CHUNK, variables - PER_CHUNK)
    truth = lax.dynamic_slice_in_dim(observed_truth, first, PER_CHUNK, axis=0)
    (outlook,) = vmem_call(outlook_body, [((variables, points), BF16)], vectors=2)(
        readout_matrix, residual
    )
    sample_outlook = outlook.reshape(1, variables, rows, zonal)
    payload, loss = vmem_call(
        pair_body,
        [((members, 16, points), BF16), ((1, zonal), F32)],
        [pltpu.VMEM((members, 16, points), F32), pltpu.VMEM((CHUNK_ROWS, points), F32)],
        scalars=1,
        vectors=3,
    )(place, everyone, truth, weight)
    back = exchange(payload, "ens")
    (average,) = vmem_call(average_body, [((variables, points), F32)], vectors=1)(back)
    sample_average_spread = average.reshape(1, variables, rows, zonal)

    packet = ((2 * members, 2 * depth_z + share, channels), F32)
    send, keep = vmem_call(
        gradient_body,
        [packet, packet],
        [
            pltpu.VMEM(wide, F32),
            pltpu.VMEM((points, hidden), F32),
            pltpu.VMEM((points, hidden), BF16),
            pltpu.VMEM((hidden, channels), F32),
            pltpu.VMEM((hidden, channels), F32),
            pltpu.VMEM((members * 16, channels), F32),
            pltpu.VMEM((1, channels), F32),
            pltpu.VMEM((points, channels), F32),
            pltpu.VMEM((members * share, channels), F32),
        ],
        scalars=1,
        vectors=15,
    )(
        place, back, readout_matrix, residual, gated, slope, normed, scaled, inverse, gain, mine,
        theirs, loss, field, partner, other,
    )

    total = (keep + core_swap(send)).astype(BF16)
    arrived = exchange(total, AXES, plane_groups(members, bands)).astype(F32)
    columns = [
        list(range(h * bands // 2 + c, (h + 1) * bands // 2, 2)) for h in range(2) for c in range(2)
    ]
    part = jnp.sum(arrived, axis=0)
    outgoing = jnp.concatenate(
        [
            jnp.broadcast_to(part[None, 2 * depth_z :], (depth_z, share, channels)),
            part[: 2 * depth_z].reshape(2, depth_z, channels).transpose(1, 0, 2),
        ],
        axis=1,
    )
    done = jnp.sum(exchange(outgoing, "lat", columns), axis=0)
    arrived = exchange(jnp.broadcast_to(done[None], (members,) + done.shape), "ens")
    up, down, taps, gain_total, readout, loss = vmem_call(
        final_body,
        [
            ((members, channels), F32),
            ((members, channels), F32),
            ((STENCIL_SIDE * STENCIL_SIDE, channels), F32),
            ((1, channels), F32),
            ((variables, channels), F32),
            ((1, 1), F32),
        ],
        [pltpu.VMEM((members * share, channels), F32)],
        vectors=1,
        kept=range(6),
    )(arrived)
    return (
        loss.reshape(()),
        taps,
        gain_total.reshape(channels),
        up,
        down,
        readout,
        sample_outlook,
        sample_average_spread,
    )


def solution(mesh):
    in_specs = (
        P("lat", None, None),
        P("ens", "lat", None, None),
        P(None, "lat", None),
        P(),
        P(),
        P("lat", None),
        P("lat", None),
        P(),
    )
    out_specs = (
        P(),
        P(),
        P(),
        P("lat", None),
        P("lat", None),
        P(),
        P("ens", None, "lat", None),
        P("ens", None, "lat", None),
    )

    return jax.shard_map(
        on_device, mesh=mesh, in_specs=in_specs, out_specs=out_specs, check_vma=False
    )
```

```python
import math

import jax
import jax.numpy as jnp
from jax import lax
from jax.experimental import pallas as pl
from jax.experimental.pallas import tpu as pltpu
from jax.sharding import PartitionSpec as P

STENCIL_SIDE = 7
SQRT_TWO_PI = 0.7978845608028654
CUBIC = 0.044715
EPSILON = 1e-06
SMOOTHING = 0.01
PER_CHUNK = 5
CHUNK_ROWS = 8
EDGE = 8
STRIP = 16
TAPS_AT = 69
DEPTH_Z = 8
F32, BF16 = jnp.float32, jnp.bfloat16


def core_swap(value):
    count = lax.axis_size("lat")
    return lax.ppermute(value, "lat", [(i, i ^ 1) for i in range(count)])


def odd_swap(value):
    count = lax.axis_size("lat")
    pairs = [(i, i + 1) for i in range(1, count - 1, 2)]
    return lax.ppermute(value, "lat", pairs + [(b, a) for a, b in pairs])


def halo_rows(field, half):
    even = lax.rem(lax.axis_index("lat"), 2) == 0
    head, tail = field[:half], field[field.shape[0] - half :]
    return core_swap(jnp.where(even, tail, head)), odd_swap(jnp.where(even, head, tail))


def exchange(value, axis, groups=None):
    return lax.all_to_all(value, axis, 0, 0, tiled=True, axis_index_groups=groups)


AXES = ("ens", "lat")


def weight_groups(members, bands):
    half = bands // 2
    groups = []
    for e in range(members):
        far = e // 4 * 4 + (e + 2) % 4
        for c in range(2):
            groups.append(
                [e * bands + b for b in range(c, half, 2)]
                + [far * bands + b for b in range(half + c, bands, 2)]
            )
    return groups


def plane_groups(members, bands):
    half = bands // 2
    return [
        [e * bands + h * half + rest for e in range(members) for h in range(2)]
        for rest in range(half)
    ]


def gelu_value(u):
    inner = jnp.tanh(SQRT_TWO_PI * (u + CUBIC * u * u * u))
    return 0.5 * u * (1.0 + inner)


def gelu_slope(u):
    inner = jnp.tanh(SQRT_TWO_PI * (u + CUBIC * u * u * u))
    return 0.5 * (1.0 + inner) + 0.5 * u * (1.0 - inner * inner) * SQRT_TWO_PI * (
        1.0 + 3.0 * CUBIC * u * u
    )


def vmem_call(body, outs, scratch=(), scalars=0, vectors=0, kept=(), aliases=None):
    vmem = pl.BlockSpec(memory_space=pltpu.VMEM)
    smem = pl.BlockSpec(memory_space=pltpu.SMEM)
    call = pl.pallas_call(
        body,
        out_shape=[
            jax.ShapeDtypeStruct(*out) if i in kept else pltpu.VMEM(*out)
            for i, out in enumerate(outs)
        ],
        in_specs=[smem] * scalars + [vmem] * vectors,
        out_specs=[vmem] * len(outs),
        scratch_shapes=list(scratch),
        input_output_aliases=aliases or {},
        compiler_params=pltpu.CompilerParams(vmem_limit_bytes=16 << 20),
    )

    def run(*operands):
        operands = operands[:scalars] + tuple(
            pltpu.with_memory_space_constraint(x, pltpu.VMEM) for x in operands[scalars:]
        )
        return call(*operands)

    return run


def dot(a, b, contract):
    return lax.dot_general(a, b, ((contract[:1], contract[1:]), ((), ())), preferred_element_type=F32)


def fill_rows(place, field, partner, other, ext):
    even = place[0] == 0
    rows, zonal, _ = field.shape
    half = STENCIL_SIDE // 2
    for r in range(rows + 2 * half):
        if r < half:
            row = jnp.where(even, other[r].astype(F32), partner[r].astype(F32))
        elif r < rows + half:
            row = field[r - half].astype(F32)
        else:
            k = r - rows - half
            row = jnp.where(even, partner[k].astype(F32), other[k].astype(F32))
        ext[r, EDGE : EDGE + zonal, :] = row
        ext[r, EDGE - half : EDGE, :] = row[zonal - half :]
        ext[r, EDGE + zonal : EDGE + zonal + half, :] = row[:half]


def stencil_body(place, field, partner, other, taps, gain, scaled, inverse, normed, ext):
    rows, zonal, _ = field.shape
    half = STENCIL_SIDE // 2
    fill_rows(place, field, partner, other, ext)
    for start in range(0, zonal, STRIP):
        total = jnp.zeros((rows, STRIP, field.shape[2]), F32)
        for b in range(STENCIL_SIDE):
            first = EDGE - half + b + start
            slab = ext[:, first : first + STRIP, :]
            for a in range(STENCIL_SIDE):
                k = a * STENCIL_SIDE + b
                total = total + taps[k : k + 1, :][None] * slab[a : a + rows]
        centred = total - jnp.mean(total, axis=-1, keepdims=True)
        recip = lax.rsqrt(jnp.mean(centred * centred, axis=-1, keepdims=True) + EPSILON)
        value = centred * recip
        rounded = (gain[0:1, :][None] * value).astype(BF16)
        wide = jnp.broadcast_to(recip, value.shape)
        for i in range(rows):
            at = pl.ds(i * zonal + start, STRIP)
            scaled[at, :] = value[i]
            inverse[at, :] = wide[i]
            normed[at, :] = rounded[i]


def selector(rows, columns, chunk_bits, offsets, turned):
    place = lax.broadcasted_iota(jnp.int32, (rows, columns), 1 if turned else 0)
    variable = lax.broadcasted_iota(jnp.int32, (rows, columns), 0 if turned else 1)
    chunk = lax.shift_right_logical(place, chunk_bits)
    inside = place & ((1 << chunk_bits) - 1)
    result = jnp.zeros((rows, columns), F32)
    for offset in offsets:
        j = inside - offset
        hit = (j >= 0) & (j < PER_CHUNK) & (chunk * PER_CHUNK + j == variable)
        result = jnp.where(hit, 1.0, result)
    return result.astype(BF16)


def matrices(shards):
    count, owned, channels = shards.shape[0], shards.shape[1] // 2, shards.shape[2]
    return (
        shards[:, :owned, :].reshape(count * owned, channels),
        shards[:, owned:, :].reshape(count * owned, channels),
    )


def expand(normed, shards, gated, upper):
    widen, shrink = matrices(shards)
    upper[...] = dot(normed[...], widen, (1, 1))

    def step(i, carry):
        at = pl.ds(pl.multiple_of(i * 16, 16), 16)
        gated[at, :] = gelu_value(upper[at, :]).astype(BF16)
        return carry

    lax.fori_loop(0, upper.shape[0] // 16, step, 0, unroll=2)
    return dot(gated[...], shrink, (1, 0))


def first_body(normed, mine, gated, upper, mixed):
    mixed[...] = expand(normed, mine, gated, upper)


def second_body(normed, theirs, mixed, field, readout, gated, upper, residual, chunks):
    points, channels = normed.shape
    total = mixed[...] + expand(normed, theirs, gated, upper)
    residual[...] = (field[...].reshape(points, channels).astype(F32) + total).astype(BF16)
    members = chunks.shape[0]
    spread = dot(selector(members * CHUNK_ROWS, readout.shape[0], 3, (0,), False), readout[...], (1, 0))
    outlook = dot(spread.astype(BF16), residual[...], (1, 1))
    for e in range(members):
        chunks[e] = outlook[e * CHUNK_ROWS : (e + 1) * CHUNK_ROWS].astype(BF16)


def slope_body(upper, slope):
    def step(i, carry):
        at = pl.ds(pl.multiple_of(i * 16, 16), 16)
        slope[at, :] = gelu_slope(upper[at, :])
        return carry

    lax.fori_loop(0, upper.shape[0] // 16, step, 0, unroll=2)


def outlook_body(readout, residual, out):
    out[...] = dot(readout[...], residual[...], (1, 1)).astype(BF16)


def pair_body(place, everyone, truth, weight, payload, loss, rows, seen):
    member = place[1]
    members, _, points = everyone.shape
    _, bands, lanes = truth.shape
    variables = TAPS_AT
    first = jnp.minimum(member * PER_CHUNK, variables - PER_CHUNK)
    for j in range(PER_CHUNK):
        row = truth[jnp.minimum(member * PER_CHUNK + j, variables - 1) - first]
        for q in range(bands):
            seen[j : j + 1, q * lanes : (q + 1) * lanes] = row[q : q + 1]
    seen[PER_CHUNK:, :] = jnp.zeros((CHUNK_ROWS - PER_CHUNK, points), F32)
    limit = jnp.minimum(PER_CHUNK, variables - member * PER_CHUNK)
    real = lax.broadcasted_iota(jnp.int32, (CHUNK_ROWS, lanes), 0) < limit
    pair_norm = 1.0 / (members * (members - 1))
    lost = jnp.zeros((CHUNK_ROWS, lanes), F32)
    for q in range(points // lanes):
        at = slice(q * lanes, (q + 1) * lanes)
        y = [everyone[m, :, at].astype(F32) for m in range(members)]
        spread = [jnp.full((CHUNK_ROWS, lanes), SMOOTHING**0.5, F32) for _ in range(members)]
        ranks = [jnp.zeros((CHUNK_ROWS, lanes), F32) for _ in range(members)]
        for m in range(members):
            for k in range(m):
                gap = y[m] - y[k]
                square = gap * gap + SMOOTHING
                root = lax.rsqrt(square)
                size, tilt = square * root, gap * root
                spread[m], spread[k] = spread[m] + size, spread[k] + size
                ranks[m], ranks[k] = ranks[m] + tilt, ranks[k] - tilt
        scale = weight[0:1, at]
        for m in range(members):
            miss = y[m] - seen[:, at]
            square = miss * miss + SMOOTHING
            root = lax.rsqrt(square)
            term = scale * (square * root * (1.0 / members) - 0.5 * pair_norm * spread[m])
            lost = lost + jnp.where(real, term, 0.0)
            flow = scale * (miss * root * (1.0 / members) - pair_norm * ranks[m])
            average = spread[m] * (1.0 / (members - 1))
            high = average.astype(BF16).astype(F32)
            rows[m, 0:CHUNK_ROWS, at] = jnp.where(real, flow, 0.0)
            rows[m, PER_CHUNK : PER_CHUNK + CHUNK_ROWS, at] = high
            rows[m, 2 * PER_CHUNK : 16, at] = (average - high)[: 16 - 2 * PER_CHUNK]
    for m in range(members):
        payload[m] = rows[m].astype(BF16)
    loss[...] = jnp.sum(lost, axis=0, keepdims=True)


def average_body(back, out):
    members, height, points = back.shape
    pick = selector(out.shape[0], members * height, 4, (PER_CHUNK, 2 * PER_CHUNK), True)
    out[...] = dot(pick, back[...].reshape(members * height, points), (1, 0))


def backward_body(
    back, readout, residual, gated, other_gated, slope, other_slope, normed, scaled, inverse, gain, mine, theirs,
    widen_grad, shrink_grad, readout_grad, gain_grad, back_depth, gate, back_upper,
):
    members, height, points = back.shape
    halves = [matrices(mine), matrices(theirs)]
    wide = slope.shape[1]
    flow = back[...].reshape(members * height, points)
    spread = dot(selector(members * height, readout.shape[0], 4, (0,), False), readout[...], (1, 0))
    back_residual = dot(flow, spread.astype(BF16), (0, 0)).astype(BF16)
    for k, (_, shrink) in enumerate(halves):
        gate[:, k * wide : (k + 1) * wide] = dot(back_residual, shrink, (1, 1))
    readout_grad[...] = dot(flow, residual[...], (1, 0))
    shrink_grad[:wide, :] = dot(gated[...], back_residual, (0, 0))
    shrink_grad[wide:, :] = dot(other_gated[...], back_residual, (0, 0))

    def step(i, carry):
        at = pl.ds(pl.multiple_of(i * 16, 16), 16)
        back_upper[at, :wide] = (gate[at, :wide] * slope[at, :]).astype(BF16)
        back_upper[at, wide:] = (gate[at, wide:] * other_slope[at, :]).astype(BF16)
        return carry

    lax.fori_loop(0, points // 16, step, 0, unroll=2)
    back_norm = sum(
        dot(back_upper[:, k * wide : (k + 1) * wide], widen, (1, 0))
        for k, (widen, _) in enumerate(halves)
    )
    widen_grad[...] = dot(back_upper[...], normed[...], (0, 0))
    value = scaled[...]
    product = back_norm * value
    gain_grad[...] = jnp.sum(product, axis=0, keepdims=True)
    g = back_norm * gain[0:1, :]
    p = jnp.mean(g, axis=-1, keepdims=True)
    q = jnp.mean(g * value, axis=-1, keepdims=True)
    back_depth[...] = inverse[...] * (g - p - value * q)


def pack_body(back_depth, ext, widen_grad, shrink_grad, readout_grad, gain_grad, loss, send, keep, small):
    half = STENCIL_SIDE // 2
    zonal = ext.shape[1] - 2 * EDGE
    rows = back_depth.shape[0] // zonal
    channels = ext.shape[2]
    members = small.shape[0] // CHUNK_ROWS
    height = readout_grad.shape[0] // members
    small[TAPS_AT + 48 :, :] = jnp.zeros((small.shape[0] - TAPS_AT - 48, channels), F32)
    for e in range(members):
        count = min(PER_CHUNK, TAPS_AT - e * PER_CHUNK)
        if count > 0:
            small[e * PER_CHUNK : e * PER_CHUNK + count, :] = readout_grad[e * height : e * height + count, :]
    for b in range(STENCIL_SIDE):
        totals = [jnp.zeros((STRIP, channels), F32) for _ in range(STENCIL_SIDE)]
        for start in range(0, zonal, STRIP):
            first = EDGE - half + b + start
            slab = ext[:, first : first + STRIP, :]
            up = [back_depth[i * zonal + start : i * zonal + start + STRIP, :] for i in range(rows)]
            for a in range(STENCIL_SIDE):
                for i in range(rows):
                    totals[a] = totals[a] + up[i] * slab[i + a]
        for a in range(STENCIL_SIDE):
            k = TAPS_AT + a * STENCIL_SIDE + b
            small[k : k + 1, :] = jnp.sum(totals[a], axis=0, keepdims=True)
    small[TAPS_AT + 49 : TAPS_AT + 50, :] = gain_grad[...]
    small[TAPS_AT + 50 : TAPS_AT + 51, :] = loss[...]
    depth_z = DEPTH_Z
    for e in range(members):
        tail = small[e * CHUNK_ROWS : (e + 1) * CHUNK_ROWS, :]
        for h in range(2):
            d = 2 * e + h
            for mat, grad in enumerate((widen_grad, shrink_grad)):
                at = slice(mat * depth_z, (mat + 1) * depth_z)
                base = h * depth_z * members + e
                keep[d, at, :] = grad[pl.ds(base, depth_z, stride=members), :]
                base = base + 2 * depth_z * members
                send[d, at, :] = grad[pl.ds(base, depth_z, stride=members), :]
            keep[d, 2 * depth_z :, :] = tail
            send[d, 2 * depth_z :, :] = tail


def gradient_body(
    place, back, readout, residual, gated, other_gated, slope, other_slope, normed, scaled, inverse, gain, mine, theirs, loss,
    field, partner, other, send, keep, ext, gate, back_upper, widen_grad, shrink_grad, readout_grad, gain_grad, back_depth, small,
):
    fill_rows(place, field, partner, other, ext)
    backward_body(
        back, readout, residual, gated, other_gated, slope, other_slope, normed, scaled, inverse,
        gain, mine, theirs, widen_grad, shrink_grad, readout_grad, gain_grad, back_depth, gate, back_upper,
    )
    pack_body(
        back_depth, ext, widen_grad, shrink_grad, readout_grad, gain_grad, loss,
        send, keep, small,
    )


def final_body(arrived, up, down, taps, gain, readout, loss, small):
    members = arrived.shape[0]
    for e in range(members):
        small[e * CHUNK_ROWS : (e + 1) * CHUNK_ROWS, :] = arrived[e, 0:CHUNK_ROWS, :]
        up[e : e + 1, :] = arrived[e, CHUNK_ROWS : CHUNK_ROWS + 1, :]
        down[e : e + 1, :] = arrived[e, CHUNK_ROWS + 1 : CHUNK_ROWS + 2, :]
    readout[...] = small[0:TAPS_AT, :]
    taps[...] = small[TAPS_AT : TAPS_AT + 49, :]
    gain[...] = small[TAPS_AT + 49 : TAPS_AT + 50, :]
    loss[...] = jnp.sum(small[TAPS_AT + 50 : TAPS_AT + 51, :], axis=1, keepdims=True)


def on_device(
    features,
    random_perturbation,
    observed_truth,
    stencil_taps,
    affine_factor,
    widen_matrix,
    shrink_matrix,
    readout_matrix,
):
    rows, zonal, channels = features.shape
    variables = readout_matrix.shape[0]
    half = STENCIL_SIDE // 2
    bands, members = lax.axis_size("lat"), lax.axis_size("ens")
    band, member = lax.axis_index("lat"), lax.axis_index("ens")
    points = rows * zonal
    latitudes = rows * bands
    hidden = widen_matrix.shape[0] * bands
    depth_z = DEPTH_Z
    share = CHUNK_ROWS
    place = jnp.stack([lax.rem(band, 2), member]).astype(jnp.int32)
    gain = lax.optimization_barrier(jnp.broadcast_to(affine_factor[None], (8, channels)))

    field = (features.astype(F32) + random_perturbation[0].astype(F32)).astype(BF16)
    partner, other = halo_rows(field, half)
    shape = (bands // 2,) + widen_matrix.shape
    pair = jnp.concatenate(
        [jnp.broadcast_to(widen_matrix[None], shape), jnp.broadcast_to(shrink_matrix[None], shape)],
        axis=1,
    )
    mine = exchange(pair, AXES, weight_groups(members, bands))
    theirs = core_swap(mine)
    latitude = (band * rows + jnp.arange(points, dtype=jnp.int32) // zonal).astype(F32)
    area = jnp.cos(math.pi * ((latitude + 0.5) / latitudes - 0.5))
    weight = (area * (1.0 / (latitudes * zonal)))[None, :]

    wide = (rows + 2 * half, zonal + 2 * EDGE, channels)
    scaled, inverse, normed = vmem_call(
        stencil_body,
        [
            ((points, channels), F32),
            ((points, channels), F32),
            ((points, channels), BF16),
        ],
        [pltpu.VMEM(wide, F32)],
        scalars=1,
        vectors=5,
    )(place, field, partner, other, stencil_taps, gain)
    gated, upper, mixed = vmem_call(
        first_body,
        [((points, hidden // 2), BF16), ((points, hidden // 2), F32), ((points, channels), F32)],
        vectors=2,
    )(normed, mine)
    other_gated, other_upper, residual, chunks = vmem_call(
        second_body,
        [
            ((points, hidden // 2), BF16),
            ((points, hidden // 2), F32),
            ((points, channels), BF16),
            ((members, CHUNK_ROWS, points), BF16),
        ],
        vectors=5,
    )(normed, theirs, mixed, field, readout_matrix)
    everyone = exchange(chunks, "ens")
    slope, other_slope = (
        vmem_call(
            slope_body, [((points, hidden // 2), F32)], vectors=1, aliases={0: 0}
        )(half_upper)[0]
        for half_upper in (upper, other_upper)
    )
    first = jnp.minimum(member * PER_CHUNK, variables - PER_CHUNK)
    truth = lax.dynamic_slice_in_dim(observed_truth, first, PER_CHUNK, axis=0)
    (outlook,) = vmem_call(outlook_body, [((variables, points), BF16)], vectors=2)(
        readout_matrix, residual
    )
    sample_outlook = outlook.reshape(1, variables, rows, zonal)
    payload, loss = vmem_call(
        pair_body,
        [((members, 16, points), BF16), ((1, zonal), F32)],
        [pltpu.VMEM((members, 16, points), F32), pltpu.VMEM((CHUNK_ROWS, points), F32)],
        scalars=1,
        vectors=3,
    )(place, everyone, truth, weight)
    back = exchange(payload, "ens")
    (average,) = vmem_call(average_body, [((variables, points), F32)], vectors=1)(back)
    sample_average_spread = average.reshape(1, variables, rows, zonal)

    packet = ((2 * members, 2 * depth_z + share, channels), F32)
    send, keep = vmem_call(
        gradient_body,
        [packet, packet],
        [
            pltpu.VMEM(wide, F32),
            pltpu.VMEM((points, hidden), F32),
            pltpu.VMEM((points, hidden), BF16),
            pltpu.VMEM((hidden, channels), F32),
            pltpu.VMEM((hidden, channels), F32),
            pltpu.VMEM((members * 16, channels), F32),
            pltpu.VMEM((1, channels), F32),
            pltpu.VMEM((points, channels), F32),
            pltpu.VMEM((members * share, channels), F32),
        ],
        scalars=1,
        vectors=17,
    )(
        place, back, readout_matrix, residual, gated, other_gated, slope, other_slope, normed,
        scaled, inverse, gain, mine, theirs, loss, field, partner, other,
    )

    total = (keep + core_swap(send)).astype(BF16)
    arrived = exchange(total, AXES, plane_groups(members, bands)).astype(F32)
    columns = [
        list(range(h * bands // 2 + c, (h + 1) * bands // 2, 2)) for h in range(2) for c in range(2)
    ]
    part = jnp.sum(arrived, axis=0)
    outgoing = jnp.concatenate(
        [
            jnp.broadcast_to(part[None, 2 * depth_z :], (depth_z, share, channels)),
            part[: 2 * depth_z].reshape(2, depth_z, channels).transpose(1, 0, 2),
        ],
        axis=1,
    )
    done = jnp.sum(exchange(outgoing, "lat", columns), axis=0)
    arrived = exchange(jnp.broadcast_to(done[None], (members,) + done.shape), "ens")
    up, down, taps, gain_total, readout, loss = vmem_call(
        final_body,
        [
            ((members, channels), F32),
            ((members, channels), F32),
            ((STENCIL_SIDE * STENCIL_SIDE, channels), F32),
            ((1, channels), F32),
            ((variables, channels), F32),
            ((1, 1), F32),
        ],
        [pltpu.VMEM((members * share, channels), F32)],
        vectors=1,
        kept=range(6),
    )(arrived)
    return (
        loss.reshape(()),
        taps,
        gain_total.reshape(channels),
        up,
        down,
        readout,
        sample_outlook,
        sample_average_spread,
    )


def solution(mesh):
    in_specs = (
        P("lat", None, None),
        P("ens", "lat", None, None),
        P(None, "lat", None),
        P(),
        P(),
        P("lat", None),
        P("lat", None),
        P(),
    )
    out_specs = (
        P(),
        P(),
        P(),
        P("lat", None),
        P("lat", None),
        P(),
        P("ens", None, "lat", None),
        P("ens", None, "lat", None),
    )

    return jax.shard_map(
        on_device, mesh=mesh, in_specs=in_specs, out_specs=out_specs, check_vma=False
    )
```
